32 devices in a mesh: ea: 4 (over z), ta: 4 (over y, x), dev: 2 (over core).
Axes of the slice: x: 2, y: 2, z: 4, core: 2. Of those that a mesh axis runs over, the one named last changes fastest.
Arguments:
- tokens: bfloat16 [16, 197, 768], P(('ea', 'dev')), may hold values from -6 to 6
- expert_ids: int32 [16, 197, 2], P(('ea', 'dev')), may hold values from 0 to 3, all different within a row
- pair_ranks: int32 [16, 197, 2], P(('ea', 'dev')), may hold values from 0 to 787, as said below
- cotangent: bfloat16 [16, 197, 768], P(('ea', 'dev')), may hold values from -6 to 6
- w_qkv: bfloat16 [3, 768, 768], P(None, None, 'ta'), may hold values from -0.21875 to 0.21875
- b_qv: float32 [2, 768], P(None, 'ta'), may hold values from -3 to 3
- w_out: bfloat16 [768, 768], P('ta'), may hold values from -0.875 to 0.875
- b_out: float32 [768], replicated, may hold values from -3 to 3
- ln1_gain: float32 [768], replicated, may hold values from 0.5 to 1.5
- ln1_bias: float32 [768], replicated, may hold values from -3 to 3
- ln2_gain: float32 [768], replicated, may hold values from 0.5 to 1.5
- ln2_bias: float32 [768], replicated, may hold values from -3 to 3
- w_router: bfloat16 [768, 4], replicated, may hold values from -0.21875 to 0.21875
- w_up: bfloat16 [4, 768, 3072], P('ea', None, 'ta'), may hold values from -0.21875 to 0.21875
- b_up: float32 [4, 3072], P('ea', 'ta'), may hold values from -3 to 3
- w_down: bfloat16 [4, 3072, 768], P('ea', 'ta'), may hold values from -0.875 to 0.875
- b_down: float32 [4, 768], P('ea'), may hold values from -4 to 4
Outputs:
- output: bfloat16 [16, 197, 768], P(('ea', 'dev'))
- input_grad: float32 [16, 197, 768], P(('ea', 'dev'))
- qkv_grad: float32 [3, 768, 768], P(None, None, 'ta')
- qv_bias_grad: float32 [2, 768], P(None, 'ta')
- out_grad: float32 [768, 768], P('ta')
- out_bias_grad: float32 [768], replicated
- ln1_gain_grad: float32 [768], replicated
- ln1_bias_grad: float32 [768], replicated
- ln2_gain_grad: float32 [768], replicated
- ln2_bias_grad: float32 [768], replicated
- router_grad: float32 [768, 4], replicated
- up_grad: float32 [4, 768, 3072], P('ea', None, 'ta')
- up_bias_grad: float32 [4, 3072], P('ea', 'ta')
- down_grad: float32 [4, 3072, 768], P('ea', 'ta')
- down_bias_grad: float32 [4, 768], P('ea')
The draws below stay inside these ranges and needn't reach their ends.
Inputs may be any that keep to these rules, and one draw needn't show every extreme that they name: `expert_ids`: the 2 experts of one token differ. `pair_ranks`: within each routing group of 2 images the ranks are distinct, each of 0 to 787 once.
All inputs are finite; a program needn't handle non-finite values.
Results may differ from the reference program's by a relative error of at most 0.018.
The reference program's roundings to bfloat16 on the way count: a program that leaves them out, or rounds other values in their place, can miss the bound.
Values may be sent and summed in bfloat16 or wider, within the bound.
A program may use at most 128 MiB of HBM per device.

```python
import jax
import jax.numpy as jnp
from jax import lax

D = 768
HEADS = 12
HDIM = 64
FF = 3072
TOP = 2
SEQ = 197
IMG_DEV = 2
EXPERTS = 4
IMAGES = 16
CAP = 222


def draw_pair_ranks(key, part):
    groups = IMAGES // IMG_DEV
    pair_total = IMG_DEV * SEQ * TOP
    key_list = jax.random.split(key, groups)
    permuted = jax.vmap(lambda group_key: jax.random.permutation(group_key, pair_total))(key_list)
    return permuted.reshape(IMAGES, SEQ, TOP).astype(jnp.int32)


def block_levels(rng, dims, pieces, low, largest):
    level = 1.0
    for dim, parts in pieces:
        draws = jax.random.uniform(jax.random.fold_in(jax.random.fold_in(rng, 6), dim), (parts,), jnp.float32, low / len(pieces), largest / len(pieces))
        level = level * jnp.repeat(jnp.exp(draws), dims[dim] // parts).reshape((-1,) + (1,) * (len(dims) - 1 - dim))
    return level


def choose_distinct(stream_key, rows, amount, top, lift):
    ranking = jax.random.permutation(jax.random.fold_in(stream_key, 1), amount)
    boost = ranking
    for power in range(3):
        boost = boost * boost // amount
    boost = boost * lift // amount
    tickets = jax.random.randint(jax.random.fold_in(stream_key, 2), (rows, amount), 0, 4096) + boost
    holders = jax.random.permutation(jax.random.fold_in(stream_key, 3), rows)[jnp.arange(amount) % rows]
    tickets = jnp.where(jnp.arange(rows)[:, None] == holders[None, :], 1 << 14, tickets)
    score = tickets * amount + jnp.arange(amount)
    return lax.top_k(score.astype(jnp.int32), top)[1].astype(jnp.int32)


def bell_draw(rng, dims, deviation, reach, cuts=(), kind=jnp.bfloat16):
    level = block_levels(rng, dims, cuts, -0.22, 0.18) if cuts else 1.0
    values = jax.random.normal(rng, dims, jnp.float32) * deviation * level
    return jnp.minimum(jnp.maximum(values, -reach), reach).astype(kind)


def setup_inputs(seed: int = 0) -> dict:
    splits = jax.random.split(jax.random.key(seed), 18)
    return {
        "tokens": bell_draw(splits[0], (IMAGES, SEQ, D), 1.0, 6.0, ((0, 8),)),
        "expert_ids": choose_distinct(splits[1], IMAGES * SEQ, EXPERTS, TOP, 4096).reshape((IMAGES, SEQ, TOP)),
        "pair_ranks": draw_pair_ranks(jax.random.fold_in(splits[17], 71), 0),
        "cotangent": bell_draw(splits[3], (IMAGES, SEQ, D), 1.0, 6.0, ((0, 8),)),
        "w_qkv": bell_draw(splits[4], (3, D, HEADS * HDIM), D ** -0.5, 0.21875, ((2, 4),)),
        "b_qv": bell_draw(splits[5], (2, HEADS * HDIM), 0.5, 3.0, ((1, 4),), jnp.float32),
        "w_out": bell_draw(splits[6], (HEADS * HDIM, D), (HEADS * HDIM // 16) ** -0.5, 0.875, ((0, 4),)),
        "b_out": bell_draw(splits[7], (D,), 0.5, 3.0, (), jnp.float32),
        "ln1_gain": jnp.clip(1.0 + 0.1 * jax.random.normal(splits[8], (D,), jnp.float32), 0.5, 1.5),
        "ln1_bias": bell_draw(splits[9], (D,), 0.5, 3.0, (), jnp.float32),
        "ln2_gain": jnp.clip(1.0 + 0.1 * jax.random.normal(splits[10], (D,), jnp.float32), 0.5, 1.5),
        "ln2_bias": bell_draw(splits[11], (D,), 0.5, 3.0, (), jnp.float32),
        "w_router": bell_draw(splits[12], (D, EXPERTS), D ** -0.5, 0.21875),
        "w_up": bell_draw(splits[13], (EXPERTS, D, FF), D ** -0.5, 0.21875, ((0, 4), (2, 4))),
        "b_up": bell_draw(splits[14], (EXPERTS, FF), 0.5, 3.0, ((0, 4), (1, 4)), jnp.float32),
        "w_down": bell_draw(splits[15], (EXPERTS, FF, D), (max(FF // (16 * EXPERTS), 1)) ** -0.5, 0.875, ((0, 4), (1, 4))),
        "b_down": bell_draw(splits[16], (EXPERTS, D), 1.0, 4.0, ((0, 4),), jnp.float32),
    }


@jax.custom_vjp
def low(v):
    return lax.optimization_barrier(v.astype(jnp.bfloat16)).astype(jnp.float32)

@jax.custom_vjp
def low_back(v):
    return v

def low_keep(v):
    return (low(v), None)

def low_pass(kept, grad):
    return (grad,)

def back_keep(v):
    return (v, None)

def back_low(kept, grad):
    return (low(grad),)
low.defvjp(low_keep, low_pass)
low_back.defvjp(back_keep, back_low)
EPSILON = 1e-06
PRECISE = lax.Precision.HIGHEST

def layer_norm(values, gain_vec, shift_vec):
    row_mean = lax.optimization_barrier(jnp.mean(values, axis=-1, keepdims=True))
    centered = values - row_mean
    variance = lax.optimization_barrier(jnp.mean(centered * centered, axis=-1, keepdims=True))
    return centered * lax.rsqrt(variance + EPSILON) * gain_vec + shift_vec

def route_slots(pair_ids, pair_rank):
    pair_count = pair_ids.shape[0]
    ordered = jnp.zeros((pair_count,), jnp.int32).at[pair_rank].set(pair_ids)
    onehot = (ordered[:, None] == jnp.arange(EXPERTS, dtype=jnp.int32)[None, :]).astype(jnp.int32)
    before = (jnp.cumsum(onehot, axis=0) - onehot).astype(jnp.int32)
    position = lax.optimization_barrier(jnp.sum(before * onehot, axis=1)).astype(jnp.int32)[pair_rank]
    keep_mask = position < CAP
    slot_index = jnp.where(keep_mask, pair_ids * CAP + position, EXPERTS * CAP).astype(jnp.int32)
    return (slot_index, keep_mask)

def attend_group(group_rows, w_qkv, b_qv, w_out, b_out, ln1_gain, ln1_bias):
    tok_count = IMG_DEV * SEQ
    flat_rows = group_rows.reshape(tok_count, D)
    a_low = low(layer_norm(flat_rows, ln1_gain, ln1_bias))
    projected = jnp.einsum('td,cdf->ctf', a_low, w_qkv, precision=PRECISE)
    head_shape = (IMG_DEV, SEQ, HEADS, HDIM)
    queries = low(low_back(projected[0] + b_qv[0])).reshape(head_shape)
    key_rows = low(low_back(projected[1])).reshape(head_shape)
    values = low(low_back(projected[2] + b_qv[1])).reshape(head_shape)
    scores = low_back(jnp.einsum('bqhe,bkhe->bhqk', queries, key_rows, precision=PRECISE) * HDIM ** (-0.5))
    probs_low = low(jax.nn.softmax(scores, axis=-1))
    mixed = jnp.einsum('bhqk,bkhe->bqhe', probs_low, values, precision=PRECISE).reshape(tok_count, HEADS * HDIM)
    mixed_low = low(low_back(mixed))
    attention = low_back(jnp.dot(mixed_low, w_out, precision=PRECISE) + b_out)
    return flat_rows + attention

def expert_apply(row_block, up_weight, up_bias, down_weight, down_bias):
    flat_rows = row_block.reshape(-1, D)
    pre_act = low_back(jnp.dot(flat_rows, up_weight, precision=PRECISE) + up_bias)
    act_low = low(jax.nn.gelu(pre_act, approximate=False))
    return (jnp.dot(act_low, down_weight, precision=PRECISE) + down_bias).reshape(row_block.shape)

def forward(tokens, w_qkv, b_qv, w_out, b_out, ln1_gain, ln1_bias, ln2_gain, ln2_bias, w_router, w_up, b_up, w_down, b_down, choice_ids, slot_index, keep_float):
    groups = IMAGES // IMG_DEV
    tok_count = IMG_DEV * SEQ
    checked_attend = jax.checkpoint(attend_group)
    checked_expert = jax.checkpoint(expert_apply)
    hidden = lax.map(lambda group_rows: checked_attend(group_rows, w_qkv, b_qv, w_out, b_out, ln1_gain, ln1_bias), tokens.reshape(groups, IMG_DEV, SEQ, D))
    b_low = low(layer_norm(hidden, ln2_gain, ln2_bias))
    logits = low_back(jnp.einsum('gtd,de->gte', b_low, w_router, precision=PRECISE))
    router = jax.nn.softmax(logits, axis=-1)
    gate_values = jnp.take_along_axis(router, choice_ids, axis=2) * keep_float
    pair_rows = jnp.repeat(b_low, TOP, axis=1)
    buffers = jax.vmap(lambda slot_row, row_block: jnp.zeros((EXPERTS * CAP, D), jnp.float32).at[slot_row].set(row_block, mode='drop'))(slot_index, pair_rows)
    buffers = jnp.transpose(buffers.reshape(groups, EXPERTS, CAP, D), (1, 0, 2, 3))
    expert_out = lax.map(lambda packed: checked_expert(packed[0], packed[1], packed[2], packed[3], packed[4]), (buffers, w_up, b_up, w_down, b_down))
    expert_out = low_back(expert_out)
    expert_out = jnp.transpose(expert_out, (1, 0, 2, 3)).reshape(groups, EXPERTS * CAP, D)
    gather_at = jnp.minimum(slot_index, EXPERTS * CAP - 1)
    picked = jax.vmap(lambda out_table, index_row: out_table[index_row])(expert_out, gather_at).reshape(groups, tok_count, TOP, D)
    moe_out = lax.optimization_barrier(jnp.sum(picked * gate_values[..., None], axis=2))
    return (hidden + moe_out).reshape(IMAGES, SEQ, D)

def reference(tokens, expert_ids, pair_ranks, cotangent, w_qkv, b_qv, w_out, b_out, ln1_gain, ln1_bias, ln2_gain, ln2_bias, w_router, w_up, b_up, w_down, b_down):
    groups = IMAGES // IMG_DEV
    tok_count = IMG_DEV * SEQ
    choice_ids = expert_ids.reshape(groups, tok_count, TOP)
    slot_index, keep_mask = jax.vmap(route_slots)(expert_ids.reshape(groups, tok_count * TOP), pair_ranks.reshape(groups, tok_count * TOP))
    keep_float = keep_mask.astype(jnp.float32).reshape(groups, tok_count, TOP)
    floats = (tokens.astype(jnp.float32), w_qkv.astype(jnp.float32), b_qv.astype(jnp.float32), w_out.astype(jnp.float32), b_out.astype(jnp.float32), ln1_gain.astype(jnp.float32), ln1_bias.astype(jnp.float32), ln2_gain.astype(jnp.float32), ln2_bias.astype(jnp.float32), w_router.astype(jnp.float32), w_up.astype(jnp.float32), b_up.astype(jnp.float32), w_down.astype(jnp.float32), b_down.astype(jnp.float32))
    output, pullback = jax.vjp(lambda *params: forward(*params, choice_ids, slot_index, keep_float), *floats)
    gradients = pullback(cotangent.astype(jnp.float32))
    return (output.astype(jnp.bfloat16), gradients[0], gradients[1], gradients[2], gradients[3], gradients[4], gradients[5], gradients[6], gradients[7], gradients[8], gradients[9], gradients[10], gradients[11], gradients[12], gradients[13])
```

```python
import functools

import jax
import jax.numpy as jnp
from jax import lax
from jax.experimental import pallas as pl
from jax.experimental.pallas import tpu as pltpu
from jax.sharding import PartitionSpec as P

HDIM = 64
EPSILON = 1e-06
F32, BF16 = jnp.float32, jnp.bfloat16
EXACT = lax.Precision.HIGHEST
MESH = pl.DeviceIdType.MESH
NT = (((1,), (1,)), ((), ()))
TN = (((0,), (0,)), ((), ()))
NN = (((1,), (0,)), ((), ()))


def ceil_to(value, unit):
    return -(-value // unit) * unit


def mm(a, b, dims=NN, precision=None):
    return lax.dot_general(a, b, dims, precision=precision, preferred_element_type=F32)


def iota(shape, dim):
    return lax.broadcasted_iota(jnp.int32, shape, dim)


def onehot(mask):
    return jnp.where(mask, 1.0, 0.0).astype(F32)


class Sizes:
    def __init__(self, tokens, expert_ids, w_qkv, w_up):
        self.images, self.length, self.d = tokens.shape
        self.top = expert_ids.shape[2]
        self.tokens = self.images * self.length
        self.ea = lax.axis_size("ea")
        self.nq = lax.axis_size("ta")
        assert w_up.shape[0] == 1
        self.experts = self.ea
        self.cap = (9 * self.tokens * self.top + 8 * self.experts - 1) // (8 * self.experts)
        self.inner = w_qkv.shape[2]
        self.heads = self.inner // HDIM
        self.hidden = w_up.shape[2]
        self.lp = ceil_to(self.length, 16)
        self.tp = self.images * self.lp
        per_quarter = -(-self.tokens // self.nq)
        self.qt = ceil_to(per_quarter, 16)
        spread = (self.cap + (self.nq - 1) * self.experts) // self.nq
        self.cs = ceil_to(min(self.cap, per_quarter, spread), 16)
        self.ep = ceil_to(self.experts, 16)


def route(sz, expert_ids, pair_ranks):
    ids = expert_ids.reshape(-1)
    ranks = pair_ranks.reshape(-1)
    before = (ids[None, :] == ids[:, None]) & (ranks[None, :] < ranks[:, None])
    kept = jnp.sum(before, axis=1, dtype=jnp.int32) < sz.cap
    dest = jnp.where(kept, ids, sz.experts).reshape(sz.tokens, sz.top)
    low, high = jnp.min(dest, axis=1), jnp.max(dest, axis=1)
    key = (low * (sz.experts + 1) + high) * sz.tokens + jnp.arange(sz.tokens, dtype=jnp.int32)
    order = jnp.sum(key[None, :] < key[:, None], axis=1, dtype=jnp.int32)
    quarter, index = order % sz.nq, order // sz.nq
    pair_dest = dest.reshape(-1)
    pair_group = pair_dest * sz.nq + jnp.repeat(quarter, sz.top)
    pair_order = jnp.repeat(order, sz.top)
    earlier = (pair_group[None, :] == pair_group[:, None]) & (
        pair_order[None, :] < pair_order[:, None]
    )
    slot = jnp.sum(earlier, axis=1, dtype=jnp.int32)
    place = jnp.where(pair_dest < sz.experts, pair_dest * sz.cs + slot, -1)
    place = place.reshape(sz.tokens, sz.top)
    perm = (quarter * sz.qt + index).reshape(sz.images, sz.length)
    perm = jnp.pad(perm, ((0, 0), (0, sz.lp - sz.length)), constant_values=-1).reshape(sz.tp)
    mine = lax.axis_index("ta")
    wanted = jnp.arange(sz.qt, dtype=jnp.int32) * sz.nq + mine
    member = order[None, :] == wanted[:, None]
    place_mine = (
        jnp.sum(jnp.where(member[:, :, None], place[None] + 1, 0), axis=1, dtype=jnp.int32) - 1
    )
    return perm, place_mine


def layer_norm(values, gain_vec, shift_vec):
    row_mean = jnp.mean(values, axis=-1, keepdims=True)
    centered = values - row_mean
    variance = jnp.mean(centered * centered, axis=-1, keepdims=True)
    inverse = lax.rsqrt(variance + EPSILON)
    normed = centered * inverse
    return (normed * gain_vec + shift_vec, normed, inverse)


def norm_back(grad_rows, normed, inverse, gain_vec):
    scaled = grad_rows * gain_vec
    return inverse * (
        scaled
        - jnp.mean(scaled, axis=-1, keepdims=True)
        - normed * jnp.mean(scaled * normed, axis=-1, keepdims=True)
    )


def push(src, dst, send_sem, recv_sem, device):
    return pltpu.make_async_remote_copy(
        src_ref=src,
        dst_ref=dst,
        send_sem=send_sem,
        recv_sem=recv_sem,
        device_id=device,
        device_id_type=MESH,
    )


def meet(devices):
    barrier = pltpu.get_barrier_semaphore()
    for device in devices:
        pl.semaphore_signal(barrier, inc=1, device_id=device, device_id_type=MESH)
    pl.semaphore_wait(barrier, len(devices))


def head_mask(sz, head, dtype):
    lane = iota((1, sz.inner), 1)
    return onehot((lane >= head * HDIM) & (lane < (head + 1) * HDIM)).astype(dtype)


def front_kernel(
    sz,
    tok_ref,
    cot_ref,
    wqkv_ref,
    bqv_ref,
    wout_ref,
    bout_ref,
    gain1_ref,
    bias1_ref,
    gain2_ref,
    bias2_ref,
    router_ref,
    perm_ref,
    place_ref,
    rows_all,
    dy_all,
    gate_all,
    q_out,
    k_out,
    v_out,
    mixed_out,
    lse_out,
    hidden_out,
    low_out,
    probs_out,
    dy_out,
    padded,
    w_full,
    mixed_in,
    mixed_send,
    dy_send,
    row_send,
    gate_send,
    w_sem,
    mixed_sem,
    dyz_sem,
    dyt_sem,
    rowz_sem,
    rowt_sem,
    gatez_sem,
    gatet_sem,
):
    z, j = lax.axis_index("ea"), lax.axis_index("ta")
    nq, ea = sz.nq, sz.ea
    ta_peer = [{"ta": lax.rem(j + p, nq)} for p in range(nq)]
    ea_peer = [{"ea": lax.rem(z + s, ea)} for s in range(ea)]
    meet(ta_peer[1:] + ea_peer[1:])

    started = []

    def go(copy):
        copy.start()
        started.append(copy)

    def from_ta(ref, p, sem, *more):
        source = lax.rem(j - p + nq, nq)
        index = (source,) + more
        push(ref.at[index], ref.at[index], sem, sem, ta_peer[p]).wait_recv()

    for p in range(1, nq):
        go(push(wout_ref, w_full.at[j], w_sem.at[0, p], w_sem.at[1, p], ta_peer[p]))
    w_full[j] = wout_ref[...]

    perm = perm_ref[...]
    pick_all = onehot(iota((nq * sz.qt, sz.tp), 0) == perm).astype(BF16)
    pick_mine = onehot(iota((sz.qt, sz.tp), 0) + j * sz.qt == perm).astype(BF16)
    place = place_ref[...]

    def slots_of(expert):
        row = iota((sz.cs, sz.qt), 0) + expert * sz.cs
        return onehot((row == place[0:1]) | (row == place[1:2])).astype(BF16)

    tail = (sz.length // 16) * 16
    for image in range(sz.images):
        padded[image, tail:] = jnp.zeros((sz.lp - tail, sz.d), BF16)
        padded[image, 0 : sz.length] = cot_ref[image]
    dy_mine = mm(pick_mine, padded[...].reshape(sz.tp, sz.d)).astype(BF16)
    dy_out[...] = dy_mine
    for expert in range(sz.experts):
        dy_send[expert] = mm(slots_of(expert), dy_mine).astype(BF16)
    for s in range(1, ea):
        to = lax.rem(z + s, ea)
        go(push(dy_send.at[to], dy_all.at[j, z], dyz_sem.at[0, s], dyz_sem.at[1, s], ea_peer[s]))
    dy_all[j, z] = dy_send[z]

    def forward(ref, z_sem, t_sem):
        for s in range(ea):
            source = lax.rem(z - s + ea, ea)
            block = ref.at[j, source]
            if s:
                push(block, block, z_sem.at[1, s], z_sem.at[1, s], ea_peer[s]).wait_recv()
            for p in range(1, nq):
                go(push(block, block, t_sem.at[0, p, s], t_sem.at[1, p, s], ta_peer[p]))

    for image in range(sz.images):
        padded[image, 0 : sz.length] = tok_ref[image]
    x_pad = padded[...].reshape(sz.tp, sz.d)
    normed_one, _, _ = layer_norm(x_pad.astype(F32), gain1_ref[...], bias1_ref[...])
    a_low = normed_one.astype(BF16)
    q_out[...] = (mm(a_low, wqkv_ref[0]) + bqv_ref[0:1]).astype(BF16).reshape(q_out.shape)
    k_out[...] = mm(a_low, wqkv_ref[1]).astype(BF16).reshape(q_out.shape)
    v_out[...] = (mm(a_low, wqkv_ref[2]) + bqv_ref[1:2]).astype(BF16).reshape(q_out.shape)

    forward(dy_all, dyz_sem, dyt_sem)

    live = iota((1, sz.lp), 1) < sz.length
    for image in range(sz.images):
        queries, keys, values = q_out[image], k_out[image], v_out[image]
        mixed = jnp.zeros((sz.lp, sz.inner), F32)
        logs = jnp.zeros((sz.lp, 128), F32)
        for head in range(sz.heads):
            scores = mm(queries * head_mask(sz, head, BF16), keys, NT) * HDIM ** (-0.5)
            scores = jnp.where(live, scores, -1e30)
            peak = jnp.max(scores, axis=-1, keepdims=True)
            exps = jnp.exp(scores - peak)
            total = jnp.sum(exps, axis=-1, keepdims=True)
            probs_low = (exps / total).astype(BF16)
            mixed = mixed + mm(probs_low, values) * head_mask(sz, head, F32)
            logs = logs + jnp.where(iota((1, 128), 1) == head, peak + jnp.log(total), 0.0)
        mixed_out[image] = mixed.astype(BF16)
        lse_out[image] = logs
    dealt = mm(pick_all, mixed_out[...].reshape(sz.tp, sz.inner)).astype(BF16)
    mixed_send[...] = dealt.reshape(nq, sz.qt, sz.inner)
    for p in range(1, nq):
        to = lax.rem(j + p, nq)
        go(
            push(
                mixed_send.at[to],
                mixed_in.at[j],
                mixed_sem.at[0, p],
                mixed_sem.at[1, p],
                ta_peer[p],
            )
        )
    mixed_in[j] = mixed_send[j]
    x_mine = mm(pick_mine, padded[...].reshape(sz.tp, sz.d))
    for p in range(1, nq):
        from_ta(w_full, p, w_sem.at[1, p])
    for p in range(1, nq):
        from_ta(mixed_in, p, mixed_sem.at[1, p])

    attention = bout_ref[...]
    for q in range(nq):
        attention = attention + mm(mixed_in[q], w_full[q])
    hidden = x_mine + attention
    hidden_out[...] = hidden
    normed_two, _, _ = layer_norm(hidden, gain2_ref[...], bias2_ref[...])
    b_low = normed_two.astype(BF16)
    low_out[...] = b_low
    logits = mm(router_ref[...], b_low, NT)
    logits = jnp.where(iota((sz.ep, 1), 0) < sz.experts, logits, -1e30)
    exps = jnp.exp(logits - jnp.max(logits, axis=0, keepdims=True))
    router = exps / jnp.sum(exps, axis=0, keepdims=True)
    probs_out[...] = router
    for expert in range(sz.experts):
        slots = slots_of(expert)
        row_send[expert] = mm(slots, b_low).astype(BF16)
        level = jnp.broadcast_to(router[expert : expert + 1], (8, sz.qt))
        gate_send[expert, :, 0 : sz.cs] = mm(level, slots.astype(F32), NT, EXACT)
    for s in range(1, ea):
        to = lax.rem(z + s, ea)
        go(
            push(
                gate_send.at[to],
                gate_all.at[j, z],
                gatez_sem.at[0, s],
                gatez_sem.at[1, s],
                ea_peer[s],
            )
        )
        go(
            push(
                row_send.at[to],
                rows_all.at[j, z],
                rowz_sem.at[0, s],
                rowz_sem.at[1, s],
                ea_peer[s],
            )
        )
    rows_all[j, z] = row_send[z]
    gate_all[j, z] = gate_send[z]
    forward(rows_all, rowz_sem, rowt_sem)
    forward(gate_all, gatez_sem, gatet_sem)
    for ref, sem in ((dy_all, dyt_sem), (rows_all, rowt_sem), (gate_all, gatet_sem)):
        for p in range(1, nq):
            for s in range(ea):
                from_ta(ref, p, sem.at[1, p, s], lax.rem(z - s + ea, ea))
    for copy in started:
        copy.wait_send()


def front(sz, args, perm, place):
    (tokens, cotangent, w_qkv, b_qv, w_out, b_out, g1, c1, g2, c2, w_router) = args
    row = lambda vec: vec.reshape(1, -1)
    router_rows = jnp.pad(w_router.T, ((0, sz.ep - sz.experts), (0, 0)))
    vm = pl.BlockSpec(memory_space=pltpu.VMEM)
    shape = jax.ShapeDtypeStruct
    outs = (
        shape((sz.nq, sz.ea, sz.cs, sz.d), BF16),
        shape((sz.nq, sz.ea, sz.cs, sz.d), BF16),
        shape((sz.nq, sz.ea, 8, 128), F32),
        shape((sz.images, sz.lp, sz.inner), BF16),
        shape((sz.images, sz.lp, sz.inner), BF16),
        shape((sz.images, sz.lp, sz.inner), BF16),
        shape((sz.images, sz.lp, sz.inner), BF16),
        shape((sz.images, sz.lp, 128), F32),
        shape((sz.qt, sz.d), F32),
        shape((sz.qt, sz.d), BF16),
        shape((sz.ep, sz.qt), F32),
        shape((sz.qt, sz.d), BF16),
    )
    dma = pltpu.SemaphoreType.DMA
    scratch = [
        pltpu.VMEM((sz.images, sz.lp, sz.d), BF16),
        pltpu.VMEM((sz.nq, sz.inner, sz.d), BF16),
        pltpu.VMEM((sz.nq, sz.qt, sz.inner), BF16),
        pltpu.VMEM((sz.nq, sz.qt, sz.inner), BF16),
        pltpu.VMEM((sz.experts, sz.cs, sz.d), BF16),
        pltpu.VMEM((sz.experts, sz.cs, sz.d), BF16),
        pltpu.VMEM((sz.experts, 8, 128), F32),
        dma((2, sz.nq)),
        dma((2, sz.nq)),
        dma((2, sz.ea)),
        dma((2, sz.nq, sz.ea)),
        dma((2, sz.ea)),
        dma((2, sz.nq, sz.ea)),
        dma((2, sz.ea)),
        dma((2, sz.nq, sz.ea)),
    ]
    return pl.pallas_call(
        functools.partial(front_kernel, sz),
        out_shape=outs,
        in_specs=[vm] * 13,
        out_specs=[vm] * len(outs),
        scratch_shapes=scratch,
        name="front",
        compiler_params=pltpu.CompilerParams(
            collective_id=0, has_side_effects=True, vmem_limit_bytes=56 << 20
        ),
    )(
        tokens,
        cotangent,
        w_qkv,
        b_qv,
        w_out,
        row(b_out),
        row(g1),
        row(c1),
        row(g2),
        row(c2),
        router_rows,
        perm.reshape(1, -1),
        place.T,
    )


def gelu_parts(values):
    cdf = 0.5 * (1.0 + lax.erf(values * (0.5**0.5)))
    density = jnp.exp(-0.5 * values * values) * (0.5 / jnp.pi) ** 0.5
    return cdf, density


def local(
    tokens,
    expert_ids,
    pair_ranks,
    cotangent,
    w_qkv,
    b_qv,
    w_out,
    b_out,
    ln1_gain,
    ln1_bias,
    ln2_gain,
    ln2_bias,
    w_router,
    w_up,
    b_up,
    w_down,
    b_down,
):
    sz = Sizes(tokens, expert_ids, w_qkv, w_up)
    nq, ea, cs, d = sz.nq, sz.ea, sz.cs, sz.d
    perm, place = route(sz, expert_ids, pair_ranks)
    (rows_all, dy_all, gate_all, q, k, v, mixed, lse, hidden, b_low, router, dy_mine) = front(
        sz,
        (tokens, cotangent, w_qkv, b_qv, w_out, b_out, ln1_gain, ln1_bias, ln2_gain, ln2_bias, w_router),
        perm,
        place,
    )
    total = nq * ea * cs
    rows, dy = rows_all.reshape(total, d), dy_all.reshape(total, d)
    gate = gate_all[:, :, 0, :cs].reshape(total, 1)
    pre_act = mm(rows, w_up[0]) + b_up
    cdf, density = gelu_parts(pre_act)
    act_low = (pre_act * cdf).astype(BF16)
    first = jnp.where(lax.axis_index("ta") == 0, 1.0, 0.0)
    expert_out = mm(act_low, w_down[0]) + first * b_down
    dgate_slot = jnp.sum(expert_out * dy.astype(F32), axis=1)
    slot_grad = (gate * dy.astype(F32)).astype(BF16)
    pre_grad = (mm(slot_grad, w_down[0], NT) * (cdf + pre_act * density)).astype(BF16)
    row_grad = mm(pre_grad, w_up[0], NT)
    up_grad, down_grad = mm(rows, pre_grad, TN), mm(act_low, slot_grad, TN)
    up_bias_grad = jnp.sum(pre_grad, axis=0, dtype=F32)
    down_bias_grad = jnp.sum(slot_grad, axis=0, dtype=F32)

    def home(values):
        part = lax.psum_scatter(values.reshape(nq, ea, cs, -1), "ta", scatter_dimension=0)
        return lax.all_to_all(part, "ea", 0, 0, tiled=True).reshape(ea * cs, -1)

    out_back = home(expert_out * gate).astype(BF16)
    grad_back = home(row_grad).astype(BF16)
    dgate_back = home(jnp.broadcast_to(dgate_slot[:, None], (total, 128)))[:, 0]
    slots = onehot(
        (iota((ea * cs, sz.qt), 0) == place[:, 0]) | (iota((ea * cs, sz.qt), 0) == place[:, 1])
    )
    slots_low = slots.astype(BF16)
    output_mine = (hidden + mm(slots_low, out_back, TN)).astype(BF16)
    own = onehot(iota((sz.ep, ea * cs), 0) == iota((sz.ep, ea * cs), 1) // cs)
    drouter = mm(own * dgate_back[None, :], slots, NN, EXACT)
    dlogits = (router * (drouter - jnp.sum(router * drouter, axis=0, keepdims=True))).astype(BF16)
    router_rows = jnp.pad(w_router.T, ((0, sz.ep - sz.experts), (0, 0)))
    into_two = mm(slots_low, grad_back, TN) + mm(dlogits, router_rows, TN)
    _, hat_two, inv_two = layer_norm(hidden, ln2_gain, ln2_bias)
    dhidden = dy_mine.astype(F32) + norm_back(into_two, hat_two, inv_two, ln2_gain)
    dattn_mine = dhidden.astype(BF16)
    small = [
        mm(dlogits, b_low),
        jnp.sum(into_two * hat_two, axis=0, keepdims=True),
        jnp.sum(into_two, axis=0, keepdims=True),
        jnp.sum(dattn_mine, axis=0, keepdims=True, dtype=F32),
    ]

    def gather(mine):
        return lax.all_gather(mine, "ta").reshape(nq * sz.qt, -1)

    pick = onehot(perm[:, None] == iota((sz.tp, nq * sz.qt), 1)).astype(BF16)
    dattn = mm(pick, gather(dattn_mine)).astype(BF16)
    out_grad = mm(mixed.reshape(sz.tp, -1), dattn, TN)
    head_shape = (sz.images, sz.lp, sz.heads, HDIM)
    dmixed = mm(dattn, w_out, NT).astype(BF16).reshape(head_shape)
    q, k, v = (t.reshape(head_shape) for t in (q, k, v))
    ein = functools.partial(jnp.einsum, preferred_element_type=F32)
    scale = HDIM ** (-0.5)
    scores = ein("bqhe,bkhe->bhqk", q, k) * scale
    live = jnp.arange(sz.lp) < sz.length
    logs = jnp.transpose(lse[:, :, : sz.heads], (0, 2, 1))[..., None]
    probs = jnp.where(live, jnp.exp(scores - logs), 0.0)
    dvalue = ein("bhqk,bqhe->bkhe", probs.astype(BF16), dmixed)
    dprobs = ein("bqhe,bkhe->bhqk", dmixed, v)
    dscores = (probs * (dprobs - jnp.sum(probs * dprobs, axis=-1, keepdims=True))).astype(BF16)
    dquery = ein("bhqk,bkhe->bqhe", dscores, k) * scale
    dkey = ein("bhqk,bqhe->bkhe", dscores, q) * scale
    dproj = [t.reshape(sz.tp, sz.inner).astype(BF16) for t in (dquery, dkey, dvalue)]
    x_pad = jnp.pad(tokens, ((0, 0), (0, sz.lp - sz.length), (0, 0))).reshape(sz.tp, d)
    normed_one, hat_one, inv_one = layer_norm(x_pad.astype(F32), ln1_gain, ln1_bias)
    a_low = normed_one.astype(BF16)
    qkv_grad = jnp.stack([mm(a_low, t, TN) for t in dproj])
    qv_bias_grad = jnp.stack([jnp.sum(dproj[c], axis=0, dtype=F32) for c in (0, 2)])
    into_part = sum(mm(t, w_qkv[c], NT) for c, t in enumerate(dproj))
    small += [
        jnp.sum(into_part * hat_one, axis=0, keepdims=True),
        jnp.sum(into_part, axis=0, keepdims=True),
    ]
    dealt = mm(pick, into_part.astype(BF16), TN).reshape(nq, sz.qt, d)
    into_one = lax.psum_scatter(dealt, "ta", scatter_dimension=0)
    mine = lax.axis_index("ta")
    pick_mine = lax.dynamic_slice_in_dim(pick, mine * sz.qt, sz.qt, 1)
    x_mine = mm(pick_mine, x_pad, TN)
    _, hat_mine, inv_mine = layer_norm(x_mine, ln1_gain, ln1_bias)
    input_mine = (dhidden + norm_back(into_one, hat_mine, inv_mine, ln1_gain)).astype(BF16)

    def natural(mine_rows, dtype):
        full = mm(pick, gather(mine_rows)).astype(dtype)
        return full.reshape(sz.images, sz.lp, d)[:, : sz.length]

    output, input_grad = natural(output_mine, BF16), natural(input_mine, F32)
    qkv_grad, qv_bias_grad, out_grad = lax.psum((qkv_grad, qv_bias_grad, out_grad), ("ea", "dev"))
    small = lax.psum(jnp.concatenate(small), ("ea", "ta", "dev"))
    up_grad, up_bias_grad, down_grad, down_bias_grad = lax.psum(
        (up_grad, up_bias_grad, down_grad, down_bias_grad), "dev"
    )
    return (
        output,
        input_grad,
        qkv_grad,
        qv_bias_grad,
        out_grad,
        small[sz.ep + 2],
        small[sz.ep + 3],
        small[sz.ep + 4],
        small[sz.ep],
        small[sz.ep + 1],
        small[: sz.experts].T,
        up_grad[None],
        up_bias_grad[None],
        down_grad[None],
        down_bias_grad[None],
    )


def solution(mesh):
    in_specs = (
        P(("ea", "dev"), None, None),
        P(("ea", "dev"), None, None),
        P(("ea", "dev"), None, None),
        P(("ea", "dev"), None, None),
        P(None, None, "ta"),
        P(None, "ta"),
        P("ta", None),
        P(),
        P(),
        P(),
        P(),
        P(),
        P(),
        P("ea", None, "ta"),
        P("ea", "ta"),
        P("ea", "ta", None),
        P("ea", None),
    )
    out_specs = (
        P(("ea", "dev"), None, None),
        P(("ea", "dev"), None, None),
        P(None, None, "ta"),
        P(None, "ta"),
        P("ta", None),
        P(),
        P(),
        P(),
        P(),
        P(),
        P(),
        P("ea", None, "ta"),
        P("ea", "ta"),
        P("ea", "ta", None),
        P("ea", None),
    )
    return jax.shard_map(local, mesh=mesh, in_specs=in_specs, out_specs=out_specs, check_vma=False)
```

```python
import functools
import types

import jax
import jax.numpy as jnp
from jax import lax
from jax.experimental import pallas as pl
from jax.experimental.pallas import tpu as pltpu
from jax.sharding import PartitionSpec as P

HDIM = 64
EPSILON = 1e-06
F32, BF16 = jnp.float32, jnp.bfloat16
EXACT = lax.Precision.HIGHEST
MESH = pl.DeviceIdType.MESH
NT = (((1,), (1,)), ((), ()))
TN = (((0,), (0,)), ((), ()))
NN = (((1,), (0,)), ((), ()))


def ceil_to(value, unit):
    return -(-value // unit) * unit


def mm(a, b, dims=NN, precision=None):
    return lax.dot_general(a, b, dims, precision=precision, preferred_element_type=F32)


def iota(shape, dim):
    return lax.broadcasted_iota(jnp.int32, shape, dim)


def onehot(mask):
    return jnp.where(mask, 1.0, 0.0).astype(F32)


class Sizes:
    def __init__(self, tokens, expert_ids, w_qkv, w_up):
        self.images, self.length, self.d = tokens.shape
        self.top = expert_ids.shape[2]
        self.tokens = self.images * self.length
        self.ea = lax.axis_size("ea")
        self.nq = lax.axis_size("ta")
        assert w_up.shape[0] == 1
        self.experts = self.ea
        self.cap = (9 * self.tokens * self.top + 8 * self.experts - 1) // (8 * self.experts)
        self.inner = w_qkv.shape[2]
        self.heads = self.inner // HDIM
        self.hidden = w_up.shape[2]
        self.lp = ceil_to(self.length, 16)
        self.tp = self.images * self.lp
        per_quarter = -(-self.tokens // self.nq)
        self.qt = ceil_to(per_quarter, 16)
        spread = (self.cap + (self.nq - 1) * self.experts) // self.nq
        self.cs = ceil_to(min(self.cap, per_quarter, spread), 16)
        self.ep = ceil_to(self.experts, 16)
        self.half = self.inner // 2
        self.piece = self.half // self.ea
        self.early = ceil_to(self.experts + 3, 8)
        self.blocks = max(1, min(self.ea, (256 if self.ea <= 8 else 64) // self.cs))
        self.chunks = self.ea // self.blocks
        self.direct = self.ea <= 8
        assert self.top == 2 and self.nq == 4


def route(sz, table):
    rows = [table[n : n + 1, : sz.tp] for n in range(4)]
    cols = table.T[: sz.tp]
    wide = iota((sz.tp, 128), 1)

    def count(mask):
        return jnp.sum(jnp.where(mask, 1.0, 0.0), axis=1, keepdims=True)

    def flip(*columns):
        spread = jnp.zeros((sz.tp, 128), F32)
        for n, column in enumerate(columns):
            spread = spread + jnp.where(wide == n, column, 0.0)
        turned = spread.T
        return [turned[n : n + 1] for n in range(len(columns))]

    real = cols[:, 0:1] < sz.experts
    dest = []
    for k in range(2):
        ids, ranks = cols[:, k : k + 1], cols[:, 2 + k : 3 + k]
        position = sum(count((rows[m] == ids) & (rows[2 + m] < ranks)) for m in range(2))
        dest.append(jnp.where((position < sz.cap) & real, ids, float(sz.experts)))
    low, high = jnp.minimum(*dest), jnp.maximum(*dest)
    index = iota((sz.tp, 1), 0).astype(F32)
    kind = jnp.where(real, low * (sz.experts + 1) + high, float((sz.experts + 1) ** 2))
    key = kind * sz.tp + index
    (key_row,) = flip(key)
    order = count(key_row < key)
    lap = jnp.floor((order + 0.5) * (1.0 / sz.nq))
    quarter = order - lap * sz.nq
    group = [d * sz.nq + quarter for d in dest]
    perm = jnp.where(real, quarter * sz.qt + lap, -1.0)
    order_row, perm_row, *group_row = flip(order, perm, *group)
    place = []
    for k in range(2):
        slot = sum(count((group_row[m] == group[k]) & (order_row < order)) for m in range(2))
        place.append(jnp.where(dest[k] < sz.experts, dest[k] * sz.cs + slot + 1.0, 0.0))
    place_row = flip(*place)
    return perm, perm_row, place, place_row


def layer_norm(values, gain_vec, shift_vec):
    row_mean = jnp.mean(values, axis=-1, keepdims=True)
    centered = values - row_mean
    variance = jnp.mean(centered * centered, axis=-1, keepdims=True)
    inverse = lax.rsqrt(variance + EPSILON)
    normed = centered * inverse
    return (normed * gain_vec + shift_vec, normed, inverse)


def norm_back(grad_rows, normed, inverse, gain_vec):
    scaled = grad_rows * gain_vec
    return inverse * (
        scaled
        - jnp.mean(scaled, axis=-1, keepdims=True)
        - normed * jnp.mean(scaled * normed, axis=-1, keepdims=True)
    )


def push(src, dst, send_sem, recv_sem, device):
    return pltpu.make_async_remote_copy(
        src_ref=src,
        dst_ref=dst,
        send_sem=send_sem,
        recv_sem=recv_sem,
        device_id=device,
        device_id_type=MESH,
    )


def meet(devices):
    barrier = pltpu.get_barrier_semaphore()
    for device in devices:
        pl.semaphore_signal(barrier, inc=1, device_id=device, device_id_type=MESH)
    pl.semaphore_wait(barrier, len(devices))


def head_mask(sz, head, dtype):
    lane = iota((1, sz.inner), 1)
    return onehot((lane >= head * HDIM) & (lane < (head + 1) * HDIM)).astype(dtype)


def gelu_parts(values):
    cdf = 0.5 * (1.0 + lax.erf(values * (0.5**0.5)))
    density = jnp.exp(-0.5 * values * values) * (0.5 / jnp.pi) ** 0.5
    return cdf, density


def block_kernel(sz, names, *refs):
    r = types.SimpleNamespace(**dict(zip(names, refs)))
    z, j, c = lax.axis_index("ea"), lax.axis_index("ta"), lax.axis_index("dev")
    nq, ea, d, cs, qt = sz.nq, sz.ea, sz.d, sz.cs, sz.qt
    quarter = [j, j + 1 - 2 * lax.rem(j, 2), j + 2 - 4 * lax.div(j, 2), 3 - j]
    ta_peer = [{"ta": q} for q in quarter]
    ea_peer = [{"ea": lax.rem(z + s, ea)} for s in range(ea)]
    source = [lax.rem(z - s + ea, ea) for s in range(ea)]
    target = [lax.rem(z + s, ea) for s in range(ea)]
    other = {"dev": 1 - c}
    later = [s for s in range(1, ea)]
    partners = (1, 2, 3)
    started = []

    def go(src, dst, sem, index, device):
        index = index if isinstance(index, tuple) else (index,)
        copy = push(src, dst, sem.at[(0,) + index], sem.at[(1,) + index], device)
        copy.start()
        started.append(copy)
        return copy

    def got(dst, sem, index, device):
        index = index if isinstance(index, tuple) else (index,)
        push(dst, dst, sem.at[(1,) + index], sem.at[(1,) + index], device).wait_recv()

    load_up = pltpu.make_async_copy(r.w_up, r.up_w, r.load_sem.at[0])
    load_down = pltpu.make_async_copy(r.w_down, r.down_w, r.load_sem.at[1])
    load_up.start()
    load_down.start()

    meet(ta_peer[1:] + ea_peer[1:] + [other])

    for p in partners:
        go(r.w_out.at[c], r.w_full.at[j, c], r.w_sem, p, ta_peer[p])
    r.w_full[j] = r.w_out[...]

    perm_col, perm, place, place_rows = route(sz, r.table[...])
    perm = perm.astype(jnp.int32)
    r.perm_col[...] = jnp.broadcast_to(perm_col, (sz.tp, 128))
    pick_all = onehot(iota((nq * qt, sz.tp), 0) == perm).astype(BF16)

    def pick_of(q):
        return onehot(iota((qt, sz.tp), 0) + q * qt == perm).astype(BF16)

    spread = iota((8, 1), 0)
    both = jnp.where(spread == 0, place_rows[0], 0.0) + jnp.where(spread == 1, place_rows[1], 0.0)
    for which, q in ((0, quarter[0]), (1, quarter[3])):
        chosen = mm(both, onehot(iota((qt, sz.tp), 0) + q * qt == perm), NT, EXACT)
        r.place_row[2 * which : 2 * which + 2] = (chosen[0:2] + 0.5).astype(jnp.int32) - 1
    pair_col = jnp.where(iota((1, 128), 1) == 0, place[0], 0.0)
    pair_col = pair_col + jnp.where(iota((1, 128), 1) == 1, place[1], 0.0)
    chosen = mm(onehot(iota((qt, sz.tp), 0) + j * qt == perm), pair_col, NN, EXACT)
    r.place_col[...] = (chosen + 0.5).astype(jnp.int32) - 1

    def slots_of(expert, which):
        row = iota((cs, qt), 0) + expert * cs
        first, second = r.place_row[2 * which : 2 * which + 1], r.place_row[2 * which + 1 : 2 * which + 2]
        return onehot((row == first) | (row == second))

    tail = (sz.length // 16) * 16
    for image in range(sz.images):
        r.padded[image, tail:] = jnp.zeros((sz.lp - tail, d), BF16)
        r.padded[image, 0 : sz.length] = r.cot[image]
    for which, q in ((0, quarter[0]), (1, quarter[3])):
        dy_rows = mm(pick_of(q), r.padded[...].reshape(sz.tp, d)).astype(BF16)
        if which == 0:
            r.dy_mine[...] = dy_rows
        for expert in range(sz.experts):
            r.dy_send[which, expert] = mm(slots_of(expert, which).astype(BF16), dy_rows).astype(BF16)
    dy_copies = []
    for which, q in ((0, quarter[0]), (1, quarter[3])):
        for s in later:
            copy = go(r.dy_send.at[which, target[s]], r.dy_all.at[q, z], r.dyz_sem, (which, s), ea_peer[s])
            dy_copies.append(copy)
        r.dy_all[q, z] = r.dy_send[which, z]

    def forward(ref, z_sem, t_sem):
        copies = []
        for s in range(ea):
            block = ref.at[j, source[s]]
            if s:
                got(block, z_sem, (0, s), ea_peer[s])
            for p in (1, 2):
                copies.append(go(block, block, t_sem, (p, s), ta_peer[p]))
        return copies

    for image in range(sz.images):
        r.padded[image, 0 : sz.length] = r.tok[image]
    normed_one, _, _ = layer_norm(
        r.padded[...].reshape(sz.tp, d).astype(F32), flat_row(r.gain1), flat_row(r.bias1)
    )
    a_low = normed_one.astype(BF16)
    r.a_low[...] = a_low
    flat = (sz.images, sz.lp, sz.inner)
    r.q[...] = (mm(a_low, r.w_qkv[0], NT) + r.b_qv[0:1]).astype(BF16).reshape(flat)
    r.k[...] = mm(a_low, r.w_qkv[1], NT).astype(BF16).reshape(flat)
    r.v[...] = (mm(a_low, r.w_qkv[2], NT) + r.b_qv[1:2]).astype(BF16).reshape(flat)

    dy_forwards = forward(r.dy_all, r.dyz_sem, r.dyt_sem)
    for p in partners:
        block = r.w_full.at[quarter[p], c]
        got(block, r.w_sem, p, ta_peer[p])
        go(block, block, r.wd_sem, p, other)

    scale = HDIM ** (-0.5)
    live = iota((1, sz.lp), 1) < sz.length
    for image in range(sz.images):
        queries, keys, values = r.q[image], r.k[image], r.v[image]
        mixed = jnp.zeros((sz.lp, sz.inner), F32)
        logs = jnp.zeros((sz.lp, 128), F32)
        for head in range(sz.heads):
            scores = mm(queries * head_mask(sz, head, BF16), keys, NT) * scale
            scores = jnp.where(live, scores, -1e30)
            peak = jnp.max(scores, axis=-1, keepdims=True)
            exps = jnp.exp(scores - peak)
            total = jnp.sum(exps, axis=-1, keepdims=True)
            probs_low = (exps / total).astype(BF16)
            mixed = mixed + mm(probs_low, values) * head_mask(sz, head, F32)
            logs = logs + jnp.where(iota((1, 128), 1) == head, peak + jnp.log(total), 0.0)
        r.mixed[image] = mixed.astype(BF16)
        r.lse[image] = logs
    dealt = mm(pick_all, r.mixed[...].reshape(sz.tp, sz.inner)).astype(BF16)
    r.mix_send[...] = dealt.reshape(nq, qt, sz.inner)
    for p in partners:
        go(r.mix_send.at[quarter[p]], r.mix_in.at[0, j], r.mix_sem, (0, p), ta_peer[p])
        go(r.mix_send.at[quarter[3 - p]], r.mix_in.at[1, j], r.mix_sem, (1, p), ta_peer[p])
    r.mix_in[0, j] = r.mix_send[j]
    r.mix_in[1, j] = r.mix_send[quarter[3]]
    x_rows = [mm(pick_of(q), r.padded[...].reshape(sz.tp, d)) for q in (quarter[0], quarter[3])]
    for p in partners:
        got(r.w_full.at[quarter[p], 1 - c], r.wd_sem, p, other)
    for p in partners:
        got(r.mix_in.at[0, quarter[p]], r.mix_sem, (0, p), ta_peer[p])
        got(r.mix_in.at[1, quarter[p]], r.mix_sem, (1, p), ta_peer[p])

    finished = []
    if not sz.direct:
        r.row_send = r.dy_send
        for copy in dy_copies:
            copy.wait_send()
        finished += dy_copies
    router_w = r.router[...]
    if sz.ep > sz.experts:
        router_w = jnp.concatenate([router_w, jnp.zeros((sz.ep - sz.experts, d), BF16)])
    for which in (0, 1):
        attention = flat_row(r.b_out)
        for q in range(nq):
            attention = attention + mm(r.mix_in[which, q], r.w_full[q].reshape(sz.inner, d))
        hidden = x_rows[which] + attention
        normed_two, _, _ = layer_norm(hidden, flat_row(r.gain2), flat_row(r.bias2))
        b_low = normed_two.astype(BF16)
        logits = mm(router_w, b_low, NT)
        logits = jnp.where(iota((sz.ep, 1), 0) < sz.experts, logits, -1e30)
        exps = jnp.exp(logits - jnp.max(logits, axis=0, keepdims=True))
        router = exps / jnp.sum(exps, axis=0, keepdims=True)
        if which == 0:
            r.hidden[...], r.b_low[...], r.probs[...] = hidden, b_low, router
        for expert in range(sz.experts):
            slots = slots_of(expert, which)
            r.row_send[which, expert] = mm(slots.astype(BF16), b_low).astype(BF16)
            level = jnp.broadcast_to(router[expert : expert + 1], (8, qt))
            r.gate_send[which, expert, :, 0:cs] = mm(level, slots, NT, EXACT)
        q = quarter[3 * which]
        for s in later:
            t = target[s]
            go(r.gate_send.at[which, t], r.gate_all.at[q, z], r.gatez_sem, (which, s), ea_peer[s])
            go(r.row_send.at[which, t], r.rows_all.at[q, z], r.rowz_sem, (which, s), ea_peer[s])
        r.rows_all[q, z] = r.row_send[which, z]
        r.gate_all[q, z] = r.gate_send[which, z]
    row_forwards = forward(r.rows_all, r.rowz_sem, r.rowt_sem)
    for s in later:
        got(r.gate_all.at[j, source[s]], r.gatez_sem, (0, s), ea_peer[s])
    for p in (1, 2):
        go(r.gate_all.at[j], r.gate_all.at[j], r.gatet_sem, p, ta_peer[p])

    load_up.wait()
    load_down.wait()
    first = jnp.where(j == 0, 1.0, 0.0)
    spot = iota((cs, cs), 0) == iota((cs, cs), 1)
    rows_n = sz.blocks * cs

    def expert_chunk(q, p, chunk, fresh):
        at = pl.ds(chunk * sz.blocks, sz.blocks) if sz.chunks > 1 else slice(None)
        rows = r.rows_all[q, at].reshape(rows_n, d)
        dy = r.dy_all[q, at].reshape(rows_n, d).astype(F32)
        gates = []
        for b in range(sz.blocks):
            g = chunk * sz.blocks + b
            level = r.gate_all[q, g][0:1, 0:cs]
            gates.append(jnp.sum(jnp.where(spot, level, 0.0), axis=1, keepdims=True))
        gate = jnp.concatenate(gates, axis=0) if len(gates) > 1 else gates[0]
        pre_act = mm(rows, r.up_w[...]) + r.b_up[...]
        cdf, density = gelu_parts(pre_act)
        act_low = (pre_act * cdf).astype(BF16)
        slot_grad = (gate * dy).astype(BF16)
        pre_grad = (mm(slot_grad, r.down_w[...], NT) * (cdf + pre_act * density)).astype(BF16)
        row_grad = mm(pre_grad, r.up_w[...], NT).astype(BF16)
        r.act_t[...], r.pre_t[...], r.slot_t[...] = act_low, pre_grad, slot_grad
        r.dy_all[q, at] = row_grad.reshape(sz.blocks, cs, d)
        expert_out = mm(act_low, r.down_w[...]) + first * r.b_down[...]
        r.out_t[...] = (gate * expert_out).astype(BF16)
        dgate = jnp.sum(expert_out * dy, axis=1, keepdims=True)
        for b in range(sz.blocks):
            g = chunk * sz.blocks + b
            level = jnp.sum(
                jnp.where(spot, dgate[b * cs : (b + 1) * cs], 0.0), axis=0, keepdims=True
            )
            r.dg_send[p, g, :, 0:cs] = jnp.broadcast_to(level, (8, cs))

    def weight_chunk(q, chunk, fresh):
        at = pl.ds(chunk * sz.blocks, sz.blocks) if sz.chunks > 1 else slice(None)
        rows = r.rows_all[q, at].reshape(rows_n, d)
        up = mm(rows, r.pre_t[...], TN)
        down = mm(r.act_t[...], r.slot_t[...], TN)
        biases = jnp.concatenate(
            [
                jnp.sum(r.pre_t[...].astype(F32), axis=0, keepdims=True),
                jnp.sum(r.slot_t[...].astype(F32), axis=0, keepdims=True),
                jnp.zeros((6, d), F32),
            ]
        )
        if fresh:
            r.up_acc[...], r.down_acc[...], r.bias_acc[...] = up, down, biases
        else:
            r.up_acc[...] += up
            r.down_acc[...] += down
            r.bias_acc[...] += biases
        r.rows_all[q, at] = r.out_t[...].reshape(sz.blocks, cs, d)

    for p in range(nq):
        q = quarter[p]
        if p == 0:
            for copy in dy_forwards + row_forwards:
                copy.wait_send()
            finished += dy_forwards + row_forwards
        elif p == 3:
            for s in later:
                got(r.dy_all.at[q, source[s]], r.dyz_sem, (1, s), ea_peer[s])
                got(r.gate_all.at[q, source[s]], r.gatez_sem, (1, s), ea_peer[s])
                got(r.rows_all.at[q, source[s]], r.rowz_sem, (1, s), ea_peer[s])
        else:
            got(r.gate_all.at[q], r.gatet_sem, p, ta_peer[p])
            for s in range(ea):
                got(r.dy_all.at[q, source[s]], r.dyt_sem, (p, s), ta_peer[p])
                got(r.rows_all.at[q, source[s]], r.rowt_sem, (p, s), ta_peer[p])
        if sz.chunks == 1:
            expert_chunk(q, p, 0, p == 0)
            sends(r, sz, go, p, q, ta_peer, target)
            weight_chunk(q, 0, p == 0)
        else:
            if p == 0:
                r.up_acc[...] = jnp.zeros((d, sz.hidden), F32)
                r.down_acc[...] = jnp.zeros((sz.hidden, d), F32)
                r.bias_acc[...] = jnp.zeros((8, d), F32)

            @pl.loop(0, sz.chunks)
            def _(chunk):
                expert_chunk(q, p, chunk, False)
                weight_chunk(q, chunk, False)

            sends(r, sz, go, p, q, ta_peer, target)

    r.up_low[...] = r.up_acc[...].astype(BF16)
    r.down_low[...] = r.down_acc[...].astype(BF16)
    go(r.up_low, r.o_up.at[1], r.rep_sem, 0, other)
    go(r.down_low, r.o_down.at[1], r.rep_sem, 1, other)
    go(r.bias_acc, r.bias_in, r.rep_sem, 2, other)
    keep_up = pltpu.make_async_copy(r.up_low, r.o_up.at[0], r.load_sem.at[0])
    keep_down = pltpu.make_async_copy(r.down_low, r.o_down.at[0], r.load_sem.at[1])
    keep_up.start()
    keep_down.start()

    home_copies = []
    for p in partners:
        got(r.dg_in.at[p], r.dg_sem, p, ta_peer[p])
    for s in later + [0]:
        g = target[s]
        for p in partners:
            got(r.rg_in.at[p - 1, g], r.rg_sem, (p, s), ta_peer[p])
        share = r.dy_all[j, g].astype(F32)
        dgate = r.dg_send[0, g]
        for p in partners:
            share = share + r.rg_in[p - 1, g].astype(F32)
            dgate = dgate + r.dg_in[p, g]
        if s:
            r.rgz_send[g] = share.astype(BF16)
            r.dgz_send[g] = dgate
            go(r.dgz_send.at[g], r.dg_back.at[z], r.dgz_sem, s, ea_peer[s])
            home_copies.append(go(r.rgz_send.at[g], r.rg_back.at[z], r.rgz_sem, s, ea_peer[s]))
        else:
            r.rg_back[z] = share.astype(BF16)
            r.dg_back[z] = dgate
    for p in (1, 2):
        for s in range(ea):
            go(r.rows_all.at[quarter[p], target[s]], r.eo_in.at[p - 1, target[s]], r.eo_sem, (p, s), ta_peer[p])

    place_0, place_1 = r.place_col[:, 0:1], r.place_col[:, 1:2]
    lane = iota((qt, sz.experts * cs), 1)
    back = onehot((lane == place_0) | (lane == place_1)).astype(BF16)
    for s in later:
        got(r.dg_back.at[source[s]], r.dgz_sem, s, ea_peer[s])
        got(r.rg_back.at[source[s]], r.rgz_sem, s, ea_peer[s])

    drouter = jnp.zeros((sz.ep, qt), F32)
    for expert in range(sz.experts):
        level = mm(r.dg_back[expert][:, 0:cs], slots_of(expert, 0), NN, EXACT)
        drouter = drouter + jnp.where(iota((sz.ep, 1), 0) == expert, level[0:1], 0.0)
    router = r.probs[...]
    dlogits = (router * (drouter - jnp.sum(router * drouter, axis=0, keepdims=True))).astype(BF16)
    into_two = mm(back, r.rg_back[...].reshape(sz.experts * cs, d)) + mm(dlogits, router_w, TN)
    _, hat_two, inv_two = layer_norm(r.hidden[...], flat_row(r.gain2), flat_row(r.bias2))
    dhidden = r.dy_mine[...].astype(F32) + norm_back(into_two, hat_two, inv_two, flat_row(r.gain2))
    r.dhidden[...] = dhidden
    dattn = dhidden.astype(BF16)
    r.da_all[j] = dattn
    for p in partners:
        go(r.da_all.at[j], r.da_all.at[j], r.da_sem, p, ta_peer[p])
    router_grad = mm(dlogits, r.b_low[...])
    rows_at = iota((sz.early, 1), 0)
    early = jnp.where(rows_at < sz.experts, fit(router_grad, sz.early), 0.0)
    for offset, values in enumerate((into_two * hat_two, into_two, dattn.astype(F32))):
        total = jnp.sum(values, axis=0, keepdims=True)
        early = early + jnp.where(rows_at == sz.experts + offset, total, 0.0)

    def small_start(values, by_ta, sem):
        by_ta[j] = values
        for p in partners:
            go(by_ta.at[j], by_ta.at[j], sem, (0, p), ta_peer[p])

    def small_middle(by_ta, by_dev, sem, own_rows):
        for p in partners:
            got(by_ta.at[quarter[p]], sem, (0, p), ta_peer[p])
        total = by_ta[0]
        for q in range(1, nq):
            total = total + by_ta[q]
        if own_rows:
            total = jnp.where(iota((8, 1), 0) < 2, total, by_ta[j])
        by_dev[c] = total
        go(by_dev.at[c], by_dev.at[c], sem, (1, 0), other)

    def small_last(by_dev, by_ea, sem):
        got(by_dev.at[1 - c], sem, (1, 0), other)
        by_ea[z] = by_dev[0] + by_dev[1]
        for s in later:
            go(by_ea.at[z], by_ea.at[z], sem, (2, s), ea_peer[s])

    def small_end(by_ea, out, sem):
        for s in later:
            got(by_ea.at[source[s]], sem, (2, s), ea_peer[s])
        total = by_ea[0]
        for e in range(1, ea):
            total = total + by_ea[e]
        out[...] = total

    if sz.direct:
        small_start(early, r.early_ta, r.early_sem)
    else:
        r.o_early[...] = early

    for p in partners:
        got(r.da_all.at[quarter[p]], r.da_sem, p, ta_peer[p])
    for s in range(ea):
        go(r.rows_all.at[quarter[3], target[s]], r.eo_in.at[2, target[s]], r.eo_sem, (3, s), ta_peer[3])
    if sz.direct:
        small_middle(r.early_ta, r.early_dev, r.early_sem, False)

    unpick = onehot(iota((sz.tp, nq * qt), 1) == r.perm_col[:, 0:1].astype(jnp.int32)).astype(BF16)
    dattn = mm(unpick, r.da_all[...].reshape(nq * qt, d)).astype(BF16)
    w_out = r.w_out[...].reshape(sz.inner, d)
    dmixed = mm(dattn, w_out, NT).astype(BF16).reshape(flat)

    def piece_start(n, values):
        half = values.reshape(2, sz.half, d)
        r.pd_send[n] = half.astype(BF16)
        go(r.pd_send.at[n, 1 - c], r.pd_in.at[n], r.pd_sem, n, other)

    def piece_middle(n):
        got(r.pd_in.at[n], r.pd_sem, n, other)
        both = r.pd_send[n, c].astype(F32) + r.pd_in[n].astype(F32)
        for e in range(ea):
            r.pz_send[n, e] = both[e * sz.piece : (e + 1) * sz.piece].astype(BF16)
        for s in later:
            t = target[s]
            go(r.pz_send.at[n, t], r.pz_in.at[n, z], r.pz_sem, (n, s), ea_peer[s])
        r.pz_in[n, z] = r.pz_send[n, z]

    def piece_last(n):
        for s in later:
            got(r.pz_in.at[n, source[s]], r.pz_sem, (n, s), ea_peer[s])
        total = r.pz_in[n, 0].astype(F32)
        for e in range(1, ea):
            total = total + r.pz_in[n, e].astype(F32)
        r.p_all[n, c, z] = total.astype(BF16)
        for s in later:
            block = r.p_all.at[n, c, z]
            go(block, block, r.pa_sem, (n, s), ea_peer[s])
        go(r.p_all.at[n, c, z], r.p_all.at[n, c, z], r.pb_sem, (n, 0), other)

    def piece_pass(n):
        for s in later:
            block = r.p_all.at[n, c, source[s]]
            got(block, r.pa_sem, (n, s), ea_peer[s])
            go(block, block, r.pb_sem, (n, s), other)

    def piece_end(n):
        for s in range(ea):
            got(r.p_all.at[n, 1 - c, source[s]], r.pb_sem, (n, s), other)

    if not sz.direct:

        def piece_start(n, values):
            r.o_piece[n] = values

        piece_middle = piece_last = piece_pass = piece_end = lambda n: None

    piece_start(0, mm(r.mixed[...].reshape(sz.tp, sz.inner), dattn, TN))
    if sz.direct:
        small_last(r.early_dev, r.early_ea, r.early_sem)

    for image in range(sz.images):
        queries, keys, values, dmix = r.q[image], r.k[image], r.v[image], dmixed[image]
        dquery = jnp.zeros((sz.lp, sz.inner), F32)
        dkey, dvalue = dquery, dquery
        for head in range(sz.heads):
            mask_low, mask = head_mask(sz, head, BF16), head_mask(sz, head, F32)
            scores = mm(queries * mask_low, keys, NT) * scale
            probs = jnp.where(live, jnp.exp(scores - r.lse[image][:, head : head + 1]), 0.0)
            dprobs = mm(dmix * mask_low, values, NT)
            dvalue = dvalue + mm(probs.astype(BF16), dmix, TN) * mask
            inner = jnp.sum(probs * dprobs, axis=-1, keepdims=True)
            dscores = (probs * (dprobs - inner)).astype(BF16)
            dquery = dquery + mm(dscores, keys) * (mask * scale)
            dkey = dkey + mm(dscores, queries, TN) * (mask * scale)
        for n, values in enumerate((dquery, dkey, dvalue)):
            r.dproj[n, image] = values.astype(BF16)
    dproj = [r.dproj[n].reshape(sz.tp, sz.inner) for n in range(3)]
    into_part = mm(dproj[0], r.w_qkv[0]) + mm(dproj[1], r.w_qkv[1]) + mm(dproj[2], r.w_qkv[2])
    r.in_send[...] = mm(pick_all, into_part.astype(BF16)).astype(BF16).reshape(nq, qt, d)
    for p in partners:
        go(r.in_send.at[quarter[p]], r.in_part.at[j], r.ip_sem, p, ta_peer[p])
    r.in_part[j] = r.in_send[j]
    for n in range(3):
        piece_start(n + 1, mm(dproj[n], r.a_low[...], TN))
    _, hat_one, _ = layer_norm(r.padded[...].reshape(sz.tp, d).astype(F32), flat_row(r.gain1), flat_row(r.bias1))
    rows_at = iota((8, 1), 0)
    late = jnp.where(rows_at == 0, jnp.sum(into_part * hat_one, axis=0, keepdims=True), 0.0)
    late = late + jnp.where(rows_at == 1, jnp.sum(into_part, axis=0, keepdims=True), 0.0)
    for row, n in ((2, 0), (3, 2)):
        total = jnp.sum(dproj[n].astype(F32), axis=0, keepdims=True)
        wide = jnp.concatenate([total, jnp.zeros((1, d - sz.inner), F32)], axis=1)
        late = late + jnp.where(rows_at == row, wide, 0.0)
    if sz.direct:
        small_start(late, r.late_ta, r.late_sem)
    else:
        r.o_late[...] = late
    for n in range(4):
        piece_middle(n)
    if sz.direct:
        small_middle(r.late_ta, r.late_dev, r.late_sem, True)

    for p in partners:
        got(r.in_part.at[quarter[p]], r.ip_sem, p, ta_peer[p])
    into_one = r.in_part[0].astype(F32)
    for q in range(1, nq):
        into_one = into_one + r.in_part[q].astype(F32)
    x_mine = mm(pick_of(j), r.padded[...].reshape(sz.tp, d))
    _, hat_mine, inv_mine = layer_norm(x_mine, flat_row(r.gain1), flat_row(r.bias1))
    grad = r.dhidden[...] + norm_back(into_one, hat_mine, inv_mine, flat_row(r.gain1))
    r.ig_all[j] = grad.astype(BF16)
    for p in partners:
        go(r.ig_all.at[j], r.ig_all.at[j], r.ig_sem, p, ta_peer[p])
    if sz.direct:
        small_last(r.late_dev, r.late_ea, r.late_sem)

    for copy in home_copies:
        copy.wait_send()
    finished += home_copies
    for s in later + [0]:
        g = target[s]
        for p in partners:
            got(r.eo_in.at[p - 1, g], r.eo_sem, (p, s), ta_peer[p])
        share = r.rows_all[j, g].astype(F32)
        for p in partners:
            share = share + r.eo_in[p - 1, g].astype(F32)
        if s:
            r.rgz_send[g] = share.astype(BF16)
            go(r.rgz_send.at[g], r.eo_back.at[z], r.eoz_sem, s, ea_peer[s])
        else:
            r.eo_back[z] = share.astype(BF16)
    for n in range(4):
        piece_last(n)
    for s in later:
        got(r.eo_back.at[source[s]], r.eoz_sem, s, ea_peer[s])
    output = r.hidden[...] + mm(back, r.eo_back[...].reshape(sz.experts * cs, d))
    r.out_all[j] = output.astype(BF16)
    for p in partners:
        go(r.out_all.at[j], r.out_all.at[j], r.out_sem, p, ta_peer[p])
    got(r.o_up.at[1], r.rep_sem, 0, other)
    got(r.o_down.at[1], r.rep_sem, 1, other)
    keep_up.wait()
    keep_down.wait()
    got(r.bias_in, r.rep_sem, 2, other)
    r.o_bias[...] = r.bias_acc[...] + r.bias_in[...]
    for n in range(4):
        piece_pass(n)
    for p in partners:
        got(r.ig_all.at[quarter[p]], r.ig_sem, p, ta_peer[p])
    r.o_in[...] = mm(unpick, r.ig_all[...].reshape(nq * qt, d)).astype(BF16).reshape(r.o_in.shape)
    for p in partners:
        got(r.out_all.at[quarter[p]], r.out_sem, p, ta_peer[p])
    r.o_out[...] = mm(unpick, r.out_all[...].reshape(nq * qt, d)).astype(BF16).reshape(r.o_in.shape)
    if sz.direct:
        small_end(r.early_ea, r.o_early, r.early_sem)
        small_end(r.late_ea, r.o_late, r.late_sem)
    for n in range(4):
        piece_end(n)
    for copy in started:
        if not any(copy is done for done in finished):
            copy.wait_send()


def flat_row(ref):
    return ref[...].reshape(1, -1)


def fit(values, rows):
    have = values.shape[0]
    if have >= rows:
        return values[:rows]
    return jnp.concatenate([values, jnp.zeros((rows - have, values.shape[1]), F32)])


def sends(r, sz, go, p, q, ta_peer, target):
    if p:
        go(r.dg_send.at[p], r.dg_in.at[p], r.dg_sem, p, ta_peer[p])
        for s in list(range(1, sz.ea)) + [0]:
            go(r.dy_all.at[q, target[s]], r.rg_in.at[p - 1, target[s]], r.rg_sem, (p, s), ta_peer[p])


def run_block(sz, inputs):
    nq, ea, d, cs, qt = sz.nq, sz.ea, sz.d, sz.cs, sz.qt
    dma = pltpu.SemaphoreType.DMA
    rows = sz.blocks * cs
    outs = {
        "o_out": ((sz.images, sz.lp, d), BF16),
        "o_in": ((sz.images, sz.lp, d), BF16),
        "o_early": ((sz.early, d), F32),
        "o_late": ((8, d), F32),
        "o_up": ((2, d, sz.hidden), BF16),
        "o_down": ((2, sz.hidden, d), BF16),
        "o_bias": ((8, d), F32),
    }
    flat = (sz.images, sz.lp, sz.inner)
    block = (cs, d)
    buffers = {
        "up_w": ((d, sz.hidden), BF16),
        "down_w": ((sz.hidden, d), BF16),
        "w_full": ((nq, 2, sz.half, d), BF16),
        "padded": ((sz.images, sz.lp, d), BF16),
        "perm_col": ((sz.tp, 128), F32),
        "place_row": ((4, qt), jnp.int32),
        "place_col": ((qt, 128), jnp.int32),
        "a_low": ((sz.tp, d), BF16),
        "q": (flat, BF16),
        "k": (flat, BF16),
        "v": (flat, BF16),
        "mixed": (flat, BF16),
        "lse": ((sz.images, sz.lp, 128), F32),
        "dproj": ((3,) + flat, BF16),
        "mix_send": ((nq, qt, sz.inner), BF16),
        "mix_in": ((2, nq, qt, sz.inner), BF16),
        "dy_mine": ((qt, d), BF16),
        "hidden": ((qt, d), F32),
        "dhidden": ((qt, d), F32),
        "b_low": ((qt, d), BF16),
        "probs": ((sz.ep, qt), F32),
        "dy_send": ((2, ea) + block, BF16),
        "gate_send": ((2, ea, 8, 128), F32),
        "dy_all": ((nq, ea) + block, BF16),
        "rows_all": ((nq, ea) + block, BF16),
        "gate_all": ((nq, ea, 8, 128), F32),
        "act_t": ((rows, sz.hidden), BF16),
        "pre_t": ((rows, sz.hidden), BF16),
        "slot_t": ((rows, d), BF16),
        "out_t": ((rows, d), BF16),
        "dg_send": ((nq, ea, 8, 128), F32),
        "dg_in": ((nq, ea, 8, 128), F32),
        "rg_in": ((nq - 1, ea) + block, BF16),
        "eo_in": ((nq - 1, ea) + block, BF16),
        "rgz_send": ((ea,) + block, BF16),
        "dgz_send": ((ea, 8, 128), F32),
        "rg_back": ((ea,) + block, BF16),
        "eo_back": ((ea,) + block, BF16),
        "dg_back": ((ea, 8, 128), F32),
        "up_acc": ((d, sz.hidden), F32),
        "down_acc": ((sz.hidden, d), F32),
        "bias_acc": ((8, d), F32),
        "up_low": ((d, sz.hidden), BF16),
        "down_low": ((sz.hidden, d), BF16),
        "bias_in": ((8, d), F32),
        "da_all": ((nq, qt, d), BF16),
        "ig_all": ((nq, qt, d), BF16),
        "out_all": ((nq, qt, d), BF16),
        "in_send": ((nq, qt, d), BF16),
        "in_part": ((nq, qt, d), BF16),
    }
    sems = {
        "w_sem": (nq,),
        "wd_sem": (nq,),
        "dyz_sem": (2, ea),
        "dyt_sem": (nq, ea),
        "mix_sem": (2, nq),
        "gatez_sem": (2, ea),
        "rowz_sem": (2, ea),
        "rowt_sem": (nq, ea),
        "gatet_sem": (nq,),
        "dg_sem": (nq,),
        "rg_sem": (nq, ea),
        "rep_sem": (3,),
        "dgz_sem": (ea,),
        "rgz_sem": (ea,),
        "eo_sem": (nq, ea),
        "eoz_sem": (ea,),
        "da_sem": (nq,),
        "early_sem": (3, max(nq, ea)),
        "late_sem": (3, max(nq, ea)),
        "pd_sem": (4,),
        "pz_sem": (4, ea),
        "pa_sem": (4, ea),
        "pb_sem": (4, ea),
        "ip_sem": (nq,),
        "ig_sem": (nq,),
        "out_sem": (nq,),
    }
    if sz.direct:
        outs["p_all"] = ((4, 2, ea, sz.piece, d), BF16)
        buffers |= {
            "early_ta": ((nq, sz.early, d), F32),
            "early_dev": ((2, sz.early, d), F32),
            "early_ea": ((ea, sz.early, d), F32),
            "late_ta": ((nq, 8, d), F32),
            "late_dev": ((2, 8, d), F32),
            "late_ea": ((ea, 8, d), F32),
            "pd_send": ((4, 2, sz.half, d), BF16),
            "pd_in": ((4, sz.half, d), BF16),
            "pz_send": ((4, ea, sz.piece, d), BF16),
            "pz_in": ((4, ea, sz.piece, d), BF16),
        }
    else:
        outs["o_piece"] = ((4, sz.inner, d), F32)
    if sz.direct:
        buffers["row_send"] = ((2, ea) + block, BF16)
    names = list(inputs) + list(outs) + list(buffers) + list(sems) + ["load_sem"]
    vm = pl.BlockSpec(memory_space=pltpu.VMEM)
    far = pl.BlockSpec(memory_space=pl.ANY)
    results = pl.pallas_call(
        functools.partial(block_kernel, sz, names),
        out_shape=[jax.ShapeDtypeStruct(*spec) for spec in outs.values()],
        in_specs=[far if name in ("w_up", "w_down") else vm for name in inputs],
        out_specs=[far if name in ("o_up", "o_down") else vm for name in outs],
        scratch_shapes=[pltpu.VMEM(*spec) for spec in buffers.values()]
        + [dma((2,) + shape) for shape in sems.values()]
        + [dma((2,))],
        name="block",
        compiler_params=pltpu.CompilerParams(
            collective_id=0, has_side_effects=True, vmem_limit_bytes=60 << 20
        ),
    )(*inputs.values())
    return dict(zip(outs, results))


def local(
    tokens,
    expert_ids,
    pair_ranks,
    cotangent,
    w_qkv,
    b_qv,
    w_out,
    b_out,
    ln1_gain,
    ln1_bias,
    ln2_gain,
    ln2_bias,
    w_router,
    w_up,
    b_up,
    w_down,
    b_down,
):
    sz = Sizes(tokens, expert_ids, w_qkv, w_up)
    pairs = jnp.stack([jnp.transpose(t, (2, 0, 1)) for t in (expert_ids, pair_ranks)])
    pairs = jnp.pad(
        pairs, ((0, 0), (0, 0), (0, 0), (0, sz.lp - sz.length)), constant_values=sz.tokens * 2
    )
    table = jnp.pad(pairs.reshape(4, sz.tp).astype(F32), ((0, 4), (0, ceil_to(sz.tp, 128) - sz.tp)))
    inputs = {
        "tok": tokens,
        "cot": cotangent,
        "w_qkv": jnp.swapaxes(w_qkv, 1, 2),
        "b_qv": b_qv,
        "w_out": w_out.reshape(2, sz.half, sz.d),
        "b_out": b_out,
        "gain1": ln1_gain,
        "bias1": ln1_bias,
        "gain2": ln2_gain,
        "bias2": ln2_bias,
        "router": w_router.T,
        "w_up": w_up[0],
        "b_up": b_up,
        "w_down": w_down[0],
        "b_down": b_down,
        "table": table,
    }
    got = run_block(sz, inputs)
    n = sz.experts
    early, late = got["o_early"], got["o_late"]
    if sz.direct:
        piece = got["p_all"].reshape(4, sz.inner, sz.d).astype(F32)
    else:
        piece, shared = lax.psum((got["o_piece"], late[2:4]), ("ea", "dev"))
        early, late = lax.psum((early, late), ("ea", "ta", "dev"))
        late = jnp.concatenate([late[:2], shared, late[4:]])
    return (
        got["o_out"][:, : sz.length],
        got["o_in"][:, : sz.length].astype(F32),
        jnp.swapaxes(piece[1:], 1, 2),
        late[2:4, : sz.inner],
        piece[0],
        early[n + 2],
        late[0],
        late[1],
        early[n],
        early[n + 1],
        early[:n].T,
        (got["o_up"][0].astype(F32) + got["o_up"][1].astype(F32))[None],
        got["o_bias"][0:1],
        (got["o_down"][0].astype(F32) + got["o_down"][1].astype(F32))[None],
        got["o_bias"][1:2],
    )


def solution(mesh):
    in_specs = (
        P(("ea", "dev"), None, None),
        P(("ea", "dev"), None, None),
        P(("ea", "dev"), None, None),
        P(("ea", "dev"), None, None),
        P(None, None, "ta"),
        P(None, "ta"),
        P("ta", None),
        P(),
        P(),
        P(),
        P(),
        P(),
        P(),
        P("ea", None, "ta"),
        P("ea", "ta"),
        P("ea", "ta", None),
        P("ea", None),
    )
    out_specs = (
        P(("ea", "dev"), None, None),
        P(("ea", "dev"), None, None),
        P(None, None, "ta"),
        P(None, "ta"),
        P("ta", None),
        P(),
        P(),
        P(),
        P(),
        P(),
        P(),
        P("ea", None, "ta"),
        P("ea", "ta"),
        P("ea", "ta", None),
        P("ea", None),
    )
    return jax.shard_map(local, mesh=mesh, in_specs=in_specs, out_specs=out_specs, check_vma=False)
```

```python
import functools
import types

import jax
import jax.numpy as jnp
from jax import lax
from jax.experimental import pallas as pl
from jax.experimental.pallas import tpu as pltpu
from jax.sharding import PartitionSpec as P

HDIM = 64
EPSILON = 1e-06
F32, BF16 = jnp.float32, jnp.bfloat16
EXACT = lax.Precision.HIGHEST
MESH = pl.DeviceIdType.MESH
NT = (((1,), (1,)), ((), ()))
TN = (((0,), (0,)), ((), ()))
NN = (((1,), (0,)), ((), ()))


def ceil_to(value, unit):
    return -(-value // unit) * unit


def mm(a, b, dims=NN, precision=None):
    return lax.dot_general(a, b, dims, precision=precision, preferred_element_type=F32)


def iota(shape, dim):
    return lax.broadcasted_iota(jnp.int32, shape, dim)


def onehot(mask):
    return jnp.where(mask, 1.0, 0.0).astype(F32)


class Sizes:
    def __init__(self, tokens, expert_ids, w_qkv, w_up):
        self.images, self.length, self.d = tokens.shape
        self.top = expert_ids.shape[2]
        self.tokens = self.images * self.length
        self.ea = lax.axis_size("ea")
        self.nq = lax.axis_size("ta")
        assert w_up.shape[0] == 1
        self.experts = self.ea
        self.cap = (9 * self.tokens * self.top + 8 * self.experts - 1) // (8 * self.experts)
        self.inner = w_qkv.shape[2]
        self.heads = self.inner // HDIM
        self.hidden = w_up.shape[2]
        self.lp = ceil_to(self.length, 16)
        self.tp = self.images * self.lp
        per_quarter = -(-self.tokens // self.nq)
        self.qt = ceil_to(per_quarter, 16)
        spread = (self.cap + (self.nq - 1) * self.experts) // self.nq
        self.cs = ceil_to(min(self.cap, per_quarter, spread), 16)
        self.ep = ceil_to(self.experts, 16)
        self.half = self.inner // 2
        self.piece = self.half // self.ea
        self.early = ceil_to(self.experts + 3, 8)
        self.blocks = max(1, min(self.ea, (256 if self.ea <= 8 else 64) // self.cs))
        self.chunks = self.ea // self.blocks
        self.direct = self.ea <= 8
        self.relay = [s for s in range(1, self.ea) if self.direct and s >= 2]
        self.kept = self.nq if self.chunks == 1 else 1
        assert self.top == 2 and self.nq == 4


def route(sz, table):
    rows = [table[n : n + 1, : sz.tp] for n in range(4)]
    cols = table.T[: sz.tp]
    wide = iota((sz.tp, 128), 1)

    def count(mask):
        return jnp.sum(jnp.where(mask, 1.0, 0.0), axis=1, keepdims=True)

    def flip(*columns):
        spread = jnp.zeros((sz.tp, 128), F32)
        for n, column in enumerate(columns):
            spread = spread + jnp.where(wide == n, column, 0.0)
        turned = spread.T
        return [turned[n : n + 1] for n in range(len(columns))]

    real = cols[:, 0:1] < sz.experts
    dest = []
    for k in range(2):
        ids, ranks = cols[:, k : k + 1], cols[:, 2 + k : 3 + k]
        position = sum(count((rows[m] == ids) & (rows[2 + m] < ranks)) for m in range(2))
        dest.append(jnp.where((position < sz.cap) & real, ids, float(sz.experts)))
    low, high = jnp.minimum(*dest), jnp.maximum(*dest)
    index = iota((sz.tp, 1), 0).astype(F32)
    kind = jnp.where(real, low * (sz.experts + 1) + high, float((sz.experts + 1) ** 2))
    key = kind * sz.tp + index
    (key_row,) = flip(key)
    order = count(key_row < key)
    lap = jnp.floor((order + 0.5) * (1.0 / sz.nq))
    quarter = order - lap * sz.nq
    group = [d * sz.nq + quarter for d in dest]
    perm = jnp.where(real, quarter * sz.qt + lap, -1.0)
    order_row, perm_row, *group_row = flip(order, perm, *group)
    place = []
    for k in range(2):
        slot = sum(count((group_row[m] == group[k]) & (order_row < order)) for m in range(2))
        place.append(jnp.where(dest[k] < sz.experts, dest[k] * sz.cs + slot + 1.0, 0.0))
    place_row = flip(*place)
    return perm, perm_row, place, place_row


def layer_norm(values, gain_vec, shift_vec):
    row_mean = jnp.mean(values, axis=-1, keepdims=True)
    centered = values - row_mean
    variance = jnp.mean(centered * centered, axis=-1, keepdims=True)
    inverse = lax.rsqrt(variance + EPSILON)
    normed = centered * inverse
    return (normed * gain_vec + shift_vec, normed, inverse)


def norm_back(grad_rows, normed, inverse, gain_vec):
    scaled = grad_rows * gain_vec
    return inverse * (
        scaled
        - jnp.mean(scaled, axis=-1, keepdims=True)
        - normed * jnp.mean(scaled * normed, axis=-1, keepdims=True)
    )


def push(src, dst, send_sem, recv_sem, device):
    return pltpu.make_async_remote_copy(
        src_ref=src,
        dst_ref=dst,
        send_sem=send_sem,
        recv_sem=recv_sem,
        device_id=device,
        device_id_type=MESH,
    )


def greet(devices):
    barrier = pltpu.get_barrier_semaphore()
    for device in devices:
        pl.semaphore_signal(barrier, inc=1, device_id=device, device_id_type=MESH)


def head_mask(sz, head, dtype):
    lane = iota((1, sz.inner), 1)
    return onehot((lane >= head * HDIM) & (lane < (head + 1) * HDIM)).astype(dtype)


def gelu_parts(values):
    cdf = 0.5 * (1.0 + lax.erf(values * (0.5**0.5)))
    density = jnp.exp(-0.5 * values * values) * (0.5 / jnp.pi) ** 0.5
    return cdf, density


def block_kernel(sz, names, *refs):
    r = types.SimpleNamespace(**dict(zip(names, refs)))
    z, j, c = lax.axis_index("ea"), lax.axis_index("ta"), lax.axis_index("dev")
    nq, ea, d, cs, qt = sz.nq, sz.ea, sz.d, sz.cs, sz.qt
    quarter = [j, j + 1 - 2 * lax.rem(j, 2), j + 2 - 4 * lax.div(j, 2), 3 - j]
    ta_peer = [{"ta": q} for q in quarter]
    ea_peer = [{"ea": lax.rem(z + s, ea)} for s in range(ea)]
    source = [lax.rem(z - s + ea, ea) for s in range(ea)]
    target = [lax.rem(z + s, ea) for s in range(ea)]
    other = {"dev": 1 - c}
    later = [s for s in range(1, ea)]
    partners = (1, 2, 3)
    started = []

    def go(src, dst, sem, index, device):
        index = index if isinstance(index, tuple) else (index,)
        copy = push(src, dst, sem.at[(0,) + index], sem.at[(1,) + index], device)
        copy.start()
        started.append(copy)
        return copy

    def got(dst, sem, index, device):
        index = index if isinstance(index, tuple) else (index,)
        push(dst, dst, sem.at[(1,) + index], sem.at[(1,) + index], device).wait_recv()

    everyone = ta_peer[1:] + ea_peer[1:] + [other]
    greet(everyone)
    loads = []
    for n, (src, dst) in enumerate(
        ((r.cot, r.cot_v), (r.tok, r.tok_v), (r.w_qkv, r.qkv_w), (r.w_up, r.up_w), (r.w_down, r.down_w))
    ):
        loads.append(pltpu.make_async_copy(src, dst, r.load_sem.at[n]))
        loads[-1].start()
    perm_col, perm, place, place_rows = route(sz, r.table[...])
    pl.semaphore_wait(pltpu.get_barrier_semaphore(), len(everyone))

    for p in partners:
        go(r.w_out.at[c], r.w_full.at[j, c], r.w_sem, p, ta_peer[p])
    r.w_full[j] = r.w_out[...]

    perm = perm.astype(jnp.int32)
    r.perm_col[...] = jnp.broadcast_to(perm_col, (sz.tp, 128))
    pick_all = onehot(iota((nq * qt, sz.tp), 0) == perm).astype(BF16)

    def pick_of(q):
        return onehot(iota((qt, sz.tp), 0) + q * qt == perm).astype(BF16)

    spread = iota((8, 1), 0)
    both = jnp.where(spread == 0, place_rows[0], 0.0) + jnp.where(spread == 1, place_rows[1], 0.0)
    for which, q in ((0, quarter[0]), (1, quarter[3])):
        chosen = mm(both, onehot(iota((qt, sz.tp), 0) + q * qt == perm), NT, EXACT)
        r.place_row[2 * which : 2 * which + 2] = (chosen[0:2] + 0.5).astype(jnp.int32) - 1
    pair_col = jnp.where(iota((1, 128), 1) == 0, place[0], 0.0)
    pair_col = pair_col + jnp.where(iota((1, 128), 1) == 1, place[1], 0.0)
    chosen = mm(onehot(iota((qt, sz.tp), 0) + j * qt == perm), pair_col, NN, EXACT)
    r.place_col[...] = (chosen + 0.5).astype(jnp.int32) - 1

    def slots_of(expert, which):
        row = iota((cs, qt), 0) + expert * cs
        first, second = r.place_row[2 * which : 2 * which + 1], r.place_row[2 * which + 1 : 2 * which + 2]
        return onehot((row == first) | (row == second))

    tail = (sz.length // 16) * 16
    loads[0].wait()
    for image in range(sz.images):
        r.padded[image, tail:] = jnp.zeros((sz.lp - tail, d), BF16)
        r.padded[image, 0 : sz.length] = r.cot_v[image]
    for which, q in ((0, quarter[0]), (1, quarter[3])):
        dy_rows = mm(pick_of(q), r.padded[...].reshape(sz.tp, d)).astype(BF16)
        if which == 0:
            r.dy_mine[...] = dy_rows
        for expert in range(sz.experts):
            r.dy_send[which, expert] = mm(slots_of(expert, which).astype(BF16), dy_rows).astype(BF16)
    dy_copies = []
    for which, q in ((0, quarter[0]), (1, quarter[3])):
        for s in later:
            copy = go(r.dy_send.at[which, target[s]], r.dy_all.at[q, z], r.dyz_sem, (which, s), ea_peer[s])
            dy_copies.append(copy)
        r.dy_all[q, z] = r.dy_send[which, z]

    def forward(ref, z_sem, t_sem):
        copies = []
        for s in [0] + later[1:] + later[:1]:
            block = ref.at[j, source[s]]
            if s:
                got(block, z_sem, (0, s), ea_peer[s])
            for p in (1, 2):
                copies.append(go(block, block, t_sem, (p, s), ta_peer[p]))
        return copies

    loads[1].wait()
    loads[2].wait()
    for image in range(sz.images):
        r.padded[image, 0 : sz.length] = r.tok_v[image]
    normed_one, _, _ = layer_norm(
        r.padded[...].reshape(sz.tp, d).astype(F32), flat_row(r.gain1), flat_row(r.bias1)
    )
    a_low = normed_one.astype(BF16)
    r.a_low[...] = a_low
    flat = (sz.images, sz.lp, sz.inner)
    r.q[...] = (mm(a_low, r.qkv_w[0], NT) + r.b_qv[0:1]).astype(BF16).reshape(flat)
    r.k[...] = mm(a_low, r.qkv_w[1], NT).astype(BF16).reshape(flat)
    r.v[...] = (mm(a_low, r.qkv_w[2], NT) + r.b_qv[1:2]).astype(BF16).reshape(flat)

    for p in partners:
        block = r.w_full.at[quarter[p], c]
        got(block, r.w_sem, p, ta_peer[p])
        go(block, block, r.wd_sem, p, other)

    scale = HDIM ** (-0.5)
    live = iota((1, sz.lp), 1) < sz.length
    for image in range(sz.images):
        queries, keys, values = r.q[image], r.k[image], r.v[image]
        mixed = jnp.zeros((sz.lp, sz.inner), F32)
        logs = jnp.zeros((sz.lp, 128), F32)
        for head in range(sz.heads):
            scores = mm(queries * head_mask(sz, head, BF16), keys, NT) * scale
            scores = jnp.where(live, scores, -1e30)
            peak = jnp.max(scores, axis=-1, keepdims=True)
            exps = jnp.exp(scores - peak)
            total = jnp.sum(exps, axis=-1, keepdims=True)
            probs_low = (exps / total).astype(BF16)
            mixed = mixed + mm(probs_low, values) * head_mask(sz, head, F32)
            logs = logs + jnp.where(iota((1, 128), 1) == head, peak + jnp.log(total), 0.0)
        r.mixed[image] = mixed.astype(BF16)
        r.lse[image] = logs
    dealt = mm(pick_all, r.mixed[...].reshape(sz.tp, sz.inner)).astype(BF16)
    r.mix_send[...] = dealt.reshape(nq, qt, sz.inner)
    for p in partners:
        go(r.mix_send.at[quarter[p]], r.mix_in.at[0, j], r.mix_sem, (0, p), ta_peer[p])
        go(r.mix_send.at[quarter[3 - p]], r.mix_in.at[1, j], r.mix_sem, (1, p), ta_peer[p])
    r.mix_in[0, j] = r.mix_send[j]
    r.mix_in[1, j] = r.mix_send[quarter[3]]
    x_rows = [mm(pick_of(q), r.padded[...].reshape(sz.tp, d)) for q in (quarter[0], quarter[3])]
    for p in partners:
        got(r.w_full.at[quarter[p], 1 - c], r.wd_sem, p, other)
    for p in partners:
        got(r.mix_in.at[0, quarter[p]], r.mix_sem, (0, p), ta_peer[p])
        got(r.mix_in.at[1, quarter[p]], r.mix_sem, (1, p), ta_peer[p])

    dy_forwards = forward(r.dy_all, r.dyz_sem, r.dyt_sem)

    finished = []
    if not sz.direct:
        r.row_send = r.dy_send
        for copy in dy_copies:
            copy.wait_send()
        finished += dy_copies
    router_w = r.router[...]
    if sz.ep > sz.experts:
        router_w = jnp.concatenate([router_w, jnp.zeros((sz.ep - sz.experts, d), BF16)])
    for which in (0, 1):
        attention = flat_row(r.b_out)
        for q in range(nq):
            attention = attention + mm(r.mix_in[which, q], r.w_full[q].reshape(sz.inner, d))
        hidden = x_rows[which] + attention
        normed_two, _, _ = layer_norm(hidden, flat_row(r.gain2), flat_row(r.bias2))
        b_low = normed_two.astype(BF16)
        logits = mm(router_w, b_low, NT)
        logits = jnp.where(iota((sz.ep, 1), 0) < sz.experts, logits, -1e30)
        exps = jnp.exp(logits - jnp.max(logits, axis=0, keepdims=True))
        router = exps / jnp.sum(exps, axis=0, keepdims=True)
        if which == 0:
            r.hidden[...], r.b_low[...], r.probs[...] = hidden, b_low, router
        for expert in range(sz.experts):
            slots = slots_of(expert, which)
            r.row_send[which, expert] = mm(slots.astype(BF16), b_low).astype(BF16)
            level = jnp.broadcast_to(router[expert : expert + 1], (8, qt))
            r.gate_send[which, expert, :, 0:cs] = mm(level, slots, NT, EXACT)
        q = quarter[3 * which]
        for s in later:
            t = target[s]
            go(r.gate_send.at[which, t], r.gate_all.at[q, z], r.gatez_sem, (which, s), ea_peer[s])
        for s in later[1:] + later[:1]:
            t = target[s]
            if which and s in sz.relay:
                continue
            go(r.row_send.at[which, t], r.rows_all.at[q, z], r.rowz_sem, (which, s), ea_peer[s])
        r.rows_all[q, z] = r.row_send[which, z]
        r.gate_all[q, z] = r.gate_send[which, z]
    row_forwards = forward(r.rows_all, r.rowz_sem, r.rowt_sem)
    for s in later:
        got(r.gate_all.at[j, source[s]], r.gatez_sem, (0, s), ea_peer[s])
    for p in (1, 2):
        go(r.gate_all.at[j], r.gate_all.at[j], r.gatet_sem, p, ta_peer[p])

    relays = []
    low_half, high_half = pl.ds(0, cs // 2), pl.ds(cs // 2, cs // 2)
    for s in sz.relay:
        for p, part in ((1, high_half), (2, low_half)):
            got(r.rows_all.at[quarter[p], source[s]], r.rowt_sem, (p, s), ta_peer[p])
            half = r.rows_all.at[quarter[p], source[s], part]
            relays.append(go(half, half, r.rowr_sem, (3 - p, s), ta_peer[3 - p]))

    loads[3].wait()
    loads[4].wait()
    first = jnp.where(j == 0, 1.0, 0.0)
    spot = iota((cs, cs), 0) == iota((cs, cs), 1)
    rows_n = sz.blocks * cs

    def expert_chunk(q, p, chunk):
        at = pl.ds(chunk * sz.blocks, sz.blocks) if sz.chunks > 1 else slice(None)
        keep = p if sz.kept > 1 else 0
        rows = r.rows_all[q, at].reshape(rows_n, d)
        dy = r.dy_all[q, at].reshape(rows_n, d).astype(F32)
        gates = []
        for b in range(sz.blocks):
            g = chunk * sz.blocks + b
            level = r.gate_all[q, g][0:1, 0:cs]
            gates.append(jnp.sum(jnp.where(spot, level, 0.0), axis=1, keepdims=True))
        gate = jnp.concatenate(gates, axis=0) if len(gates) > 1 else gates[0]
        pre_act = mm(rows, r.up_w[...]) + r.b_up[...]
        cdf, density = gelu_parts(pre_act)
        act_low = (pre_act * cdf).astype(BF16)
        slot_grad = (gate * dy).astype(BF16)
        pre_grad = (mm(slot_grad, r.down_w[...], NT) * (cdf + pre_act * density)).astype(BF16)
        row_grad = mm(pre_grad, r.up_w[...], NT).astype(BF16)
        r.act_t[keep], r.pre_t[keep], r.slot_t[keep] = act_low, pre_grad, slot_grad
        r.dy_all[q, at] = row_grad.reshape(sz.blocks, cs, d)
        expert_out = mm(act_low, r.down_w[...]) + first * r.b_down[...]
        r.out_t[keep] = (gate * expert_out).astype(BF16)
        dgate = jnp.sum(expert_out * dy, axis=1, keepdims=True)
        for b in range(sz.blocks):
            g = chunk * sz.blocks + b
            level = jnp.sum(
                jnp.where(spot, dgate[b * cs : (b + 1) * cs], 0.0), axis=0, keepdims=True
            )
            r.dg_send[p, g, :, 0:cs] = jnp.broadcast_to(level, (8, cs))

    def weight_chunk(q, p, chunk, fresh):
        at = pl.ds(chunk * sz.blocks, sz.blocks) if sz.chunks > 1 else slice(None)
        keep = p if sz.kept > 1 else 0
        rows = r.rows_all[q, at].reshape(rows_n, d)
        up = mm(rows, r.pre_t[keep], TN)
        down = mm(r.act_t[keep], r.slot_t[keep], TN)
        biases = jnp.concatenate(
            [
                jnp.sum(r.pre_t[keep].astype(F32), axis=0, keepdims=True),
                jnp.sum(r.slot_t[keep].astype(F32), axis=0, keepdims=True),
                jnp.zeros((6, d), F32),
            ]
        )
        if fresh:
            r.up_acc[...], r.down_acc[...], r.bias_acc[...] = up, down, biases
        else:
            r.up_acc[...] += up
            r.down_acc[...] += down
            r.bias_acc[...] += biases
        r.rows_all[q, at] = r.out_t[keep].reshape(sz.blocks, cs, d)

    parts = (None, (low_half, high_half), (high_half, low_half))
    blocks = later + [0]

    def share_diagonal(ref, relay_in, sem):
        for s in blocks:
            for n, p, part in ((0, 2, low_half), (1, 1, high_half)):
                half = ref.at[quarter[3], target[s], part]
                go(half, relay_in.at[n, target[s]], sem, (n, s), ta_peer[p])

    def share_straight(ref, taken, sem, p):
        for s in blocks:
            half = parts[p][1]
            src = ref.at[quarter[p], target[s], half]
            go(src, taken.at[p - 1, target[s], half], sem, (1 + p, s), ta_peer[p])

    def share_joined(ref, taken, relay_in, sem, p):
        for s in blocks:
            half = parts[p][0]
            g = target[s]
            got(relay_in.at[p - 1, g], sem, (p - 1, s), ta_peer[3 - p])
            joined = ref[quarter[p], g, half].astype(F32) + relay_in[p - 1, g].astype(F32)
            ref[quarter[p], g, half] = joined.astype(BF16)
            src = ref.at[quarter[p], g, half]
            go(src, taken.at[p - 1, g, half], sem, (3 + p, s), ta_peer[p])

    def share_sum(ref, taken, sem, s):
        g = target[s]
        total = ref[j, g].astype(F32)
        for p in (1, 2):
            got(taken.at[p - 1, g, parts[p][1]], sem, (1 + p, s), ta_peer[p])
            got(taken.at[p - 1, g, parts[p][0]], sem, (3 + p, s), ta_peer[p])
            total = total + taken[p - 1, g].astype(F32)
        return total

    for p in (0, 3, 1, 2):
        q = quarter[p]
        if p == 0:
            for copy in dy_forwards + row_forwards:
                copy.wait_send()
            finished += dy_forwards + row_forwards
        elif p == 3:
            for s in later:
                got(r.dy_all.at[q, source[s]], r.dyz_sem, (1, s), ea_peer[s])
                got(r.gate_all.at[q, source[s]], r.gatez_sem, (1, s), ea_peer[s])
                if s in sz.relay:
                    got(r.rows_all.at[q, source[s], low_half], r.rowr_sem, (1, s), ta_peer[1])
                    got(r.rows_all.at[q, source[s], high_half], r.rowr_sem, (2, s), ta_peer[2])
                else:
                    got(r.rows_all.at[q, source[s]], r.rowz_sem, (1, s), ea_peer[s])
        else:
            got(r.gate_all.at[q], r.gatet_sem, p, ta_peer[p])
            for s in range(ea):
                got(r.dy_all.at[q, source[s]], r.dyt_sem, (p, s), ta_peer[p])
                if s not in sz.relay:
                    got(r.rows_all.at[q, source[s]], r.rowt_sem, (p, s), ta_peer[p])
            if p == 1:
                for copy in relays:
                    copy.wait_send()
                finished += relays
        if sz.chunks == 1:
            expert_chunk(q, p, 0)
            if p == 0:
                weight_chunk(q, p, 0, True)
        else:
            if p == 0:
                r.up_acc[...] = jnp.zeros((d, sz.hidden), F32)
                r.down_acc[...] = jnp.zeros((sz.hidden, d), F32)
                r.bias_acc[...] = jnp.zeros((8, d), F32)

            @pl.loop(0, sz.chunks)
            def _(chunk):
                expert_chunk(q, p, chunk)
                weight_chunk(q, p, chunk, False)

        if p:
            go(r.dg_send.at[p], r.dg_in.at[p], r.dg_sem, p, ta_peer[p])
        if p == 3:
            share_diagonal(r.dy_all, r.rg_relay, r.rg_sem)
        elif p:
            share_straight(r.dy_all, r.rg_in, r.rg_sem, p)
            share_joined(r.dy_all, r.rg_in, r.rg_relay, r.rg_sem, p)
    if sz.chunks == 1:
        for p in (3, 1, 2):
            weight_chunk(quarter[p], p, 0, False)

    r.up_low[...] = r.up_acc[...].astype(BF16)
    r.down_low[...] = r.down_acc[...].astype(BF16)
    go(r.up_low, r.up_in, r.rep_sem, 0, other)
    go(r.down_low, r.down_in, r.rep_sem, 1, other)
    go(r.bias_acc, r.bias_in, r.rep_sem, 2, other)

    home_copies = []
    for p in partners:
        got(r.dg_in.at[p], r.dg_sem, p, ta_peer[p])
    for s in later + [0]:
        g = target[s]
        share = share_sum(r.dy_all, r.rg_in, r.rg_sem, s)
        dgate = r.dg_send[0, g]
        for p in partners:
            dgate = dgate + r.dg_in[p, g]
        if s:
            r.rgz_send[g] = share.astype(BF16)
            r.dgz_send[g] = dgate
            go(r.dgz_send.at[g], r.dg_back.at[z], r.dgz_sem, s, ea_peer[s])
            home_copies.append(go(r.rgz_send.at[g], r.rg_back.at[z], r.rgz_sem, s, ea_peer[s]))
        else:
            r.rg_back[z] = share.astype(BF16)
            r.dg_back[z] = dgate
    share_diagonal(r.rows_all, r.eo_relay, r.eo_sem)
    for p in (1, 2):
        share_straight(r.rows_all, r.eo_in, r.eo_sem, p)

    place_0, place_1 = r.place_col[:, 0:1], r.place_col[:, 1:2]
    lane = iota((qt, sz.experts * cs), 1)
    back = onehot((lane == place_0) | (lane == place_1)).astype(BF16)
    for s in later:
        got(r.dg_back.at[source[s]], r.dgz_sem, s, ea_peer[s])
        got(r.rg_back.at[source[s]], r.rgz_sem, s, ea_peer[s])

    drouter = jnp.zeros((sz.ep, qt), F32)
    for expert in range(sz.experts):
        level = mm(r.dg_back[expert][:, 0:cs], slots_of(expert, 0), NN, EXACT)
        drouter = drouter + jnp.where(iota((sz.ep, 1), 0) == expert, level[0:1], 0.0)
    router = r.probs[...]
    dlogits = (router * (drouter - jnp.sum(router * drouter, axis=0, keepdims=True))).astype(BF16)
    into_two = mm(back, r.rg_back[...].reshape(sz.experts * cs, d)) + mm(dlogits, router_w, TN)
    _, hat_two, inv_two = layer_norm(r.hidden[...], flat_row(r.gain2), flat_row(r.bias2))
    dhidden = r.dy_mine[...].astype(F32) + norm_back(into_two, hat_two, inv_two, flat_row(r.gain2))
    r.dhidden[...] = dhidden
    dattn = dhidden.astype(BF16)
    r.da_all[j] = dattn
    for p in partners:
        go(r.da_all.at[j], r.da_all.at[j], r.da_sem, p, ta_peer[p])
    router_grad = mm(dlogits, r.b_low[...])
    rows_at = iota((sz.early, 1), 0)
    early = jnp.where(rows_at < sz.experts, fit(router_grad, sz.early), 0.0)
    for offset, values in enumerate((into_two * hat_two, into_two, dattn.astype(F32))):
        total = jnp.sum(values, axis=0, keepdims=True)
        early = early + jnp.where(rows_at == sz.experts + offset, total, 0.0)

    def small_start(values, by_ta, sem):
        by_ta[j] = values
        for p in partners:
            go(by_ta.at[j], by_ta.at[j], sem, (0, p), ta_peer[p])

    def small_middle(by_ta, by_dev, sem, own_rows):
        for p in partners:
            got(by_ta.at[quarter[p]], sem, (0, p), ta_peer[p])
        total = by_ta[0]
        for q in range(1, nq):
            total = total + by_ta[q]
        if own_rows:
            total = jnp.where(iota((8, 1), 0) < 2, total, by_ta[j])
        by_dev[c] = total
        go(by_dev.at[c], by_dev.at[c], sem, (1, 0), other)

    def small_last(by_dev, by_ea, sem):
        got(by_dev.at[1 - c], sem, (1, 0), other)
        by_ea[z] = by_dev[0] + by_dev[1]
        for s in later:
            go(by_ea.at[z], by_ea.at[z], sem, (2, s), ea_peer[s])

    def small_end(by_ea, out, sem):
        for s in later:
            got(by_ea.at[source[s]], sem, (2, s), ea_peer[s])
        total = by_ea[0]
        for e in range(1, ea):
            total = total + by_ea[e]
        out[...] = total

    if sz.direct:
        small_start(early, r.early_ta, r.early_sem)
    else:
        r.o_early[...] = early

    for p in partners:
        got(r.da_all.at[quarter[p]], r.da_sem, p, ta_peer[p])
    for p in (1, 2):
        share_joined(r.rows_all, r.eo_in, r.eo_relay, r.eo_sem, p)
    if sz.direct:
        small_middle(r.early_ta, r.early_dev, r.early_sem, False)

    unpick = onehot(iota((sz.tp, nq * qt), 1) == r.perm_col[:, 0:1].astype(jnp.int32)).astype(BF16)
    dattn = mm(unpick, r.da_all[...].reshape(nq * qt, d)).astype(BF16)
    w_out = r.w_out[...].reshape(sz.inner, d)
    dmixed = mm(dattn, w_out, NT).astype(BF16).reshape(flat)

    def piece_start(n, values):
        half = values.reshape(2, sz.half, d)
        r.pd_send[n] = half.astype(BF16)
        go(r.pd_send.at[n, 1 - c], r.pd_in.at[n], r.pd_sem, n, other)

    def piece_middle(n):
        got(r.pd_in.at[n], r.pd_sem, n, other)
        both = r.pd_send[n, c].astype(F32) + r.pd_in[n].astype(F32)
        for e in range(ea):
            r.pz_send[n, e] = both[e * sz.piece : (e + 1) * sz.piece].astype(BF16)
        for s in later:
            t = target[s]
            go(r.pz_send.at[n, t], r.pz_in.at[n, z], r.pz_sem, (n, s), ea_peer[s])
        r.pz_in[n, z] = r.pz_send[n, z]

    def piece_last(n):
        for s in later:
            got(r.pz_in.at[n, source[s]], r.pz_sem, (n, s), ea_peer[s])
        total = r.pz_in[n, 0].astype(F32)
        for e in range(1, ea):
            total = total + r.pz_in[n, e].astype(F32)
        r.p_all[n, c, z] = total.astype(BF16)
        for s in later:
            block = r.p_all.at[n, c, z]
            go(block, block, r.pa_sem, (n, s), ea_peer[s])
        go(r.p_all.at[n, c, z], r.p_all.at[n, c, z], r.pb_sem, (n, 0), other)

    def piece_pass(n):
        for s in later:
            block = r.p_all.at[n, c, source[s]]
            got(block, r.pa_sem, (n, s), ea_peer[s])
            go(block, block, r.pb_sem, (n, s), other)

    def piece_end(n):
        for s in range(ea):
            got(r.p_all.at[n, 1 - c, source[s]], r.pb_sem, (n, s), other)

    if not sz.direct:

        def piece_start(n, values):
            r.o_piece[n] = values

        piece_middle = piece_last = piece_pass = piece_end = lambda n: None

    keeps = []
    for n, own, taken, out in ((0, r.up_low, r.up_in, r.o_up), (1, r.down_low, r.down_in, r.o_down)):
        got(taken, r.rep_sem, n, other)
        taken[...] = (own[...].astype(F32) + taken[...].astype(F32)).astype(BF16)
        keeps.append(pltpu.make_async_copy(taken, out, r.load_sem.at[n]))
        keeps[-1].start()
    got(r.bias_in, r.rep_sem, 2, other)
    r.o_bias[...] = r.bias_acc[...] + r.bias_in[...]
    piece_start(0, mm(r.mixed[...].reshape(sz.tp, sz.inner), dattn, TN))
    if sz.direct:
        small_last(r.early_dev, r.early_ea, r.early_sem)

    def attention_back(image):
        queries, keys, values, dmix = r.q[image], r.k[image], r.v[image], dmixed[image]
        dquery = jnp.zeros((sz.lp, sz.inner), F32)
        dkey, dvalue = dquery, dquery
        for head in range(sz.heads):
            mask_low, mask = head_mask(sz, head, BF16), head_mask(sz, head, F32)
            scores = mm(queries * mask_low, keys, NT) * scale
            probs = jnp.where(live, jnp.exp(scores - r.lse[image][:, head : head + 1]), 0.0)
            dprobs = mm(dmix * mask_low, values, NT)
            dvalue = dvalue + mm(probs.astype(BF16), dmix, TN) * mask
            inner = jnp.sum(probs * dprobs, axis=-1, keepdims=True)
            dscores = (probs * (dprobs - inner)).astype(BF16)
            dquery = dquery + mm(dscores, keys) * (mask * scale)
            dkey = dkey + mm(dscores, queries, TN) * (mask * scale)
        for n, values in enumerate((dquery, dkey, dvalue)):
            r.dproj[n, image] = values.astype(BF16)

    attention_back(0)
    piece_middle(0)
    for image in range(1, sz.images):
        attention_back(image)
    for copy in home_copies:
        copy.wait_send()
    finished += home_copies
    for s in later + [0]:
        g = target[s]
        share = share_sum(r.rows_all, r.eo_in, r.eo_sem, s)
        if s:
            r.rgz_send[g] = share.astype(BF16)
            go(r.rgz_send.at[g], r.eo_back.at[z], r.eoz_sem, s, ea_peer[s])
        else:
            r.eo_back[z] = share.astype(BF16)

    dproj = [r.dproj[n].reshape(sz.tp, sz.inner) for n in range(3)]
    for n in (2, 0, 1):
        piece_start(n + 1, mm(dproj[n], r.a_low[...], TN))
    piece_last(0)
    into_part = mm(dproj[0], r.qkv_w[0]) + mm(dproj[1], r.qkv_w[1]) + mm(dproj[2], r.qkv_w[2])
    r.in_send[...] = mm(pick_all, into_part.astype(BF16)).astype(BF16).reshape(nq, qt, d)
    for p in partners:
        go(r.in_send.at[quarter[p]], r.in_part.at[j], r.ip_sem, p, ta_peer[p])
    r.in_part[j] = r.in_send[j]
    _, hat_one, _ = layer_norm(r.padded[...].reshape(sz.tp, d).astype(F32), flat_row(r.gain1), flat_row(r.bias1))
    rows_at = iota((8, 1), 0)
    late = jnp.where(rows_at == 0, jnp.sum(into_part * hat_one, axis=0, keepdims=True), 0.0)
    late = late + jnp.where(rows_at == 1, jnp.sum(into_part, axis=0, keepdims=True), 0.0)
    for row, n in ((2, 0), (3, 2)):
        total = jnp.sum(dproj[n].astype(F32), axis=0, keepdims=True)
        wide = jnp.concatenate([total, jnp.zeros((1, d - sz.inner), F32)], axis=1)
        late = late + jnp.where(rows_at == row, wide, 0.0)
    if sz.direct:
        small_start(late, r.late_ta, r.late_sem)
    else:
        r.o_late[...] = late
    for n in (3, 1, 2):
        piece_middle(n)
    if sz.direct:
        small_middle(r.late_ta, r.late_dev, r.late_sem, True)

    for p in partners:
        got(r.in_part.at[quarter[p]], r.ip_sem, p, ta_peer[p])
    into_one = r.in_part[0].astype(F32)
    for q in range(1, nq):
        into_one = into_one + r.in_part[q].astype(F32)
    x_mine = mm(pick_of(j), r.padded[...].reshape(sz.tp, d))
    _, hat_mine, inv_mine = layer_norm(x_mine, flat_row(r.gain1), flat_row(r.bias1))
    grad = r.dhidden[...] + norm_back(into_one, hat_mine, inv_mine, flat_row(r.gain1))
    r.ig_all[j] = grad.astype(BF16)
    for p in partners:
        go(r.ig_all.at[j], r.ig_all.at[j], r.ig_sem, p, ta_peer[p])
    if sz.direct:
        small_last(r.late_dev, r.late_ea, r.late_sem)

    for s in later:
        got(r.eo_back.at[source[s]], r.eoz_sem, s, ea_peer[s])
    output = r.hidden[...] + mm(back, r.eo_back[...].reshape(sz.experts * cs, d))
    r.out_all[j] = output.astype(BF16)
    for p in partners:
        go(r.out_all.at[j], r.out_all.at[j], r.out_sem, p, ta_peer[p])
    for n in (3, 1, 2):
        piece_last(n)
    for n in (0, 3, 1, 2):
        piece_pass(n)
    stores = []

    def store(n, values, src, dst):
        src[...] = values.reshape(src.shape)
        stores.append(pltpu.make_async_copy(src, dst, r.load_sem.at[n]))
        stores[-1].start()

    for p in partners:
        got(r.ig_all.at[quarter[p]], r.ig_sem, p, ta_peer[p])
    store(2, mm(unpick, r.ig_all[...].reshape(nq * qt, d)).astype(BF16), r.a_low, r.o_in)
    for p in partners:
        got(r.out_all.at[quarter[p]], r.out_sem, p, ta_peer[p])
    store(3, mm(unpick, r.out_all[...].reshape(nq * qt, d)).astype(BF16), r.padded, r.o_out)
    if sz.direct:
        small_end(r.early_ea, r.o_early, r.early_sem)
        small_end(r.late_ea, r.o_late, r.late_sem)
    for n in (0, 3, 1, 2):
        piece_end(n)
    for copy in stores + keeps:
        copy.wait()
    for copy in started:
        if not any(copy is done for done in finished):
            copy.wait_send()


def flat_row(ref):
    return ref[...].reshape(1, -1)


def fit(values, rows):
    have = values.shape[0]
    if have >= rows:
        return values[:rows]
    return jnp.concatenate([values, jnp.zeros((rows - have, values.shape[1]), F32)])


def run_block(sz, inputs):
    nq, ea, d, cs, qt = sz.nq, sz.ea, sz.d, sz.cs, sz.qt
    dma = pltpu.SemaphoreType.DMA
    rows = sz.blocks * cs
    outs = {
        "o_out": ((sz.images, sz.lp, d), BF16),
        "o_in": ((sz.tp, d), BF16),
        "o_early": ((sz.early, d), F32),
        "o_late": ((8, d), F32),
        "o_up": ((d, sz.hidden), BF16),
        "o_down": ((sz.hidden, d), BF16),
        "o_bias": ((8, d), F32),
    }
    flat = (sz.images, sz.lp, sz.inner)
    block = (cs, d)
    buffers = {
        "tok_v": ((sz.images, sz.length, d), BF16),
        "cot_v": ((sz.images, sz.length, d), BF16),
        "qkv_w": ((3, sz.inner, d), BF16),
        "up_w": ((d, sz.hidden), BF16),
        "down_w": ((sz.hidden, d), BF16),
        "w_full": ((nq, 2, sz.half, d), BF16),
        "padded": ((sz.images, sz.lp, d), BF16),
        "perm_col": ((sz.tp, 128), F32),
        "place_row": ((4, qt), jnp.int32),
        "place_col": ((qt, 128), jnp.int32),
        "a_low": ((sz.tp, d), BF16),
        "q": (flat, BF16),
        "k": (flat, BF16),
        "v": (flat, BF16),
        "mixed": (flat, BF16),
        "lse": ((sz.images, sz.lp, 128), F32),
        "dproj": ((3,) + flat, BF16),
        "mix_send": ((nq, qt, sz.inner), BF16),
        "mix_in": ((2, nq, qt, sz.inner), BF16),
        "dy_mine": ((qt, d), BF16),
        "hidden": ((qt, d), F32),
        "dhidden": ((qt, d), F32),
        "b_low": ((qt, d), BF16),
        "probs": ((sz.ep, qt), F32),
        "dy_send": ((2, ea) + block, BF16),
        "gate_send": ((2, ea, 8, 128), F32),
        "dy_all": ((nq, ea) + block, BF16),
        "rows_all": ((nq, ea) + block, BF16),
        "gate_all": ((nq, ea, 8, 128), F32),
        "act_t": ((sz.kept, rows, sz.hidden), BF16),
        "pre_t": ((sz.kept, rows, sz.hidden), BF16),
        "slot_t": ((sz.kept, rows, d), BF16),
        "out_t": ((sz.kept, rows, d), BF16),
        "dg_send": ((nq, ea, 8, 128), F32),
        "dg_in": ((nq, ea, 8, 128), F32),
        "rg_in": ((2, ea) + block, BF16),
        "rg_relay": ((2, ea, cs // 2, d), BF16),
        "eo_in": ((2, ea) + block, BF16),
        "eo_relay": ((2, ea, cs // 2, d), BF16),
        "rgz_send": ((ea,) + block, BF16),
        "dgz_send": ((ea, 8, 128), F32),
        "rg_back": ((ea,) + block, BF16),
        "eo_back": ((ea,) + block, BF16),
        "dg_back": ((ea, 8, 128), F32),
        "up_acc": ((d, sz.hidden), F32),
        "down_acc": ((sz.hidden, d), F32),
        "bias_acc": ((8, d), F32),
        "up_low": ((d, sz.hidden), BF16),
        "down_low": ((sz.hidden, d), BF16),
        "up_in": ((d, sz.hidden), BF16),
        "down_in": ((sz.hidden, d), BF16),
        "bias_in": ((8, d), F32),
        "da_all": ((nq, qt, d), BF16),
        "ig_all": ((nq, qt, d), BF16),
        "out_all": ((nq, qt, d), BF16),
        "in_send": ((nq, qt, d), BF16),
        "in_part": ((nq, qt, d), BF16),
    }
    sems = {
        "w_sem": (nq,),
        "wd_sem": (nq,),
        "dyz_sem": (2, ea),
        "dyt_sem": (nq, ea),
        "mix_sem": (2, nq),
        "gatez_sem": (2, ea),
        "rowz_sem": (2, ea),
        "rowt_sem": (nq, ea),
        "rowr_sem": (3, ea),
        "gatet_sem": (nq,),
        "dg_sem": (nq,),
        "rg_sem": (6, ea),
        "rep_sem": (3,),
        "dgz_sem": (ea,),
        "rgz_sem": (ea,),
        "eo_sem": (6, ea),
        "eoz_sem": (ea,),
        "da_sem": (nq,),
        "early_sem": (3, max(nq, ea)),
        "late_sem": (3, max(nq, ea)),
        "pd_sem": (4,),
        "pz_sem": (4, ea),
        "pa_sem": (4, ea),
        "pb_sem": (4, ea),
        "ip_sem": (nq,),
        "ig_sem": (nq,),
        "out_sem": (nq,),
    }
    if sz.direct:
        outs["p_all"] = ((4, 2, ea, sz.piece, d), BF16)
        buffers |= {
            "early_ta": ((nq, sz.early, d), F32),
            "early_dev": ((2, sz.early, d), F32),
            "early_ea": ((ea, sz.early, d), F32),
            "late_ta": ((nq, 8, d), F32),
            "late_dev": ((2, 8, d), F32),
            "late_ea": ((ea, 8, d), F32),
            "pd_send": ((4, 2, sz.half, d), BF16),
            "pd_in": ((4, sz.half, d), BF16),
            "pz_send": ((4, ea, sz.piece, d), BF16),
            "pz_in": ((4, ea, sz.piece, d), BF16),
        }
    else:
        outs["o_piece"] = ((4, sz.inner, d), F32)
    if sz.direct:
        buffers["row_send"] = ((2, ea) + block, BF16)
    names = list(inputs) + list(outs) + list(buffers) + list(sems) + ["load_sem"]
    vm = pl.BlockSpec(memory_space=pltpu.VMEM)
    far = pl.BlockSpec(memory_space=pltpu.HBM)
    results = pl.pallas_call(
        functools.partial(block_kernel, sz, names),
        out_shape=[jax.ShapeDtypeStruct(*spec) for spec in outs.values()],
        in_specs=[far if name in ("tok", "cot", "w_qkv", "w_up", "w_down") else vm for name in inputs],
        out_specs=[far if name in ("o_up", "o_down", "o_in", "o_out") else vm for name in outs],
        scratch_shapes=[pltpu.VMEM(*spec) for spec in buffers.values()]
        + [dma((2,) + shape) for shape in sems.values()]
        + [dma((8,))],
        name="block",
        compiler_params=pltpu.CompilerParams(
            collective_id=0, has_side_effects=True, vmem_limit_bytes=60 << 20
        ),
    )(*inputs.values())
    return dict(zip(outs, results))


def finish_kernel(sz, names, *refs):
    r = types.SimpleNamespace(**dict(zip(names, refs)))
    n, d = sz.experts, sz.d
    loads, stores = [], []

    def load(src, dst):
        loads.append(pltpu.make_async_copy(src, dst, r.sem_in.at[len(loads)]))
        loads[-1].start()

    def store(src, dst):
        stores.append(pltpu.make_async_copy(src, dst, r.sem_out.at[len(stores)]))
        stores[-1].start()

    third = d // 3
    spans = [pl.ds(k * third, third) for k in range(3)]
    for src, dst in ((r.up, r.up_v), (r.down, r.down_v)):
        for span in spans:
            load(src.at[span], dst.at[span])
    load(r.grad, r.grad_v)
    load(r.out, r.out_v)
    load(r.piece, r.piece_v)
    for dst, src in (
        (r.f_b, r.early[n + 2 : n + 3]),
        (r.f_g1, r.late[0:1]),
        (r.f_c1, r.late[1:2]),
        (r.f_g2, r.early[n : n + 1]),
        (r.f_c2, r.early[n + 1 : n + 2]),
    ):
        dst[...] = src.reshape(d)
    r.f_router[...] = r.early[0:n]
    r.f_qv[...] = r.late[2:4, 0 : sz.inner]
    r.f_upb[...] = r.bias[0:1]
    r.f_downb[...] = r.bias[1:2]
    at = 0
    for src, wide, dst in ((r.up_v, r.up_w, r.f_up), (r.down_v, r.down_w, r.f_down)):
        for span in spans:
            loads[at].wait()
            at += 1
            wide[span] = src[span].astype(F32)
            store(wide.at[span], dst.at[span])
    loads[at].wait()
    for image in range(sz.images):
        r.grad_w[:, image, :] = r.grad_v[image * sz.lp : image * sz.lp + sz.length].astype(F32)
    store(r.grad_w, r.f_grad)
    loads[at + 1].wait()
    for image in range(sz.images):
        r.out_w[:, image, :] = r.out_v[image, 0 : sz.length]
    store(r.out_w, r.f_out)
    loads[at + 2].wait()
    for k in range(4):
        for core in range(2):
            for e in range(sz.ea):
                start = core * sz.half + e * sz.piece
                r.piece_w[k, start : start + sz.piece] = r.piece_v[k, core, e].astype(F32)
        store(r.piece_w.at[k], r.f_qkv.at[k - 1] if k else r.f_o)
    for copy in stores:
        copy.wait()


def finish(sz, got):
    d, n = sz.d, sz.experts
    inputs = {
        "up": got["o_up"],
        "down": got["o_down"],
        "out": got["o_out"],
        "grad": got["o_in"],
        "piece": got["p_all"],
        "early": got["o_early"],
        "late": got["o_late"],
        "bias": got["o_bias"],
    }
    outs = {
        "f_out": ((sz.length, sz.images, d), BF16),
        "f_grad": ((sz.length, sz.images, d), F32),
        "f_qkv": ((3, sz.inner, d), F32),
        "f_qv": ((2, sz.inner), F32),
        "f_o": ((sz.inner, d), F32),
        "f_b": ((d,), F32),
        "f_g1": ((d,), F32),
        "f_c1": ((d,), F32),
        "f_g2": ((d,), F32),
        "f_c2": ((d,), F32),
        "f_router": ((n, d), F32),
        "f_up": ((d, sz.hidden), F32),
        "f_upb": ((1, sz.hidden), F32),
        "f_down": ((sz.hidden, d), F32),
        "f_downb": ((1, d), F32),
    }
    buffers = {
        "up_v": ((d, sz.hidden), BF16),
        "down_v": ((sz.hidden, d), BF16),
        "grad_v": ((sz.tp, d), BF16),
        "out_v": ((sz.images, sz.lp, d), BF16),
        "piece_v": ((4, 2, sz.ea, sz.piece, d), BF16),
        "up_w": ((d, sz.hidden), F32),
        "down_w": ((sz.hidden, d), F32),
        "grad_w": ((sz.length, sz.images, d), F32),
        "out_w": ((sz.length, sz.images, d), BF16),
        "piece_w": ((4, sz.inner, d), F32),
    }
    vm = pl.BlockSpec(memory_space=pltpu.VMEM)
    far = pl.BlockSpec(memory_space=pltpu.HBM)
    large = ("up", "down", "out", "grad", "piece", "f_out", "f_grad", "f_qkv", "f_o", "f_up", "f_down")
    names = list(inputs) + list(outs) + list(buffers) + ["sem_in", "sem_out"]
    results = pl.pallas_call(
        functools.partial(finish_kernel, sz, names),
        out_shape=[jax.ShapeDtypeStruct(*spec) for spec in outs.values()],
        in_specs=[far if name in large else vm for name in inputs],
        out_specs=[far if name in large else vm for name in outs],
        scratch_shapes=[pltpu.VMEM(*spec) for spec in buffers.values()]
        + [pltpu.SemaphoreType.DMA((16,)), pltpu.SemaphoreType.DMA((16,))],
        name="finish",
        compiler_params=pltpu.CompilerParams(vmem_limit_bytes=60 << 20),
    )(*inputs.values())
    (out, grad, qkv, qv, o, b, g1, c1, g2, c2, router, up, up_b, down, down_b) = results
    turn = lambda t: jnp.swapaxes(t, 0, 1)
    return (
        turn(out),
        turn(grad),
        jnp.swapaxes(qkv, 1, 2),
        qv,
        o,
        b,
        g1,
        c1,
        g2,
        c2,
        router.T,
        up[None],
        up_b,
        down[None],
        down_b,
    )


def local(
    tokens,
    expert_ids,
    pair_ranks,
    cotangent,
    w_qkv,
    b_qv,
    w_out,
    b_out,
    ln1_gain,
    ln1_bias,
    ln2_gain,
    ln2_bias,
    w_router,
    w_up,
    b_up,
    w_down,
    b_down,
):
    sz = Sizes(tokens, expert_ids, w_qkv, w_up)
    pairs = jnp.stack([jnp.transpose(t, (2, 0, 1)) for t in (expert_ids, pair_ranks)])
    pairs = jnp.pad(
        pairs, ((0, 0), (0, 0), (0, 0), (0, sz.lp - sz.length)), constant_values=sz.tokens * 2
    )
    table = jnp.pad(pairs.reshape(4, sz.tp).astype(F32), ((0, 4), (0, ceil_to(sz.tp, 128) - sz.tp)))
    inputs = {
        "tok": tokens,
        "cot": cotangent,
        "w_qkv": jnp.swapaxes(w_qkv, 1, 2),
        "b_qv": b_qv,
        "w_out": w_out.reshape(2, sz.half, sz.d),
        "b_out": b_out,
        "gain1": ln1_gain,
        "bias1": ln1_bias,
        "gain2": ln2_gain,
        "bias2": ln2_bias,
        "router": w_router.T,
        "w_up": w_up[0],
        "b_up": b_up,
        "w_down": w_down[0],
        "b_down": b_down,
        "table": table,
    }
    got = run_block(sz, inputs)
    if sz.direct:
        return finish(sz, got)
    n = sz.experts
    piece, shared = lax.psum((got["o_piece"], got["o_late"][2:4]), ("ea", "dev"))
    early, late = lax.psum((got["o_early"], got["o_late"][:2]), ("ea", "ta", "dev"))
    return (
        got["o_out"][:, : sz.length],
        got["o_in"].reshape(got["o_out"].shape)[:, : sz.length].astype(F32),
        jnp.swapaxes(piece[1:], 1, 2),
        shared[:, : sz.inner],
        piece[0],
        early[n + 2],
        late[0],
        late[1],
        early[n],
        early[n + 1],
        early[:n].T,
        got["o_up"].astype(F32)[None],
        got["o_bias"][0:1],
        got["o_down"].astype(F32)[None],
        got["o_bias"][1:2],
    )


def solution(mesh):
    in_specs = (
        P(("ea", "dev"), None, None),
        P(("ea", "dev"), None, None),
        P(("ea", "dev"), None, None),
        P(("ea", "dev"), None, None),
        P(None, None, "ta"),
        P(None, "ta"),
        P("ta", None),
        P(),
        P(),
        P(),
        P(),
        P(),
        P(),
        P("ea", None, "ta"),
        P("ea", "ta"),
        P("ea", "ta", None),
        P("ea", None),
    )
    out_specs = (
        P(("ea", "dev"), None, None),
        P(("ea", "dev"), None, None),
        P(None, None, "ta"),
        P(None, "ta"),
        P("ta", None),
        P(),
        P(),
        P(),
        P(),
        P(),
        P(),
        P("ea", None, "ta"),
        P("ea", "ta"),
        P("ea", "ta", None),
        P("ea", None),
    )
    return jax.shard_map(local, mesh=mesh, in_specs=in_specs, out_specs=out_specs, check_vma=False)
```

```python
import functools
import types

import jax
import jax.numpy as jnp
from jax import lax
from jax.experimental import pallas as pl
from jax.experimental.pallas import tpu as pltpu
from jax.sharding import PartitionSpec as P

HDIM = 64
EPSILON = 1e-06
F32, BF16 = jnp.float32, jnp.bfloat16
EXACT = lax.Precision.HIGHEST
MESH = pl.DeviceIdType.MESH
NT = (((1,), (1,)), ((), ()))
TN = (((0,), (0,)), ((), ()))
NN = (((1,), (0,)), ((), ()))


def ceil_to(value, unit):
    return -(-value // unit) * unit


def mm(a, b, dims=NN, precision=None):
    return lax.dot_general(a, b, dims, precision=precision, preferred_element_type=F32)


def iota(shape, dim):
    return lax.broadcasted_iota(jnp.int32, shape, dim)


def onehot(mask):
    return jnp.where(mask, 1.0, 0.0).astype(F32)


class Sizes:
    def __init__(self, tokens, expert_ids, w_qkv, w_up):
        self.images, self.length, self.d = tokens.shape
        self.top = expert_ids.shape[2]
        self.tokens = self.images * self.length
        self.ea = lax.axis_size("ea")
        self.nq = lax.axis_size("ta")
        assert w_up.shape[0] == 1
        self.experts = self.ea
        self.cap = (9 * self.tokens * self.top + 8 * self.experts - 1) // (8 * self.experts)
        self.inner = w_qkv.shape[2]
        self.heads = self.inner // HDIM
        self.hidden = w_up.shape[2]
        self.lp = ceil_to(self.length, 16)
        self.tp = self.images * self.lp
        per_quarter = -(-self.tokens // self.nq)
        self.qt = ceil_to(per_quarter, 16)
        spread = (self.cap + (self.nq - 1) * self.experts) // self.nq
        self.cs = ceil_to(min(self.cap, per_quarter, spread), 16)
        self.ep = ceil_to(self.experts, 16)
        self.half = self.inner // 2
        self.piece = self.half // self.ea
        self.early = ceil_to(self.experts + 3, 8)
        self.blocks = max(1, min(self.ea, (256 if self.ea <= 8 else 64) // self.cs))
        self.chunks = self.ea // self.blocks
        self.direct = self.ea <= 8
        self.relay = [s for s in range(1, self.ea) if self.direct and s >= 2]
        self.kept = self.nq if self.chunks == 1 else 1
        assert self.top == 2 and self.nq == 4


def route(sz, table):
    rows = [table[n : n + 1, : sz.tp] for n in range(4)]
    cols = table.T[: sz.tp]
    wide = iota((sz.tp, 128), 1)

    def count(mask):
        return jnp.sum(jnp.where(mask, 1.0, 0.0), axis=1, keepdims=True)

    def flip(*columns):
        spread = jnp.zeros((sz.tp, 128), F32)
        for n, column in enumerate(columns):
            spread = spread + jnp.where(wide == n, column, 0.0)
        turned = spread.T
        return [turned[n : n + 1] for n in range(len(columns))]

    real = cols[:, 0:1] < sz.experts
    dest = []
    for k in range(2):
        ids, ranks = cols[:, k : k + 1], cols[:, 2 + k : 3 + k]
        position = sum(count((rows[m] == ids) & (rows[2 + m] < ranks)) for m in range(2))
        dest.append(jnp.where((position < sz.cap) & real, ids, float(sz.experts)))
    low, high = jnp.minimum(*dest), jnp.maximum(*dest)
    index = iota((sz.tp, 1), 0).astype(F32)
    kind = jnp.where(real, low * (sz.experts + 1) + high, float((sz.experts + 1) ** 2))
    key = kind * sz.tp + index
    (key_row,) = flip(key)
    order = count(key_row < key)
    lap = jnp.floor((order + 0.5) * (1.0 / sz.nq))
    quarter = order - lap * sz.nq
    group = [d * sz.nq + quarter for d in dest]
    perm = jnp.where(real, quarter * sz.qt + lap, -1.0)
    order_row, perm_row, *group_row = flip(order, perm, *group)
    place = []
    for k in range(2):
        slot = sum(count((group_row[m] == group[k]) & (order_row < order)) for m in range(2))
        place.append(jnp.where(dest[k] < sz.experts, dest[k] * sz.cs + slot + 1.0, 0.0))
    place_row = flip(*place)
    return perm, perm_row, place, place_row


def layer_norm(values, gain_vec, shift_vec):
    row_mean = jnp.mean(values, axis=-1, keepdims=True)
    centered = values - row_mean
    variance = jnp.mean(centered * centered, axis=-1, keepdims=True)
    inverse = lax.rsqrt(variance + EPSILON)
    normed = centered * inverse
    return (normed * gain_vec + shift_vec, normed, inverse)


def norm_back(grad_rows, normed, inverse, gain_vec):
    scaled = grad_rows * gain_vec
    return inverse * (
        scaled
        - jnp.mean(scaled, axis=-1, keepdims=True)
        - normed * jnp.mean(scaled * normed, axis=-1, keepdims=True)
    )


def push(src, dst, send_sem, recv_sem, device):
    return pltpu.make_async_remote_copy(
        src_ref=src,
        dst_ref=dst,
        send_sem=send_sem,
        recv_sem=recv_sem,
        device_id=device,
        device_id_type=MESH,
    )


def greet(devices):
    barrier = pltpu.get_barrier_semaphore()
    for device in devices:
        pl.semaphore_signal(barrier, inc=1, device_id=device, device_id_type=MESH)


def head_mask(sz, head, dtype):
    lane = iota((1, sz.inner), 1)
    return onehot((lane >= head * HDIM) & (lane < (head + 1) * HDIM)).astype(dtype)


def gelu_parts(values):
    cdf = 0.5 * (1.0 + lax.erf(values * (0.5**0.5)))
    density = jnp.exp(-0.5 * values * values) * (0.5 / jnp.pi) ** 0.5
    return cdf, density


def block_kernel(sz, names, *refs):
    r = types.SimpleNamespace(**dict(zip(names, refs)))
    z, j, c = lax.axis_index("ea"), lax.axis_index("ta"), lax.axis_index("dev")
    nq, ea, d, cs, qt = sz.nq, sz.ea, sz.d, sz.cs, sz.qt
    quarter = [j, j + 1 - 2 * lax.rem(j, 2), j + 2 - 4 * lax.div(j, 2), 3 - j]
    ta_peer = [{"ta": q} for q in quarter]
    ea_peer = [{"ea": lax.rem(z + s, ea)} for s in range(ea)]
    source = [lax.rem(z - s + ea, ea) for s in range(ea)]
    target = [lax.rem(z + s, ea) for s in range(ea)]
    other = {"dev": 1 - c}
    later = [s for s in range(1, ea)]
    partners = (1, 2, 3)
    started = []

    def go(src, dst, sem, index, device):
        index = index if isinstance(index, tuple) else (index,)
        copy = push(src, dst, sem.at[(0,) + index], sem.at[(1,) + index], device)
        copy.start()
        started.append(copy)
        return copy

    def got(dst, sem, index, device):
        index = index if isinstance(index, tuple) else (index,)
        push(dst, dst, sem.at[(1,) + index], sem.at[(1,) + index], device).wait_recv()

    everyone = ta_peer[1:] + ea_peer[1:] + [other]
    greet(everyone)
    loads = []
    for n, (src, dst) in enumerate(
        ((r.cot, r.cot_v), (r.tok, r.tok_v), (r.w_qkv, r.qkv_w), (r.w_up, r.up_w), (r.w_down, r.down_w))
    ):
        loads.append(pltpu.make_async_copy(src, dst, r.load_sem.at[n]))
        loads[-1].start()
    perm_col, perm, place, place_rows = route(sz, r.table[...])
    pl.semaphore_wait(pltpu.get_barrier_semaphore(), len(everyone))

    for p in partners:
        go(r.w_out.at[c], r.w_full.at[j, c], r.w_sem, p, ta_peer[p])
    r.w_full[j] = r.w_out[...]

    perm = perm.astype(jnp.int32)
    r.perm_col[...] = jnp.broadcast_to(perm_col, (sz.tp, 128))
    pick_all = onehot(iota((nq * qt, sz.tp), 0) == perm).astype(BF16)

    def pick_of(q):
        return onehot(iota((qt, sz.tp), 0) + q * qt == perm).astype(BF16)

    spread = iota((8, 1), 0)
    both = jnp.where(spread == 0, place_rows[0], 0.0) + jnp.where(spread == 1, place_rows[1], 0.0)
    for which, q in ((0, quarter[0]), (1, quarter[3])):
        chosen = mm(both, onehot(iota((qt, sz.tp), 0) + q * qt == perm), NT, EXACT)
        r.place_row[2 * which : 2 * which + 2] = (chosen[0:2] + 0.5).astype(jnp.int32) - 1
    pair_col = jnp.where(iota((1, 128), 1) == 0, place[0], 0.0)
    pair_col = pair_col + jnp.where(iota((1, 128), 1) == 1, place[1], 0.0)
    chosen = mm(onehot(iota((qt, sz.tp), 0) + j * qt == perm), pair_col, NN, EXACT)
    r.place_col[...] = (chosen + 0.5).astype(jnp.int32) - 1

    def slots_of(expert, which):
        row = iota((cs, qt), 0) + expert * cs
        first, second = r.place_row[2 * which : 2 * which + 1], r.place_row[2 * which + 1 : 2 * which + 2]
        return onehot((row == first) | (row == second))

    tail = (sz.length // 16) * 16
    loads[0].wait()
    for image in range(sz.images):
        r.padded[image, tail:] = jnp.zeros((sz.lp - tail, d), BF16)
        r.padded[image, 0 : sz.length] = r.cot_v[image]
    for which, q in ((0, quarter[0]), (1, quarter[3])):
        dy_rows = mm(pick_of(q), r.padded[...].reshape(sz.tp, d)).astype(BF16)
        if which == 0:
            r.dy_mine[...] = dy_rows
        for expert in range(sz.experts):
            r.dy_send[which, expert] = mm(slots_of(expert, which).astype(BF16), dy_rows).astype(BF16)
    dy_copies = []
    for which, q in ((0, quarter[0]), (1, quarter[3])):
        for s in later:
            copy = go(r.dy_send.at[which, target[s]], r.dy_all.at[q, z], r.dyz_sem, (which, s), ea_peer[s])
            dy_copies.append(copy)
        r.dy_all[q, z] = r.dy_send[which, z]

    def forward(ref, z_sem, t_sem):
        copies = []
        for s in [0] + later[1:] + later[:1]:
            block = ref.at[j, source[s]]
            if s:
                got(block, z_sem, (0, s), ea_peer[s])
            for p in (1, 2):
                copies.append(go(block, block, t_sem, (p, s), ta_peer[p]))
        return copies

    loads[1].wait()
    loads[2].wait()
    for image in range(sz.images):
        r.padded[image, 0 : sz.length] = r.tok_v[image]
    normed_one, _, _ = layer_norm(
        r.padded[...].reshape(sz.tp, d).astype(F32), flat_row(r.gain1), flat_row(r.bias1)
    )
    a_low = normed_one.astype(BF16)
    r.a_low[...] = a_low
    flat = (sz.images, sz.lp, sz.inner)
    r.q[...] = (mm(a_low, r.qkv_w[0], NT) + r.b_qv[0:1]).astype(BF16).reshape(flat)
    r.k[...] = mm(a_low, r.qkv_w[1], NT).astype(BF16).reshape(flat)
    r.v[...] = (mm(a_low, r.qkv_w[2], NT) + r.b_qv[1:2]).astype(BF16).reshape(flat)

    for p in partners:
        block = r.w_full.at[quarter[p], c]
        got(block, r.w_sem, p, ta_peer[p])
        go(block, block, r.wd_sem, p, other)

    scale = HDIM ** (-0.5)
    live = iota((1, sz.lp), 1) < sz.length
    for image in range(sz.images):
        queries, keys, values = r.q[image], r.k[image], r.v[image]
        mixed = jnp.zeros((sz.lp, sz.inner), F32)
        logs = jnp.zeros((sz.lp, 128), F32)
        for head in range(sz.heads):
            scores = mm(queries * head_mask(sz, head, BF16), keys, NT) * scale
            scores = jnp.where(live, scores, -1e30)
            peak = jnp.max(scores, axis=-1, keepdims=True)
            exps = jnp.exp(scores - peak)
            total = jnp.sum(exps, axis=-1, keepdims=True)
            probs_low = (exps / total).astype(BF16)
            mixed = mixed + mm(probs_low, values) * head_mask(sz, head, F32)
            logs = logs + jnp.where(iota((1, 128), 1) == head, peak + jnp.log(total), 0.0)
        r.mixed[image] = mixed.astype(BF16)
        r.lse[image] = logs
    dealt = mm(pick_all, r.mixed[...].reshape(sz.tp, sz.inner)).astype(BF16)
    r.mix_send[...] = dealt.reshape(nq, qt, sz.inner)
    for p in partners:
        go(r.mix_send.at[quarter[p]], r.mix_in.at[0, j], r.mix_sem, (0, p), ta_peer[p])
        go(r.mix_send.at[quarter[3 - p]], r.mix_in.at[1, j], r.mix_sem, (1, p), ta_peer[p])
    r.mix_in[0, j] = r.mix_send[j]
    r.mix_in[1, j] = r.mix_send[quarter[3]]
    x_rows = [mm(pick_of(q), r.padded[...].reshape(sz.tp, d)) for q in (quarter[0], quarter[3])]
    for p in partners:
        got(r.w_full.at[quarter[p], 1 - c], r.wd_sem, p, other)
    for p in partners:
        got(r.mix_in.at[0, quarter[p]], r.mix_sem, (0, p), ta_peer[p])
        got(r.mix_in.at[1, quarter[p]], r.mix_sem, (1, p), ta_peer[p])

    dy_forwards = forward(r.dy_all, r.dyz_sem, r.dyt_sem)

    finished = []
    if not sz.direct:
        r.row_send = r.dy_send
        for copy in dy_copies:
            copy.wait_send()
        finished += dy_copies
    router_w = r.router[...]
    if sz.ep > sz.experts:
        router_w = jnp.concatenate([router_w, jnp.zeros((sz.ep - sz.experts, d), BF16)])
    for which in (0, 1):
        attention = flat_row(r.b_out)
        for q in range(nq):
            attention = attention + mm(r.mix_in[which, q], r.w_full[q].reshape(sz.inner, d))
        hidden = x_rows[which] + attention
        normed_two, _, _ = layer_norm(hidden, flat_row(r.gain2), flat_row(r.bias2))
        b_low = normed_two.astype(BF16)
        logits = mm(router_w, b_low, NT)
        logits = jnp.where(iota((sz.ep, 1), 0) < sz.experts, logits, -1e30)
        exps = jnp.exp(logits - jnp.max(logits, axis=0, keepdims=True))
        router = exps / jnp.sum(exps, axis=0, keepdims=True)
        if which == 0:
            r.hidden[...], r.b_low[...], r.probs[...] = hidden, b_low, router
        for expert in range(sz.experts):
            slots = slots_of(expert, which)
            r.row_send[which, expert] = mm(slots.astype(BF16), b_low).astype(BF16)
            level = jnp.broadcast_to(router[expert : expert + 1], (8, qt))
            r.gate_send[which, expert, :, 0:cs] = mm(level, slots, NT, EXACT)
        q = quarter[3 * which]
        for s in later:
            t = target[s]
            go(r.gate_send.at[which, t], r.gate_all.at[q, z], r.gatez_sem, (which, s), ea_peer[s])
        for s in later[1:] + later[:1]:
            t = target[s]
            if which and s in sz.relay:
                continue
            go(r.row_send.at[which, t], r.rows_all.at[q, z], r.rowz_sem, (which, s), ea_peer[s])
        r.rows_all[q, z] = r.row_send[which, z]
        r.gate_all[q, z] = r.gate_send[which, z]
    row_forwards = forward(r.rows_all, r.rowz_sem, r.rowt_sem)
    for s in later:
        got(r.gate_all.at[j, source[s]], r.gatez_sem, (0, s), ea_peer[s])
    for p in (1, 2):
        go(r.gate_all.at[j], r.gate_all.at[j], r.gatet_sem, p, ta_peer[p])

    relays = []
    low_half, high_half = pl.ds(0, cs // 2), pl.ds(cs // 2, cs // 2)
    for s in sz.relay:
        for p, part in ((1, high_half), (2, low_half)):
            got(r.rows_all.at[quarter[p], source[s]], r.rowt_sem, (p, s), ta_peer[p])
            half = r.rows_all.at[quarter[p], source[s], part]
            relays.append(go(half, half, r.rowr_sem, (3 - p, s), ta_peer[3 - p]))

    loads[3].wait()
    loads[4].wait()
    first = jnp.where(j == 0, 1.0, 0.0)
    spot = iota((cs, cs), 0) == iota((cs, cs), 1)
    rows_n = sz.blocks * cs

    def expert_chunk(q, p, chunk):
        at = pl.ds(chunk * sz.blocks, sz.blocks) if sz.chunks > 1 else slice(None)
        keep = p if sz.kept > 1 else 0
        rows = r.rows_all[q, at].reshape(rows_n, d)
        dy = r.dy_all[q, at].reshape(rows_n, d).astype(F32)
        gates = []
        for b in range(sz.blocks):
            g = chunk * sz.blocks + b
            level = r.gate_all[q, g][0:1, 0:cs]
            gates.append(jnp.sum(jnp.where(spot, level, 0.0), axis=1, keepdims=True))
        gate = jnp.concatenate(gates, axis=0) if len(gates) > 1 else gates[0]
        pre_act = mm(rows, r.up_w[...]) + r.b_up[...]
        cdf, density = gelu_parts(pre_act)
        act_low = (pre_act * cdf).astype(BF16)
        slot_grad = (gate * dy).astype(BF16)
        pre_grad = (mm(slot_grad, r.down_w[...], NT) * (cdf + pre_act * density)).astype(BF16)
        row_grad = mm(pre_grad, r.up_w[...], NT).astype(BF16)
        r.act_t[keep], r.pre_t[keep], r.slot_t[keep] = act_low, pre_grad, slot_grad
        r.dy_all[q, at] = row_grad.reshape(sz.blocks, cs, d)
        expert_out = mm(act_low, r.down_w[...]) + first * r.b_down[...]
        r.out_t[keep] = (gate * expert_out).astype(BF16)
        dgate = jnp.sum(expert_out * dy, axis=1, keepdims=True)
        for b in range(sz.blocks):
            g = chunk * sz.blocks + b
            level = jnp.sum(
                jnp.where(spot, dgate[b * cs : (b + 1) * cs], 0.0), axis=0, keepdims=True
            )
            r.dg_send[p, g, :, 0:cs] = jnp.broadcast_to(level, (8, cs))

    def weight_chunk(q, p, chunk, fresh):
        at = pl.ds(chunk * sz.blocks, sz.blocks) if sz.chunks > 1 else slice(None)
        keep = p if sz.kept > 1 else 0
        rows = r.rows_all[q, at].reshape(rows_n, d)
        up = mm(rows, r.pre_t[keep], TN)
        down = mm(r.act_t[keep], r.slot_t[keep], TN)
        biases = jnp.concatenate(
            [
                jnp.sum(r.pre_t[keep].astype(F32), axis=0, keepdims=True),
                jnp.sum(r.slot_t[keep].astype(F32), axis=0, keepdims=True),
                jnp.zeros((6, d), F32),
            ]
        )
        if fresh:
            r.up_acc[...], r.down_acc[...], r.bias_acc[...] = up, down, biases
        else:
            r.up_acc[...] += up
            r.down_acc[...] += down
            r.bias_acc[...] += biases
        r.rows_all[q, at] = r.out_t[keep].reshape(sz.blocks, cs, d)

    parts = (None, (low_half, high_half), (high_half, low_half))
    blocks = later + [0]

    def share_diagonal(ref, relay_in, sem):
        for s in blocks:
            for n, p, part in ((0, 2, low_half), (1, 1, high_half)):
                half = ref.at[quarter[3], target[s], part]
                go(half, relay_in.at[n, target[s]], sem, (n, s), ta_peer[p])

    def share_straight(ref, taken, sem, p):
        for s in blocks:
            half = parts[p][1]
            src = ref.at[quarter[p], target[s], half]
            go(src, taken.at[p - 1, target[s], half], sem, (1 + p, s), ta_peer[p])

    def share_joined(ref, taken, relay_in, sem, p):
        for s in blocks:
            half = parts[p][0]
            g = target[s]
            got(relay_in.at[p - 1, g], sem, (p - 1, s), ta_peer[3 - p])
            joined = ref[quarter[p], g, half].astype(F32) + relay_in[p - 1, g].astype(F32)
            ref[quarter[p], g, half] = joined.astype(BF16)
            src = ref.at[quarter[p], g, half]
            go(src, taken.at[p - 1, g, half], sem, (3 + p, s), ta_peer[p])

    def share_sum(ref, taken, sem, s):
        g = target[s]
        total = ref[j, g].astype(F32)
        for p in (1, 2):
            got(taken.at[p - 1, g, parts[p][1]], sem, (1 + p, s), ta_peer[p])
            got(taken.at[p - 1, g, parts[p][0]], sem, (3 + p, s), ta_peer[p])
            total = total + taken[p - 1, g].astype(F32)
        return total

    for p in (0, 3, 1, 2):
        q = quarter[p]
        if p == 0:
            for copy in dy_forwards + row_forwards:
                copy.wait_send()
            finished += dy_forwards + row_forwards
        elif p == 3:
            for s in later:
                got(r.dy_all.at[q, source[s]], r.dyz_sem, (1, s), ea_peer[s])
                got(r.gate_all.at[q, source[s]], r.gatez_sem, (1, s), ea_peer[s])
                if s in sz.relay:
                    got(r.rows_all.at[q, source[s], low_half], r.rowr_sem, (1, s), ta_peer[1])
                    got(r.rows_all.at[q, source[s], high_half], r.rowr_sem, (2, s), ta_peer[2])
                else:
                    got(r.rows_all.at[q, source[s]], r.rowz_sem, (1, s), ea_peer[s])
        else:
            got(r.gate_all.at[q], r.gatet_sem, p, ta_peer[p])
            for s in range(ea):
                got(r.dy_all.at[q, source[s]], r.dyt_sem, (p, s), ta_peer[p])
                if s not in sz.relay:
                    got(r.rows_all.at[q, source[s]], r.rowt_sem, (p, s), ta_peer[p])
            if p == 1:
                for copy in relays:
                    copy.wait_send()
                finished += relays
        if sz.chunks == 1:
            expert_chunk(q, p, 0)
            if p == 0:
                weight_chunk(q, p, 0, True)
        else:
            if p == 0:
                r.up_acc[...] = jnp.zeros((d, sz.hidden), F32)
                r.down_acc[...] = jnp.zeros((sz.hidden, d), F32)
                r.bias_acc[...] = jnp.zeros((8, d), F32)

            @pl.loop(0, sz.chunks)
            def _(chunk):
                expert_chunk(q, p, chunk)
                weight_chunk(q, p, chunk, False)

        if p:
            go(r.dg_send.at[p], r.dg_in.at[p], r.dg_sem, p, ta_peer[p])
        if p == 3:
            share_diagonal(r.dy_all, r.rg_relay, r.rg_sem)
        elif p:
            share_straight(r.dy_all, r.rg_in, r.rg_sem, p)
            share_joined(r.dy_all, r.rg_in, r.rg_relay, r.rg_sem, p)
    if sz.chunks == 1:
        for p in (3, 1, 2):
            weight_chunk(quarter[p], p, 0, False)

    r.up_low[...] = r.up_acc[...].astype(BF16)
    r.down_low[...] = r.down_acc[...].astype(BF16)
    go(r.up_low, r.up_in, r.rep_sem, 0, other)
    go(r.down_low, r.down_in, r.rep_sem, 1, other)
    go(r.bias_acc, r.bias_in, r.rep_sem, 2, other)

    home_copies = []
    for p in partners:
        got(r.dg_in.at[p], r.dg_sem, p, ta_peer[p])
    for s in later + [0]:
        g = target[s]
        share = share_sum(r.dy_all, r.rg_in, r.rg_sem, s)
        dgate = r.dg_send[0, g]
        for p in partners:
            dgate = dgate + r.dg_in[p, g]
        if s:
            r.rgz_send[g] = share.astype(BF16)
            r.dgz_send[g] = dgate
            go(r.dgz_send.at[g], r.dg_back.at[z], r.dgz_sem, s, ea_peer[s])
            home_copies.append(go(r.rgz_send.at[g], r.rg_back.at[z], r.rgz_sem, s, ea_peer[s]))
        else:
            r.rg_back[z] = share.astype(BF16)
            r.dg_back[z] = dgate
    share_diagonal(r.rows_all, r.eo_relay, r.eo_sem)
    for p in (1, 2):
        share_straight(r.rows_all, r.eo_in, r.eo_sem, p)

    place_0, place_1 = r.place_col[:, 0:1], r.place_col[:, 1:2]
    lane = iota((qt, sz.experts * cs), 1)
    back = onehot((lane == place_0) | (lane == place_1)).astype(BF16)
    for s in later:
        got(r.dg_back.at[source[s]], r.dgz_sem, s, ea_peer[s])
        got(r.rg_back.at[source[s]], r.rgz_sem, s, ea_peer[s])

    drouter = jnp.zeros((sz.ep, qt), F32)
    for expert in range(sz.experts):
        level = mm(r.dg_back[expert][:, 0:cs], slots_of(expert, 0), NN, EXACT)
        drouter = drouter + jnp.where(iota((sz.ep, 1), 0) == expert, level[0:1], 0.0)
    router = r.probs[...]
    dlogits = (router * (drouter - jnp.sum(router * drouter, axis=0, keepdims=True))).astype(BF16)
    into_two = mm(back, r.rg_back[...].reshape(sz.experts * cs, d)) + mm(dlogits, router_w, TN)
    _, hat_two, inv_two = layer_norm(r.hidden[...], flat_row(r.gain2), flat_row(r.bias2))
    dhidden = r.dy_mine[...].astype(F32) + norm_back(into_two, hat_two, inv_two, flat_row(r.gain2))
    r.dhidden[...] = dhidden
    dattn = dhidden.astype(BF16)
    r.da_all[j] = dattn
    for p in partners:
        go(r.da_all.at[j], r.da_all.at[j], r.da_sem, p, ta_peer[p])
    router_grad = mm(dlogits, r.b_low[...])
    rows_at = iota((sz.early, 1), 0)
    early = jnp.where(rows_at < sz.experts, fit(router_grad, sz.early), 0.0)
    for offset, values in enumerate((into_two * hat_two, into_two, dattn.astype(F32))):
        total = jnp.sum(values, axis=0, keepdims=True)
        early = early + jnp.where(rows_at == sz.experts + offset, total, 0.0)

    def small_start(values, by_ta, sem):
        by_ta[j] = values
        for p in partners:
            go(by_ta.at[j], by_ta.at[j], sem, (0, p), ta_peer[p])

    def small_middle(by_ta, by_dev, sem, own_rows):
        for p in partners:
            got(by_ta.at[quarter[p]], sem, (0, p), ta_peer[p])
        total = by_ta[0]
        for q in range(1, nq):
            total = total + by_ta[q]
        if own_rows:
            total = jnp.where(iota((8, 1), 0) < 2, total, by_ta[j])
        by_dev[c] = total
        go(by_dev.at[c], by_dev.at[c], sem, (1, 0), other)

    def small_last(by_dev, by_ea, sem):
        got(by_dev.at[1 - c], sem, (1, 0), other)
        by_ea[z] = by_dev[0] + by_dev[1]
        for s in later:
            go(by_ea.at[z], by_ea.at[z], sem, (2, s), ea_peer[s])

    def small_end(by_ea, out, sem):
        for s in later:
            got(by_ea.at[source[s]], sem, (2, s), ea_peer[s])
        total = by_ea[0]
        for e in range(1, ea):
            total = total + by_ea[e]
        out[...] = total

    if sz.direct:
        small_start(early, r.early_ta, r.early_sem)
    else:
        r.o_early[...] = early

    for p in partners:
        got(r.da_all.at[quarter[p]], r.da_sem, p, ta_peer[p])
    for p in (1, 2):
        share_joined(r.rows_all, r.eo_in, r.eo_relay, r.eo_sem, p)
    if sz.direct:
        small_middle(r.early_ta, r.early_dev, r.early_sem, False)

    unpick = onehot(iota((sz.tp, nq * qt), 1) == r.perm_col[:, 0:1].astype(jnp.int32)).astype(BF16)
    dattn = mm(unpick, r.da_all[...].reshape(nq * qt, d)).astype(BF16)
    w_out = r.w_out[...].reshape(sz.inner, d)
    dmixed = mm(dattn, w_out, NT).astype(BF16).reshape(flat)

    def piece_start(n, values):
        half = values.reshape(2, sz.half, d)
        r.pd_send[n] = half.astype(BF16)
        go(r.pd_send.at[n, 1 - c], r.pd_in.at[n], r.pd_sem, n, other)

    def piece_middle(n):
        got(r.pd_in.at[n], r.pd_sem, n, other)
        both = r.pd_send[n, c].astype(F32) + r.pd_in[n].astype(F32)
        for e in range(ea):
            r.pz_send[n, e] = both[e * sz.piece : (e + 1) * sz.piece].astype(BF16)
        for s in later:
            t = target[s]
            go(r.pz_send.at[n, t], r.pz_in.at[n, z], r.pz_sem, (n, s), ea_peer[s])
        r.pz_in[n, z] = r.pz_send[n, z]

    def piece_last(n):
        for s in later:
            got(r.pz_in.at[n, source[s]], r.pz_sem, (n, s), ea_peer[s])
        total = r.pz_in[n, 0].astype(F32)
        for e in range(1, ea):
            total = total + r.pz_in[n, e].astype(F32)
        r.p_all[n, c, z] = total.astype(BF16)
        for s in later:
            block = r.p_all.at[n, c, z]
            go(block, block, r.pa_sem, (n, s), ea_peer[s])
        go(r.p_all.at[n, c, z], r.p_all.at[n, c, z], r.pb_sem, (n, 0), other)

    def piece_pass(n):
        for s in later:
            block = r.p_all.at[n, c, source[s]]
            got(block, r.pa_sem, (n, s), ea_peer[s])
            go(block, block, r.pb_sem, (n, s), other)

    def piece_end(n):
        for s in range(ea):
            got(r.p_all.at[n, 1 - c, source[s]], r.pb_sem, (n, s), other)

    if not sz.direct:

        def piece_start(n, values):
            r.o_piece[n] = values

        piece_middle = piece_last = piece_pass = piece_end = lambda n: None

    keeps = []
    for n, own, taken, out in ((0, r.up_low, r.up_in, r.o_up), (1, r.down_low, r.down_in, r.o_down)):
        got(taken, r.rep_sem, n, other)
        taken[...] = (own[...].astype(F32) + taken[...].astype(F32)).astype(BF16)
        keeps.append(pltpu.make_async_copy(taken, out, r.load_sem.at[n]))
        keeps[-1].start()
    got(r.bias_in, r.rep_sem, 2, other)
    r.o_bias[...] = r.bias_acc[...] + r.bias_in[...]
    piece_start(0, mm(r.mixed[...].reshape(sz.tp, sz.inner), dattn, TN))
    if sz.direct:
        small_last(r.early_dev, r.early_ea, r.early_sem)

    def attention_back(image):
        queries, keys, values, dmix = r.q[image], r.k[image], r.v[image], dmixed[image]
        dquery = jnp.zeros((sz.lp, sz.inner), F32)
        dkey, dvalue = dquery, dquery
        for head in range(sz.heads):
            mask_low, mask = head_mask(sz, head, BF16), head_mask(sz, head, F32)
            scores = mm(queries * mask_low, keys, NT) * scale
            probs = jnp.where(live, jnp.exp(scores - r.lse[image][:, head : head + 1]), 0.0)
            dprobs = mm(dmix * mask_low, values, NT)
            dvalue = dvalue + mm(probs.astype(BF16), dmix, TN) * mask
            inner = jnp.sum(probs * dprobs, axis=-1, keepdims=True)
            dscores = (probs * (dprobs - inner)).astype(BF16)
            dquery = dquery + mm(dscores, keys) * (mask * scale)
            dkey = dkey + mm(dscores, queries, TN) * (mask * scale)
        for n, values in enumerate((dquery, dkey, dvalue)):
            r.dproj[n, image] = values.astype(BF16)

    attention_back(0)
    piece_middle(0)
    for image in range(1, sz.images):
        attention_back(image)
    for copy in home_copies:
        copy.wait_send()
    finished += home_copies
    for s in later + [0]:
        g = target[s]
        share = share_sum(r.rows_all, r.eo_in, r.eo_sem, s)
        if s:
            r.rgz_send[g] = share.astype(BF16)
            go(r.rgz_send.at[g], r.eo_back.at[z], r.eoz_sem, s, ea_peer[s])
        else:
            r.eo_back[z] = share.astype(BF16)

    dproj = [r.dproj[n].reshape(sz.tp, sz.inner) for n in range(3)]
    for n in (2, 0, 1):
        piece_start(n + 1, mm(dproj[n], r.a_low[...], TN))
    piece_last(0)
    into_part = mm(dproj[0], r.qkv_w[0]) + mm(dproj[1], r.qkv_w[1]) + mm(dproj[2], r.qkv_w[2])
    r.in_send[...] = mm(pick_all, into_part.astype(BF16)).astype(BF16).reshape(nq, qt, d)
    for p in partners:
        go(r.in_send.at[quarter[p]], r.in_part.at[j], r.ip_sem, p, ta_peer[p])
    r.in_part[j] = r.in_send[j]
    _, hat_one, _ = layer_norm(r.padded[...].reshape(sz.tp, d).astype(F32), flat_row(r.gain1), flat_row(r.bias1))
    rows_at = iota((8, 1), 0)
    late = jnp.where(rows_at == 0, jnp.sum(into_part * hat_one, axis=0, keepdims=True), 0.0)
    late = late + jnp.where(rows_at == 1, jnp.sum(into_part, axis=0, keepdims=True), 0.0)
    for row, n in ((2, 0), (3, 2)):
        total = jnp.sum(dproj[n].astype(F32), axis=0, keepdims=True)
        wide = jnp.concatenate([total, jnp.zeros((1, d - sz.inner), F32)], axis=1)
        late = late + jnp.where(rows_at == row, wide, 0.0)
    if sz.direct:
        small_start(late, r.late_ta, r.late_sem)
    else:
        r.o_late[...] = late
    for n in (3, 1, 2):
        piece_middle(n)
    if sz.direct:
        small_middle(r.late_ta, r.late_dev, r.late_sem, True)

    for p in partners:
        got(r.in_part.at[quarter[p]], r.ip_sem, p, ta_peer[p])
    into_one = r.in_part[0].astype(F32)
    for q in range(1, nq):
        into_one = into_one + r.in_part[q].astype(F32)
    x_mine = mm(pick_of(j), r.padded[...].reshape(sz.tp, d))
    _, hat_mine, inv_mine = layer_norm(x_mine, flat_row(r.gain1), flat_row(r.bias1))
    grad = r.dhidden[...] + norm_back(into_one, hat_mine, inv_mine, flat_row(r.gain1))
    r.ig_all[j] = grad.astype(BF16)
    for p in partners:
        go(r.ig_all.at[j], r.ig_all.at[j], r.ig_sem, p, ta_peer[p])
    if sz.direct:
        small_last(r.late_dev, r.late_ea, r.late_sem)

    for s in later:
        got(r.eo_back.at[source[s]], r.eoz_sem, s, ea_peer[s])
    output = r.hidden[...] + mm(back, r.eo_back[...].reshape(sz.experts * cs, d))
    r.out_all[j] = output.astype(BF16)
    for p in partners:
        go(r.out_all.at[j], r.out_all.at[j], r.out_sem, p, ta_peer[p])
    for n in (3, 1, 2):
        piece_last(n)
    for n in (0, 3, 1, 2):
        piece_pass(n)
    stores = []

    def store(n, values, src, dst):
        src[...] = values.reshape(src.shape)
        stores.append(pltpu.make_async_copy(src, dst, r.load_sem.at[n]))
        stores[-1].start()

    for p in partners:
        got(r.ig_all.at[quarter[p]], r.ig_sem, p, ta_peer[p])
    store(2, mm(unpick, r.ig_all[...].reshape(nq * qt, d)).astype(BF16), r.a_low, r.o_in)
    for p in partners:
        got(r.out_all.at[quarter[p]], r.out_sem, p, ta_peer[p])
    store(3, mm(unpick, r.out_all[...].reshape(nq * qt, d)).astype(BF16), r.padded, r.o_out)
    if sz.direct:
        small_end(r.early_ea, r.o_early, r.early_sem)
        small_end(r.late_ea, r.o_late, r.late_sem)
    for n in (0, 3, 1, 2):
        piece_end(n)
    for copy in stores + keeps:
        copy.wait()
    for copy in started:
        if not any(copy is done for done in finished):
            copy.wait_send()


def flat_row(ref):
    return ref[...].reshape(1, -1)


def fit(values, rows):
    have = values.shape[0]
    if have >= rows:
        return values[:rows]
    return jnp.concatenate([values, jnp.zeros((rows - have, values.shape[1]), F32)])


def run_block(sz, inputs):
    nq, ea, d, cs, qt = sz.nq, sz.ea, sz.d, sz.cs, sz.qt
    dma = pltpu.SemaphoreType.DMA
    rows = sz.blocks * cs
    outs = dict(
        o_out=((sz.images, sz.lp, d), BF16),
        o_in=((sz.tp, d), BF16),
        o_early=((sz.early, d), F32),
        o_late=((8, d), F32),
        o_up=((d, sz.hidden), BF16),
        o_down=((sz.hidden, d), BF16),
        o_bias=((8, d), F32),
    )
    flat = (sz.images, sz.lp, sz.inner)
    block = (cs, d)
    buffers = dict(
        tok_v=((sz.images, sz.length, d), BF16),
        cot_v=((sz.images, sz.length, d), BF16),
        qkv_w=((3, sz.inner, d), BF16),
        up_w=((d, sz.hidden), BF16),
        down_w=((sz.hidden, d), BF16),
        w_full=((nq, 2, sz.half, d), BF16),
        padded=((sz.images, sz.lp, d), BF16),
        perm_col=((sz.tp, 128), F32),
        place_row=((4, qt), jnp.int32),
        place_col=((qt, 128), jnp.int32),
        a_low=((sz.tp, d), BF16),
        q=(flat, BF16),
        k=(flat, BF16),
        v=(flat, BF16),
        mixed=(flat, BF16),
        lse=((sz.images, sz.lp, 128), F32),
        dproj=((3,) + flat, BF16),
        mix_send=((nq, qt, sz.inner), BF16),
        mix_in=((2, nq, qt, sz.inner), BF16),
        dy_mine=((qt, d), BF16),
        hidden=((qt, d), F32),
        dhidden=((qt, d), F32),
        b_low=((qt, d), BF16),
        probs=((sz.ep, qt), F32),
        dy_send=((2, ea) + block, BF16),
        gate_send=((2, ea, 8, 128), F32),
        dy_all=((nq, ea) + block, BF16),
        rows_all=((nq, ea) + block, BF16),
        gate_all=((nq, ea, 8, 128), F32),
        act_t=((sz.kept, rows, sz.hidden), BF16),
        pre_t=((sz.kept, rows, sz.hidden), BF16),
        slot_t=((sz.kept, rows, d), BF16),
        out_t=((sz.kept, rows, d), BF16),
        dg_send=((nq, ea, 8, 128), F32),
        dg_in=((nq, ea, 8, 128), F32),
        rg_in=((2, ea) + block, BF16),
        rg_relay=((2, ea, cs // 2, d), BF16),
        eo_in=((2, ea) + block, BF16),
        eo_relay=((2, ea, cs // 2, d), BF16),
        rgz_send=((ea,) + block, BF16),
        dgz_send=((ea, 8, 128), F32),
        rg_back=((ea,) + block, BF16),
        eo_back=((ea,) + block, BF16),
        dg_back=((ea, 8, 128), F32),
        up_acc=((d, sz.hidden), F32),
        down_acc=((sz.hidden, d), F32),
        bias_acc=((8, d), F32),
        up_low=((d, sz.hidden), BF16),
        down_low=((sz.hidden, d), BF16),
        up_in=((d, sz.hidden), BF16),
        down_in=((sz.hidden, d), BF16),
        bias_in=((8, d), F32),
        da_all=((nq, qt, d), BF16),
        ig_all=((nq, qt, d), BF16),
        out_all=((nq, qt, d), BF16),
        in_send=((nq, qt, d), BF16),
        in_part=((nq, qt, d), BF16),
    )
    sems = dict(
        w_sem=(nq,),
        wd_sem=(nq,),
        dyz_sem=(2, ea),
        dyt_sem=(nq, ea),
        mix_sem=(2, nq),
        gatez_sem=(2, ea),
        rowz_sem=(2, ea),
        rowt_sem=(nq, ea),
        rowr_sem=(3, ea),
        gatet_sem=(nq,),
        dg_sem=(nq,),
        rg_sem=(6, ea),
        rep_sem=(3,),
        dgz_sem=(ea,),
        rgz_sem=(ea,),
        eo_sem=(6, ea),
        eoz_sem=(ea,),
        da_sem=(nq,),
        early_sem=(3, max(nq, ea)),
        late_sem=(3, max(nq, ea)),
        pd_sem=(4,),
        pz_sem=(4, ea),
        pa_sem=(4, ea),
        pb_sem=(4, ea),
        ip_sem=(nq,),
        ig_sem=(nq,),
        out_sem=(nq,),
    )
    if sz.direct:
        outs["p_all"] = ((4, 2, ea, sz.piece, d), BF16)
        buffers |= dict(
            early_ta=((nq, sz.early, d), F32),
            early_dev=((2, sz.early, d), F32),
            early_ea=((ea, sz.early, d), F32),
            late_ta=((nq, 8, d), F32),
            late_dev=((2, 8, d), F32),
            late_ea=((ea, 8, d), F32),
            pd_send=((4, 2, sz.half, d), BF16),
            pd_in=((4, sz.half, d), BF16),
            pz_send=((4, ea, sz.piece, d), BF16),
            pz_in=((4, ea, sz.piece, d), BF16),
        )
    else:
        outs["o_piece"] = ((4, sz.inner, d), F32)
    if sz.direct:
        buffers["row_send"] = ((2, ea) + block, BF16)
    names = list(inputs) + list(outs) + list(buffers) + list(sems) + ["load_sem"]
    vm = pl.BlockSpec(memory_space=pltpu.VMEM)
    far = pl.BlockSpec(memory_space=pltpu.HBM)
    results = pl.pallas_call(
        functools.partial(block_kernel, sz, names),
        out_shape=[jax.ShapeDtypeStruct(*spec) for spec in outs.values()],
        in_specs=[far if name in ("tok", "cot", "w_qkv", "w_up", "w_down") else vm for name in inputs],
        out_specs=[far if name in ("o_up", "o_down", "o_in", "o_out") else vm for name in outs],
        scratch_shapes=[pltpu.VMEM(*spec) for spec in buffers.values()]
        + [dma((2,) + shape) for shape in sems.values()]
        + [dma((8,))],
        name="block",
        compiler_params=pltpu.CompilerParams(
            collective_id=0, has_side_effects=True, vmem_limit_bytes=60 << 20
        ),
    )(*inputs.values())
    return dict(zip(outs, results))


def finish_kernel(sz, names, *refs):
    r = types.SimpleNamespace(**dict(zip(names, refs)))
    n, d = sz.experts, sz.d
    loads, stores = [], []

    def load(src, dst):
        loads.append(pltpu.make_async_copy(src, dst, r.sem_in.at[len(loads)]))
        loads[-1].start()

    def store(src, dst):
        stores.append(pltpu.make_async_copy(src, dst, r.sem_out.at[len(stores)]))
        stores[-1].start()

    third = d // 3
    spans = [pl.ds(k * third, third) for k in range(3)]
    for src, dst in ((r.up, r.up_v), (r.down, r.down_v)):
        for span in spans:
            load(src.at[span], dst.at[span])
    load(r.grad, r.grad_v)
    load(r.out, r.out_v)
    load(r.piece, r.piece_v)
    for dst, src in (
        (r.f_b, r.early[n + 2 : n + 3]),
        (r.f_g1, r.late[0:1]),
        (r.f_c1, r.late[1:2]),
        (r.f_g2, r.early[n : n + 1]),
        (r.f_c2, r.early[n + 1 : n + 2]),
    ):
        dst[...] = src.reshape(d)
    r.f_router[...] = r.early[0:n]
    r.f_qv[...] = r.late[2:4, 0 : sz.inner]
    r.f_upb[...] = r.bias[0:1]
    r.f_downb[...] = r.bias[1:2]
    at = 0
    for src, wide, dst in ((r.up_v, r.up_w, r.f_up), (r.down_v, r.down_w, r.f_down)):
        for span in spans:
            loads[at].wait()
            at += 1
            wide[span] = src[span].astype(F32)
            store(wide.at[span], dst.at[span])
    loads[at].wait()
    for image in range(sz.images):
        r.grad_w[:, image, :] = r.grad_v[image * sz.lp : image * sz.lp + sz.length].astype(F32)
    store(r.grad_w, r.f_grad)
    loads[at + 1].wait()
    for image in range(sz.images):
        r.out_w[:, image, :] = r.out_v[image, 0 : sz.length]
    store(r.out_w, r.f_out)
    loads[at + 2].wait()
    for k in range(4):
        for core in range(2):
            for e in range(sz.ea):
                start = core * sz.half + e * sz.piece
                r.piece_w[k, start : start + sz.piece] = r.piece_v[k, core, e].astype(F32)
        store(r.piece_w.at[k], r.f_qkv.at[k - 1] if k else r.f_o)
    for copy in stores:
        copy.wait()


def finish(sz, got):
    d, n = sz.d, sz.experts
    inputs = dict(
        up=got["o_up"],
        down=got["o_down"],
        out=got["o_out"],
        grad=got["o_in"],
        piece=got["p_all"],
        early=got["o_early"],
        late=got["o_late"],
        bias=got["o_bias"],
    )
    outs = dict(
        f_out=((sz.length, sz.images, d), BF16),
        f_grad=((sz.length, sz.images, d), F32),
        f_qkv=((3, sz.inner, d), F32),
        f_qv=((2, sz.inner), F32),
        f_o=((sz.inner, d), F32),
        f_b=((d,), F32),
        f_g1=((d,), F32),
        f_c1=((d,), F32),
        f_g2=((d,), F32),
        f_c2=((d,), F32),
        f_router=((n, d), F32),
        f_up=((d, sz.hidden), F32),
        f_upb=((1, sz.hidden), F32),
        f_down=((sz.hidden, d), F32),
        f_downb=((1, d), F32),
    )
    buffers = dict(
        up_v=((d, sz.hidden), BF16),
        down_v=((sz.hidden, d), BF16),
        grad_v=((sz.tp, d), BF16),
        out_v=((sz.images, sz.lp, d), BF16),
        piece_v=((4, 2, sz.ea, sz.piece, d), BF16),
        up_w=((d, sz.hidden), F32),
        down_w=((sz.hidden, d), F32),
        grad_w=((sz.length, sz.images, d), F32),
        out_w=((sz.length, sz.images, d), BF16),
        piece_w=((4, sz.inner, d), F32),
    )
    vm = pl.BlockSpec(memory_space=pltpu.VMEM)
    far = pl.BlockSpec(memory_space=pltpu.HBM)
    large = ("up", "down", "out", "grad", "piece", "f_out", "f_grad", "f_qkv", "f_o", "f_up", "f_down")
    names = list(inputs) + list(outs) + list(buffers) + ["sem_in", "sem_out"]
    results = pl.pallas_call(
        functools.partial(finish_kernel, sz, names),
        out_shape=[jax.ShapeDtypeStruct(*spec) for spec in outs.values()],
        in_specs=[far if name in large else vm for name in inputs],
        out_specs=[far if name in large else vm for name in outs],
        scratch_shapes=[pltpu.VMEM(*spec) for spec in buffers.values()]
        + [pltpu.SemaphoreType.DMA((16,)), pltpu.SemaphoreType.DMA((16,))],
        name="finish",
        compiler_params=pltpu.CompilerParams(vmem_limit_bytes=60 << 20),
    )(*inputs.values())
    (out, grad, qkv, qv, o, b, g1, c1, g2, c2, router, up, up_b, down, down_b) = results
    turn = lambda t: jnp.swapaxes(t, 0, 1)
    return (
        turn(out),
        turn(grad),
        jnp.swapaxes(qkv, 1, 2),
        qv,
        o,
        b,
        g1,
        c1,
        g2,
        c2,
        router.T,
        up[None],
        up_b,
        down[None],
        down_b,
    )


def local(
    tokens,
    expert_ids,
    pair_ranks,
    cotangent,
    w_qkv,
    b_qv,
    w_out,
    b_out,
    ln1_gain,
    ln1_bias,
    ln2_gain,
    ln2_bias,
    w_router,
    w_up,
    b_up,
    w_down,
    b_down,
):
    sz = Sizes(tokens, expert_ids, w_qkv, w_up)
    pairs = jnp.stack([jnp.transpose(t, (2, 0, 1)) for t in (expert_ids, pair_ranks)])
    pairs = jnp.pad(
        pairs, ((0, 0), (0, 0), (0, 0), (0, sz.lp - sz.length)), constant_values=sz.tokens * 2
    )
    table = jnp.pad(pairs.reshape(4, sz.tp).astype(F32), ((0, 4), (0, ceil_to(sz.tp, 128) - sz.tp)))
    inputs = dict(
        tok=tokens,
        cot=cotangent,
        w_qkv=jnp.swapaxes(w_qkv, 1, 2),
        b_qv=b_qv,
        w_out=w_out.reshape(2, sz.half, sz.d),
        b_out=b_out,
        gain1=ln1_gain,
        bias1=ln1_bias,
        gain2=ln2_gain,
        bias2=ln2_bias,
        router=w_router.T,
        w_up=w_up[0],
        b_up=b_up,
        w_down=w_down[0],
        b_down=b_down,
        table=table,
    )
    got = run_block(sz, inputs)
    if sz.direct:
        return finish(sz, got)
    n = sz.experts
    piece, shared = lax.psum((got["o_piece"], got["o_late"][2:4]), ("ea", "dev"))
    early, late = lax.psum((got["o_early"], got["o_late"][:2]), ("ea", "ta", "dev"))
    return (
        got["o_out"][:, : sz.length],
        got["o_in"].reshape(got["o_out"].shape)[:, : sz.length].astype(F32),
        jnp.swapaxes(piece[1:], 1, 2),
        shared[:, : sz.inner],
        piece[0],
        early[n + 2],
        late[0],
        late[1],
        early[n],
        early[n + 1],
        early[:n].T,
        got["o_up"].astype(F32)[None],
        got["o_bias"][0:1],
        got["o_down"].astype(F32)[None],
        got["o_bias"][1:2],
    )


def solution(mesh):
    in_specs = (
        P(("ea", "dev"), None, None),
        P(("ea", "dev"), None, None),
        P(("ea", "dev"), None, None),
        P(("ea", "dev"), None, None),
        P(None, None, "ta"),
        P(None, "ta"),
        P("ta", None),
        P(),
        P(),
        P(),
        P(),
        P(),
        P(),
        P("ea", None, "ta"),
        P("ea", "ta"),
        P("ea", "ta", None),
        P("ea", None),
    )
    out_specs = (
        P(("ea", "dev"), None, None),
        P(("ea", "dev"), None, None),
        P(None, None, "ta"),
        P(None, "ta"),
        P("ta", None),
        P(),
        P(),
        P(),
        P(),
        P(),
        P(),
        P("ea", None, "ta"),
        P("ea", "ta"),
        P("ea", "ta", None),
        P("ea", None),
    )
    return jax.shard_map(local, mesh=mesh, in_specs=in_specs, out_specs=out_specs, check_vma=False)
```

```python
import functools
import types

import jax
import jax.numpy as jnp
from jax import lax
from jax.experimental import pallas as pl
from jax.experimental.pallas import tpu as pltpu
from jax.sharding import PartitionSpec as P

HDIM = 64
EPSILON = 1e-06
F32, BF16 = jnp.float32, jnp.bfloat16
EXACT = lax.Precision.HIGHEST
MESH = pl.DeviceIdType.MESH
NT = (((1,), (1,)), ((), ()))
TN = (((0,), (0,)), ((), ()))
NN = (((1,), (0,)), ((), ()))


def ceil_to(value, unit):
    return -(-value // unit) * unit


def mm(a, b, dims=NN, precision=None):
    return lax.dot_general(a, b, dims, precision=precision, preferred_element_type=F32)


def iota(shape, dim):
    return lax.broadcasted_iota(jnp.int32, shape, dim)


def onehot(mask):
    return jnp.where(mask, 1.0, 0.0).astype(F32)


class Sizes:
    def __init__(self, tokens, expert_ids, w_qkv, w_up):
        self.images, self.length, self.d = tokens.shape
        self.top = expert_ids.shape[2]
        self.tokens = self.images * self.length
        self.ea = lax.axis_size("ea")
        self.nq = lax.axis_size("ta")
        assert w_up.shape[0] == 1
        self.experts = self.ea
        self.cap = (9 * self.tokens * self.top + 8 * self.experts - 1) // (8 * self.experts)
        self.inner = w_qkv.shape[2]
        self.heads = self.inner // HDIM
        self.hidden = w_up.shape[2]
        self.lp = ceil_to(self.length, 16)
        self.tp = self.images * self.lp
        per_quarter = -(-self.tokens // self.nq)
        self.qt = ceil_to(per_quarter, 16)
        spread = (self.cap + (self.nq - 1) * self.experts) // self.nq
        self.cs = ceil_to(min(self.cap, per_quarter, spread), 16)
        self.ep = ceil_to(self.experts, 16)
        self.half = self.inner // 2
        self.piece = self.half // self.ea
        self.early = ceil_to(self.experts + 3, 8)
        self.blocks = max(1, min(self.ea, (256 if self.ea <= 8 else 64) // self.cs))
        self.chunks = self.ea // self.blocks
        self.direct = self.ea <= 8
        self.relay = [s for s in range(1, self.ea) if self.direct and s >= 2]
        self.dy_relay = [s for s in self.relay if s == 2]
        self.kept = self.nq if self.chunks == 1 else 1
        self.pool = 40
        self.arrivals = 145 if self.direct else 48 + 13 * self.ea
        assert self.top == 2 and self.nq == 4 and self.experts * self.nq <= 128


def route(sz, table):
    cols = table.T[: sz.tp]
    wide = iota((sz.tp, 128), 1)
    lane = wide.astype(F32)

    def flip(*columns):
        spread = jnp.zeros((sz.tp, 128), F32)
        for n, column in enumerate(columns):
            spread = spread + jnp.where(wide == n, column, 0.0)
        turned = spread.T
        return [turned[n : n + 1] for n in range(len(columns))]

    def total(values):
        return jnp.sum(values, axis=1, keepdims=True)

    ids = [cols[:, k : k + 1] for k in range(2)]
    real = ids[0] < sz.experts
    member = [onehot(lane == column) for column in ids]
    dest = []
    for k in range(2):
        before = jnp.zeros((sz.tp, 128), F32)
        for m in range(2):
            mask = onehot(table[2 + m : 3 + m, : sz.tp] < cols[:, 2 + k : 3 + k])
            before = before + mm(mask.astype(BF16), member[m].astype(BF16))
        kept = (total(before * member[k]) < sz.cap) & real
        dest.append(jnp.where(kept, ids[k], float(sz.experts)))
    low, high = jnp.minimum(*dest), jnp.maximum(*dest)
    index = iota((sz.tp, 1), 0).astype(F32)
    kind = jnp.where(real, low * (sz.experts + 1) + high, float((sz.experts + 1) ** 2))
    key = kind * sz.tp + index
    (key_row,) = flip(key)
    earlier = onehot(key_row < key).astype(BF16)
    order = mm(earlier, jnp.ones((sz.tp, 128), BF16))[:, 0:1]
    lap = jnp.floor((order + 0.5) * (1.0 / sz.nq))
    quarter = order - lap * sz.nq
    perm = jnp.where(real, quarter * sz.qt + lap, -1.0)
    group = [
        onehot((lane == d * sz.nq + quarter) & (d < sz.experts)) for d in dest
    ]
    ahead = mm(earlier, (group[0] + group[1]).astype(BF16))
    place = []
    for k in range(2):
        slot = total(ahead * group[k])
        place.append(jnp.where(dest[k] < sz.experts, dest[k] * sz.cs + slot + 1.0, 0.0))
    perm_row, *place_row = flip(perm, *place)
    return perm, perm_row, place, place_row


def layer_norm(values, gain_vec, shift_vec):
    row_mean = jnp.mean(values, axis=-1, keepdims=True)
    centered = values - row_mean
    variance = jnp.mean(centered * centered, axis=-1, keepdims=True)
    inverse = lax.rsqrt(variance + EPSILON)
    normed = centered * inverse
    return (normed * gain_vec + shift_vec, normed, inverse)


def norm_back(grad_rows, normed, inverse, gain_vec):
    scaled = grad_rows * gain_vec
    return inverse * (
        scaled
        - jnp.mean(scaled, axis=-1, keepdims=True)
        - normed * jnp.mean(scaled * normed, axis=-1, keepdims=True)
    )


def push(src, dst, send_sem, recv_sem, device):
    return pltpu.make_async_remote_copy(
        src_ref=src,
        dst_ref=dst,
        send_sem=send_sem,
        recv_sem=recv_sem,
        device_id=device,
        device_id_type=MESH,
    )


def greet(devices):
    barrier = pltpu.get_barrier_semaphore()
    for device in devices:
        pl.semaphore_signal(barrier, inc=1, device_id=device, device_id_type=MESH)


def head_mask(sz, head, dtype):
    lane = iota((1, sz.inner), 1)
    return onehot((lane >= head * HDIM) & (lane < (head + 1) * HDIM)).astype(dtype)


def gelu_parts(values):
    cdf = 0.5 * (1.0 + lax.erf(values * (0.5**0.5)))
    density = jnp.exp(-0.5 * values * values) * (0.5 / jnp.pi) ** 0.5
    return cdf, density


class Sent:
    def __init__(self, copy):
        self.copy, self.done = copy, False

    def wait_send(self):
        if not self.done:
            self.copy.wait_send()
        self.done = True


class Refs(types.SimpleNamespace):
    def __getattr__(self, name):
        return name


def block_kernel(sz, names, *refs):
    r = Refs(**dict(zip(names, refs)))
    z, j, c = lax.axis_index("ea"), lax.axis_index("ta"), lax.axis_index("dev")
    nq, ea, d, cs, qt = sz.nq, sz.ea, sz.d, sz.cs, sz.qt
    quarter = [j, j + 1 - 2 * lax.rem(j, 2), j + 2 - 4 * lax.div(j, 2), 3 - j]
    ta_peer = [{"ta": q} for q in quarter]
    ea_peer = [{"ea": lax.rem(z + s, ea)} for s in range(ea)]
    source = [lax.rem(z - s + ea, ea) for s in range(ea)]
    target = [lax.rem(z + s, ea) for s in range(ea)]
    other = {"dev": 1 - c}
    later = [s for s in range(1, ea)]
    partners = (1, 2, 3)
    pool, started, receive = sz.pool, [], {}

    def go(src, dst, kind, index, device):
        at = receive.setdefault((kind, index), len(receive))
        n = len(started)
        if n >= pool:
            started[n - pool].wait_send()
        copy = push(src, dst, r.sent.at[n % pool], r.arrived.at[at], device)
        copy.start()
        started.append(Sent(copy))
        return started[-1]

    def got(dst, kind, index, device):
        at = receive.setdefault((kind, index), len(receive))
        push(dst, dst, r.sent.at[0], r.arrived.at[at], device).wait_recv()

    everyone = ta_peer[1:] + ea_peer[1:] + [other]
    greet(everyone)
    loads = []
    for n, (src, dst) in enumerate(
        ((r.cot, r.cot_v), (r.tok, r.tok_v), (r.w_qkv, r.qkv_w), (r.w_up, r.up_w), (r.w_down, r.down_w))
    ):
        loads.append(pltpu.make_async_copy(src, dst, r.load_sem.at[n]))
        loads[-1].start()
    pl.semaphore_wait(pltpu.get_barrier_semaphore(), len(everyone))

    for p in partners:
        go(r.w_out.at[c], r.w_full.at[j, c], r.w_sem, p, ta_peer[p])
    r.w_full[j] = r.w_out[...]

    perm_col, perm, place, place_rows = route(sz, r.table[...])
    perm = perm.astype(jnp.int32)
    r.perm_col[...] = jnp.broadcast_to(perm_col, (sz.tp, 128))
    pick_all = onehot(iota((nq * qt, sz.tp), 0) == perm).astype(BF16)

    def pick_of(q):
        return onehot(iota((qt, sz.tp), 0) + q * qt == perm).astype(BF16)

    spread = iota((8, 1), 0)
    both = jnp.where(spread == 0, place_rows[0], 0.0) + jnp.where(spread == 1, place_rows[1], 0.0)
    for which, q in ((0, quarter[0]), (1, quarter[3])):
        chosen = mm(both, onehot(iota((qt, sz.tp), 0) + q * qt == perm), NT, EXACT)
        r.place_row[2 * which : 2 * which + 2] = (chosen[0:2] + 0.5).astype(jnp.int32) - 1
    pair_col = jnp.where(iota((1, 128), 1) == 0, place[0], 0.0)
    pair_col = pair_col + jnp.where(iota((1, 128), 1) == 1, place[1], 0.0)
    chosen = mm(onehot(iota((qt, sz.tp), 0) + j * qt == perm), pair_col, NN, EXACT)
    r.place_col[...] = (chosen + 0.5).astype(jnp.int32) - 1

    def slots_of(expert, which):
        row = iota((cs, qt), 0) + expert * cs
        first, second = r.place_row[2 * which : 2 * which + 1], r.place_row[2 * which + 1 : 2 * which + 2]
        return onehot((row == first) | (row == second))

    tail = (sz.length // 16) * 16
    loads[0].wait()
    for image in range(sz.images):
        r.padded[image, tail:] = jnp.zeros((sz.lp - tail, d), BF16)
        r.padded[image, 0 : sz.length] = r.cot_v[image]
    for which, q in ((0, quarter[0]), (1, quarter[3])):
        dy_rows = mm(pick_of(q), r.padded[...].reshape(sz.tp, d)).astype(BF16)
        if which == 0:
            r.dy_mine[...] = dy_rows
        for expert in range(sz.experts):
            r.dy_send[which, expert] = mm(slots_of(expert, which).astype(BF16), dy_rows).astype(BF16)
    dy_copies = []
    near_first = later[:1] + later[2:] + later[1:2]

    def send_dy(which, q, planes):
        for s in planes:
            block = r.dy_send.at[which, target[s]]
            dy_copies.append(go(block, r.dy_all.at[q, z], r.dyz_sem, (which, s), ea_peer[s]))

    send_dy(0, quarter[0], near_first)
    for which, q in ((0, quarter[0]), (1, quarter[3])):
        r.dy_all[q, z] = r.dy_send[which, z]

    def forward(ref, z_sem, t_sem, order):
        copies = []
        for s in order:
            block = ref.at[j, source[s]]
            if s:
                got(block, z_sem, (0, s), ea_peer[s])
            for p in (1, 2):
                copies.append(go(block, block, t_sem, (p, s), ta_peer[p]))
        return copies

    dy_forwards = forward(r.dy_all, r.dyz_sem, r.dyt_sem, [0])

    low_half, high_half = pl.ds(0, cs // 2), pl.ds(cs // 2, cs // 2)

    def relay(ref, t_sem, sem, planes):
        copies = []
        for s in planes:
            for p, part in ((1, high_half), (2, low_half)):
                got(ref.at[quarter[p], source[s]], t_sem, (p, s), ta_peer[p])
                half = ref.at[quarter[p], source[s], part]
                copies.append(go(half, half, sem, (3 - p, s), ta_peer[3 - p]))
        return copies

    loads[1].wait()
    loads[2].wait()
    for image in range(sz.images):
        r.padded[image, 0 : sz.length] = r.tok_v[image]
    normed_one, _, _ = layer_norm(
        r.padded[...].reshape(sz.tp, d).astype(F32), flat_row(r.gain1), flat_row(r.bias1)
    )
    a_low = normed_one.astype(BF16)
    r.a_low[...] = a_low
    flat = (sz.images, sz.lp, sz.inner)
    r.q[...] = (mm(a_low, r.qkv_w[0], NT) + r.b_qv[0:1]).astype(BF16).reshape(flat)
    r.k[...] = mm(a_low, r.qkv_w[1], NT).astype(BF16).reshape(flat)
    r.v[...] = (mm(a_low, r.qkv_w[2], NT) + r.b_qv[1:2]).astype(BF16).reshape(flat)

    for p in partners:
        block = r.w_full.at[quarter[p], c]
        got(block, r.w_sem, p, ta_peer[p])
        go(block, block, r.wd_sem, p, other)

    scale = HDIM ** (-0.5)
    live = iota((1, sz.lp), 1) < sz.length

    def stack(values):
        return jnp.concatenate([values * head_mask(sz, h, BF16) for h in range(sz.heads)], axis=0)

    def unstack(values):
        return sum(
            values[h * sz.lp : (h + 1) * sz.lp] * head_mask(sz, h, F32) for h in range(sz.heads)
        )

    def attention_probs(image):
        scores = mm(stack(r.q[image]), r.k[image], NT) * scale
        scores = jnp.where(live, scores, -1e30)
        exps = jnp.exp(scores - jnp.max(scores, axis=-1, keepdims=True))
        return exps / jnp.sum(exps, axis=-1, keepdims=True)

    for image in range(sz.images):
        probs = attention_probs(image)
        if sz.direct:
            r.kept_probs[image] = probs
        r.mixed[image] = unstack(mm(probs.astype(BF16), r.v[image])).astype(BF16)
    dealt = mm(pick_all, r.mixed[...].reshape(sz.tp, sz.inner)).astype(BF16)
    r.mix_send[...] = dealt.reshape(nq, qt, sz.inner)
    for p in partners:
        go(r.mix_send.at[quarter[p]], r.mix_in.at[0, j], r.mix_sem, (0, p), ta_peer[p])
        go(r.mix_send.at[quarter[3 - p]], r.mix_in.at[1, j], r.mix_sem, (1, p), ta_peer[p])
    for copy in list(dy_copies):
        copy.wait_send()
    send_dy(1, quarter[3], [s for s in near_first if s not in sz.dy_relay])
    dy_forwards += forward(r.dy_all, r.dyz_sem, r.dyt_sem, near_first)
    r.mix_in[0, j] = r.mix_send[j]
    r.mix_in[1, j] = r.mix_send[quarter[3]]
    x_rows = [mm(pick_of(q), r.padded[...].reshape(sz.tp, d)) for q in (quarter[0], quarter[3])]
    for p in partners:
        got(r.w_full.at[quarter[p], 1 - c], r.wd_sem, p, other)
    for p in partners:
        got(r.mix_in.at[0, quarter[p]], r.mix_sem, (0, p), ta_peer[p])
        got(r.mix_in.at[1, quarter[p]], r.mix_sem, (1, p), ta_peer[p])

    if not sz.direct:
        r.row_send = r.dy_send
        for copy in dy_copies:
            copy.wait_send()
    router_w = r.router[...]
    if sz.ep > sz.experts:
        router_w = jnp.concatenate([router_w, jnp.zeros((sz.ep - sz.experts, d), BF16)])
    def send_rows(which, q, planes):
        return [
            go(r.row_send.at[which, target[s]], r.rows_all.at[q, z], r.rowz_sem, (which, s), ea_peer[s])
            for s in planes
        ]

    for which in (0, 1):
        attention = flat_row(r.b_out)
        for q in range(nq):
            attention = attention + mm(r.mix_in[which, q], r.w_full[q].reshape(sz.inner, d))
        hidden = x_rows[which] + attention
        normed_two, _, _ = layer_norm(hidden, flat_row(r.gain2), flat_row(r.bias2))
        b_low = normed_two.astype(BF16)
        logits = mm(router_w, b_low, NT)
        logits = jnp.where(iota((sz.ep, 1), 0) < sz.experts, logits, -1e30)
        exps = jnp.exp(logits - jnp.max(logits, axis=0, keepdims=True))
        router = exps / jnp.sum(exps, axis=0, keepdims=True)
        if which == 0:
            r.hidden[...], r.b_low[...], r.probs[...] = hidden, b_low, router
        for expert in range(sz.experts):
            slots = slots_of(expert, which)
            r.row_send[which, expert] = mm(slots.astype(BF16), b_low).astype(BF16)
            level = jnp.broadcast_to(router[expert : expert + 1], (8, qt))
            r.gate_send[expert, which, :, 0:cs] = mm(level, slots, NT, EXACT)
        q = quarter[3 * which]
        if which:
            for s in later:
                go(r.gate_send.at[target[s]], r.gate_in.at[z], r.gatez_sem, s, ea_peer[s])
            r.gate_in[z] = r.gate_send[z]
        if which == 0:
            row_copies = send_rows(0, q, near_first[:-1])
        r.rows_all[q, z] = r.row_send[which, z]
    row_forwards = forward(r.rows_all, r.rowz_sem, r.rowt_sem, [0])
    for copy in row_copies:
        copy.wait_send()
    row_copies = send_rows(0, quarter[0], near_first[-1:])
    row_forwards += forward(r.rows_all, r.rowz_sem, r.rowt_sem, near_first[:-1])
    for copy in row_copies:
        copy.wait_send()
    send_rows(1, quarter[3], [s for s in near_first if s not in sz.relay])
    row_forwards += forward(r.rows_all, r.rowz_sem, r.rowt_sem, near_first[-1:])
    for s in later:
        got(r.gate_in.at[source[s]], r.gatez_sem, s, ea_peer[s])
    go(r.gate_in, r.gate_near, r.gatet_sem, 0, ta_peer[1])

    row_relays = relay(r.rows_all, r.rowt_sem, r.rowr_sem, [s for s in near_first if s in sz.relay])
    row_relays += relay(r.dy_all, r.dyt_sem, r.dyr_sem, sz.dy_relay)

    loads[3].wait()
    loads[4].wait()
    first = jnp.where(j == 0, 1.0, 0.0)
    spot = iota((cs, cs), 0) == iota((cs, cs), 1)
    rows_n = sz.blocks * cs

    def expert_chunk(q, p, chunk):
        at = pl.ds(chunk * sz.blocks, sz.blocks) if sz.chunks > 1 else slice(None)
        keep = p if sz.kept > 1 else 0
        rows = r.rows_all[q, at].reshape(rows_n, d)
        dy = r.dy_all[q, at].reshape(rows_n, d).astype(F32)
        gates = []
        for b in range(sz.blocks):
            g = chunk * sz.blocks + b
            held, which = ((r.gate_in, 0), (r.gate_near, 0), (r.gate_near, 1), (r.gate_in, 1))[p]
            level = held[g, which][0:1, 0:cs]
            gates.append(jnp.sum(jnp.where(spot, level, 0.0), axis=1, keepdims=True))
        gate = jnp.concatenate(gates, axis=0) if len(gates) > 1 else gates[0]
        pre_act = mm(rows, r.up_w[...]) + r.b_up[...]
        cdf, density = gelu_parts(pre_act)
        act_low = (pre_act * cdf).astype(BF16)
        slot_grad = (gate * dy).astype(BF16)
        pre_grad = (mm(slot_grad, r.down_w[...], NT) * (cdf + pre_act * density)).astype(BF16)
        row_grad = mm(pre_grad, r.up_w[...], NT).astype(BF16)
        r.act_t[keep], r.pre_t[keep], r.slot_t[keep] = act_low, pre_grad, slot_grad
        r.dy_all[q, at] = row_grad.reshape(sz.blocks, cs, d)
        expert_out = mm(act_low, r.down_w[...]) + first * r.b_down[...]
        r.out_t[keep] = (gate * expert_out).astype(BF16)
        dgate = jnp.sum(expert_out * dy, axis=1, keepdims=True)
        for b in range(sz.blocks):
            g = chunk * sz.blocks + b
            level = jnp.sum(
                jnp.where(spot, dgate[b * cs : (b + 1) * cs], 0.0), axis=0, keepdims=True
            )
            r.dg_send[p, g, :, 0:cs] = jnp.broadcast_to(level, (8, cs))

    def weight_chunk(q, p, chunk, fresh):
        at = pl.ds(chunk * sz.blocks, sz.blocks) if sz.chunks > 1 else slice(None)
        keep = p if sz.kept > 1 else 0
        rows = r.rows_all[q, at].reshape(rows_n, d)
        up = mm(rows, r.pre_t[keep], TN)
        down = mm(r.act_t[keep], r.slot_t[keep], TN)
        biases = jnp.concatenate(
            [
                jnp.sum(r.pre_t[keep].astype(F32), axis=0, keepdims=True),
                jnp.sum(r.slot_t[keep].astype(F32), axis=0, keepdims=True),
                jnp.zeros((6, d), F32),
            ]
        )
        if fresh:
            r.up_acc[...], r.down_acc[...], r.bias_acc[...] = up, down, biases
        else:
            r.up_acc[...] += up
            r.down_acc[...] += down
            r.bias_acc[...] += biases
        r.rows_all[q, at] = r.out_t[keep].reshape(sz.blocks, cs, d)

    parts = (None, (low_half, high_half), (high_half, low_half))
    blocks = later[1:2] + later[:1] + later[2:] + [0]
    early_planes = (ea + 1) // 2

    fine = [(s, target[s]) for s in blocks] if sz.direct else [(0, slice(None))]
    whole = [(0, slice(None))]

    def share_diagonal(ref, relay_in, kind, groups):
        for s, g in groups:
            for n, p, part in ((0, 2, low_half), (1, 1, high_half)):
                half = ref.at[quarter[3], g, part]
                go(half, relay_in.at[n, g], kind, (n, s), ta_peer[p])

    def share_straight(ref, taken, kind, groups, p):
        for s, g in groups:
            half = parts[p][1]
            go(ref.at[quarter[p], g, half], taken.at[p - 1, g, half], kind, (1 + p, s), ta_peer[p])

    def share_joined(ref, taken, relay_in, kind, groups, p):
        for s, g in groups:
            half = parts[p][0]
            got(relay_in.at[p - 1, g], kind, (p - 1, s), ta_peer[3 - p])
            joined = ref[quarter[p], g, half].astype(F32) + relay_in[p - 1, g].astype(F32)
            ref[quarter[p], g, half] = joined.astype(BF16)
            go(ref.at[quarter[p], g, half], taken.at[p - 1, g, half], kind, (3 + p, s), ta_peer[p])

    def share_got(taken, kind, s, g):
        for p in (1, 2):
            got(taken.at[p - 1, g, parts[p][1]], kind, (1 + p, s), ta_peer[p])
            got(taken.at[p - 1, g, parts[p][0]], kind, (3 + p, s), ta_peer[p])

    def share_sum(ref, taken, g):
        return ref[j, g].astype(F32) + taken[0, g].astype(F32) + taken[1, g].astype(F32)

    for p in (0, 3, 1, 2):
        q = quarter[p]
        if p == 0:
            for copy in dy_forwards + row_forwards:
                copy.wait_send()
        elif p == 3:
            for s in later:
                if s in sz.dy_relay:
                    got(r.dy_all.at[q, source[s], low_half], r.dyr_sem, (1, s), ta_peer[1])
                    got(r.dy_all.at[q, source[s], high_half], r.dyr_sem, (2, s), ta_peer[2])
                else:
                    got(r.dy_all.at[q, source[s]], r.dyz_sem, (1, s), ea_peer[s])
                if s in sz.relay:
                    got(r.rows_all.at[q, source[s], low_half], r.rowr_sem, (1, s), ta_peer[1])
                    got(r.rows_all.at[q, source[s], high_half], r.rowr_sem, (2, s), ta_peer[2])
                else:
                    got(r.rows_all.at[q, source[s]], r.rowz_sem, (1, s), ea_peer[s])
        else:
            if p == 1:
                got(r.gate_near, r.gatet_sem, 0, ta_peer[1])
            for s in range(ea):
                if s not in sz.dy_relay:
                    got(r.dy_all.at[q, source[s]], r.dyt_sem, (p, s), ta_peer[p])
                if s not in sz.relay:
                    got(r.rows_all.at[q, source[s]], r.rowt_sem, (p, s), ta_peer[p])
            if p == 1:
                for copy in row_relays:
                    copy.wait_send()
        if sz.chunks == 1:
            expert_chunk(q, p, 0)
            if p == 0:
                weight_chunk(q, p, 0, True)
        else:
            if p == 0:
                r.up_acc[...] = jnp.zeros((d, sz.hidden), F32)
                r.down_acc[...] = jnp.zeros((sz.hidden, d), F32)
                r.bias_acc[...] = jnp.zeros((8, d), F32)

            @pl.loop(0, sz.chunks)
            def _(chunk):
                expert_chunk(q, p, chunk)
                weight_chunk(q, p, chunk, False)

        if p:
            go(r.dg_send.at[p], r.dg_in.at[p], r.dg_sem, p, ta_peer[p])
        group = fine[:early_planes]
        if p == 3:
            share_diagonal(r.dy_all, r.rg_relay, r.rg_sem, group)
        elif p:
            share_straight(r.dy_all, r.rg_in, r.rg_sem, group, p)
    first_sent = list(started)
    for p in (1, 2):
        share_joined(r.dy_all, r.rg_in, r.rg_relay, r.rg_sem, group, p)
    if sz.chunks == 1:
        weight_chunk(quarter[3], 3, 0, False)
    group = fine[early_planes:]
    for copy in first_sent:
        copy.wait_send()
    if group:
        share_diagonal(r.dy_all, r.rg_relay, r.rg_sem, group)
        for p in (1, 2):
            share_straight(r.dy_all, r.rg_in, r.rg_sem, group, p)
    if sz.chunks == 1:
        weight_chunk(quarter[1], 1, 0, False)
    for p in (1, 2):
        share_joined(r.dy_all, r.rg_in, r.rg_relay, r.rg_sem, group, p)

    home_copies = []
    for p in partners:
        got(r.dg_in.at[p], r.dg_sem, p, ta_peer[p])

    def send_home(planes):
        for s in planes:
            g = target[s]
            if sz.direct or s == blocks[0]:
                share_got(r.rg_in, r.rg_sem, *((s, g) if sz.direct else whole[0]))
            share = share_sum(r.dy_all, r.rg_in, g)
            dgate = r.dg_send[0, g]
            for p in partners:
                dgate = dgate + r.dg_in[p, g]
            if s:
                r.rgz_send[g] = share.astype(BF16)
                r.dgz_send[g] = dgate
                go(r.dgz_send.at[g], r.dg_back.at[z], r.dgz_sem, s, ea_peer[s])
                home_copies.append(go(r.rgz_send.at[g], r.rg_back.at[z], r.rgz_sem, s, ea_peer[s]))
            else:
                r.rg_back[z] = share.astype(BF16)
                r.dg_back[z] = dgate

    send_home(blocks[:early_planes])
    if sz.chunks == 1:
        weight_chunk(quarter[2], 2, 0, False)
    send_home(blocks[early_planes:])
    share_diagonal(r.rows_all, r.eo_relay, r.eo_sem, whole)
    for p in (1, 2):
        share_straight(r.rows_all, r.eo_in, r.eo_sem, whole, p)

    r.up_low[...] = r.up_acc[...].astype(BF16)
    r.down_low[...] = r.down_acc[...].astype(BF16)
    go(r.up_low, r.up_in, r.rep_sem, 0, other)
    go(r.down_low, r.down_in, r.rep_sem, 1, other)
    go(r.bias_acc, r.bias_in, r.rep_sem, 2, other)

    place_0, place_1 = r.place_col[:, 0:1], r.place_col[:, 1:2]
    lane = iota((qt, sz.experts * cs), 1)
    back = onehot((lane == place_0) | (lane == place_1)).astype(BF16)
    for s in later:
        got(r.dg_back.at[source[s]], r.dgz_sem, s, ea_peer[s])
        got(r.rg_back.at[source[s]], r.rgz_sem, s, ea_peer[s])

    drouter = jnp.zeros((sz.ep, qt), F32)
    for expert in range(sz.experts):
        level = mm(r.dg_back[expert][:, 0:cs], slots_of(expert, 0), NN, EXACT)
        drouter = drouter + jnp.where(iota((sz.ep, 1), 0) == expert, level[0:1], 0.0)
    router = r.probs[...]
    dlogits = (router * (drouter - jnp.sum(router * drouter, axis=0, keepdims=True))).astype(BF16)
    into_two = mm(back, r.rg_back[...].reshape(sz.experts * cs, d)) + mm(dlogits, router_w, TN)
    _, hat_two, inv_two = layer_norm(r.hidden[...], flat_row(r.gain2), flat_row(r.bias2))
    dhidden = r.dy_mine[...].astype(F32) + norm_back(into_two, hat_two, inv_two, flat_row(r.gain2))
    r.dhidden[...] = dhidden
    dattn = dhidden.astype(BF16)
    r.da_all[j] = dattn
    for p in partners:
        go(r.da_all.at[j], r.da_all.at[j], r.da_sem, p, ta_peer[p])
    router_grad = mm(dlogits, r.b_low[...])
    rows_at = iota((sz.early, 1), 0)
    early = jnp.where(rows_at < sz.experts, fit(router_grad, sz.early), 0.0)
    for offset, values in enumerate((into_two * hat_two, into_two, dattn.astype(F32))):
        total = jnp.sum(values, axis=0, keepdims=True)
        early = early + jnp.where(rows_at == sz.experts + offset, total, 0.0)

    def small_start(values, by_ta, sem):
        by_ta[j] = values
        for p in partners:
            go(by_ta.at[j], by_ta.at[j], sem, (0, p), ta_peer[p])

    def small_middle(by_ta, by_dev, sem, own_rows):
        for p in partners:
            got(by_ta.at[quarter[p]], sem, (0, p), ta_peer[p])
        total = by_ta[0]
        for q in range(1, nq):
            total = total + by_ta[q]
        if own_rows:
            total = jnp.where(iota((8, 1), 0) < 2, total, by_ta[j])
        by_dev[c] = total
        go(by_dev.at[c], by_dev.at[c], sem, (1, 0), other)

    def small_last(by_dev, by_ea, sem):
        got(by_dev.at[1 - c], sem, (1, 0), other)
        by_ea[z] = by_dev[0] + by_dev[1]
        for s in later:
            go(by_ea.at[z], by_ea.at[z], sem, (2, s), ea_peer[s])

    def small_end(by_ea, out, sem):
        for s in later:
            got(by_ea.at[source[s]], sem, (2, s), ea_peer[s])
        total = by_ea[0]
        for e in range(1, ea):
            total = total + by_ea[e]
        out[...] = total

    if sz.direct:
        small_start(early, r.early_ta, r.early_sem)
    else:
        r.o_early[...] = early

    for p in partners:
        got(r.da_all.at[quarter[p]], r.da_sem, p, ta_peer[p])
    for p in (1, 2):
        share_joined(r.rows_all, r.eo_in, r.eo_relay, r.eo_sem, whole, p)
    if sz.direct:
        small_middle(r.early_ta, r.early_dev, r.early_sem, False)

    unpick = onehot(iota((sz.tp, nq * qt), 1) == r.perm_col[:, 0:1].astype(jnp.int32)).astype(BF16)
    dattn = mm(unpick, r.da_all[...].reshape(nq * qt, d)).astype(BF16)
    w_out = r.w_out[...].reshape(sz.inner, d)
    dmixed = mm(dattn, w_out, NT).astype(BF16).reshape(flat)

    spans = (pl.ds(0, 1), pl.ds(1, 3))

    def piece_start(n, values):
        r.pd_send[n] = values.reshape(2, sz.half, d).astype(BF16)

    def piece_send(n):
        go(r.pd_send.at[spans[n], 1 - c], r.pd_in.at[spans[n]], r.pd_sem, n, other)

    def piece_middle(n):
        span = spans[n]
        got(r.pd_in.at[span], r.pd_sem, n, other)
        for k in ((0,), (1, 2, 3))[n]:
            both = r.pd_send[k, c].astype(F32) + r.pd_in[k].astype(F32)
            for e in range(ea):
                r.pz_send[k, e] = both[e * sz.piece : (e + 1) * sz.piece].astype(BF16)
            r.pz_in[k, z] = r.pz_send[k, z]
        for s in later:
            go(r.pz_send.at[span, target[s]], r.pz_in.at[span, z], r.pz_sem, (n, s), ea_peer[s])

    def piece_last(n):
        span = spans[n]
        for s in later:
            got(r.pz_in.at[span, source[s]], r.pz_sem, (n, s), ea_peer[s])
        for k in ((0,), (1, 2, 3))[n]:
            total = r.pz_in[k, 0].astype(F32)
            for e in range(1, ea):
                total = total + r.pz_in[k, e].astype(F32)
            r.p_all[k, c, z] = total.astype(BF16)
        block = r.p_all.at[span, c, z]
        for s in later:
            go(block, block, r.pa_sem, (n, s), ea_peer[s])
        go(block, block, r.pb_sem, (n, 0), other)

    def piece_pass(n):
        for s in later:
            block = r.p_all.at[spans[n], c, source[s]]
            got(block, r.pa_sem, (n, s), ea_peer[s])
            go(block, block, r.pb_sem, (n, s), other)

    def piece_end(n):
        for s in range(ea):
            got(r.p_all.at[spans[n], 1 - c, source[s]], r.pb_sem, (n, s), other)

    if not sz.direct:

        def piece_start(n, values):
            r.o_piece[n] = values

        piece_send = piece_middle = piece_last = piece_pass = piece_end = lambda n: None

    keeps = []
    for n, own, taken, out in ((0, r.up_low, r.up_in, r.o_up), (1, r.down_low, r.down_in, r.o_down)):
        got(taken, r.rep_sem, n, other)
        taken[...] = (own[...].astype(F32) + taken[...].astype(F32)).astype(BF16)
        keeps.append(pltpu.make_async_copy(taken, out, r.load_sem.at[n]))
        keeps[-1].start()
    got(r.bias_in, r.rep_sem, 2, other)
    r.o_bias[...] = r.bias_acc[...] + r.bias_in[...]
    piece_start(0, mm(r.mixed[...].reshape(sz.tp, sz.inner), dattn, TN))
    piece_send(0)
    if sz.direct:
        small_last(r.early_dev, r.early_ea, r.early_sem)

    def attention_back(image):
        dmix = stack(dmixed[image])
        probs = r.kept_probs[image] if sz.direct else attention_probs(image)
        dprobs = mm(dmix, r.v[image], NT)
        dvalue = mm(probs.astype(BF16), dmix, TN)
        inner = jnp.sum(probs * dprobs, axis=-1, keepdims=True)
        dscores = (probs * (dprobs - inner)).astype(BF16)
        dquery = unstack(mm(dscores, r.k[image])) * scale
        dkey = mm(dscores, stack(r.q[image]), TN) * scale
        for n, values in enumerate((dquery, dkey, dvalue)):
            r.dproj[n, image] = values.astype(BF16)

    attention_back(0)
    piece_middle(0)
    for image in range(1, sz.images):
        attention_back(image)
    dproj = [r.dproj[n].reshape(sz.tp, sz.inner) for n in range(3)]
    for n in (2, 0, 1):
        piece_start(n + 1, mm(dproj[n], r.a_low[...], TN))
    piece_send(1)
    share_got(r.eo_in, r.eo_sem, *whole[0])
    for copy in home_copies:
        copy.wait_send()
    for s in later + [0]:
        g = target[s]
        share = share_sum(r.rows_all, r.eo_in, g)
        if s:
            r.rgz_send[g] = share.astype(BF16)
            go(r.rgz_send.at[g], r.eo_back.at[z], r.eoz_sem, s, ea_peer[s])
        else:
            r.eo_back[z] = share.astype(BF16)

    piece_last(0)
    into_part = mm(dproj[0], r.qkv_w[0]) + mm(dproj[1], r.qkv_w[1]) + mm(dproj[2], r.qkv_w[2])
    r.in_send[...] = mm(pick_all, into_part.astype(BF16)).astype(BF16).reshape(nq, qt, d)
    for p in partners:
        go(r.in_send.at[quarter[p]], r.in_part.at[j], r.ip_sem, p, ta_peer[p])
    r.in_part[j] = r.in_send[j]
    _, hat_one, _ = layer_norm(r.padded[...].reshape(sz.tp, d).astype(F32), flat_row(r.gain1), flat_row(r.bias1))
    rows_at = iota((8, 1), 0)
    late = jnp.where(rows_at == 0, jnp.sum(into_part * hat_one, axis=0, keepdims=True), 0.0)
    late = late + jnp.where(rows_at == 1, jnp.sum(into_part, axis=0, keepdims=True), 0.0)
    for row, n in ((2, 0), (3, 2)):
        total = jnp.sum(dproj[n].astype(F32), axis=0, keepdims=True)
        wide = jnp.concatenate([total, jnp.zeros((1, d - sz.inner), F32)], axis=1)
        late = late + jnp.where(rows_at == row, wide, 0.0)
    if sz.direct:
        small_start(late, r.late_ta, r.late_sem)
    else:
        r.o_late[...] = late
    piece_middle(1)
    if sz.direct:
        small_middle(r.late_ta, r.late_dev, r.late_sem, True)

    for p in partners:
        got(r.in_part.at[quarter[p]], r.ip_sem, p, ta_peer[p])
    into_one = r.in_part[0].astype(F32)
    for q in range(1, nq):
        into_one = into_one + r.in_part[q].astype(F32)
    x_mine = mm(pick_of(j), r.padded[...].reshape(sz.tp, d))
    _, hat_mine, inv_mine = layer_norm(x_mine, flat_row(r.gain1), flat_row(r.bias1))
    grad = r.dhidden[...] + norm_back(into_one, hat_mine, inv_mine, flat_row(r.gain1))
    r.ig_all[j] = grad.astype(BF16)
    for p in partners:
        go(r.ig_all.at[j], r.ig_all.at[j], r.ig_sem, p, ta_peer[p])
    if sz.direct:
        small_last(r.late_dev, r.late_ea, r.late_sem)

    for s in later:
        got(r.eo_back.at[source[s]], r.eoz_sem, s, ea_peer[s])
    output = r.hidden[...] + mm(back, r.eo_back[...].reshape(sz.experts * cs, d))
    r.out_all[j] = output.astype(BF16)
    for p in partners:
        go(r.out_all.at[j], r.out_all.at[j], r.out_sem, p, ta_peer[p])
    piece_last(1)
    piece_pass(0)
    piece_pass(1)
    stores = []

    def store(n, values, src, dst):
        src[...] = values.reshape(src.shape)
        stores.append(pltpu.make_async_copy(src, dst, r.load_sem.at[n]))
        stores[-1].start()

    for p in partners:
        got(r.ig_all.at[quarter[p]], r.ig_sem, p, ta_peer[p])
    store(2, mm(unpick, r.ig_all[...].reshape(nq * qt, d)).astype(BF16), r.a_low, r.o_in)
    for p in partners:
        got(r.out_all.at[quarter[p]], r.out_sem, p, ta_peer[p])
    store(3, mm(unpick, r.out_all[...].reshape(nq * qt, d)).astype(BF16), r.padded, r.o_out)
    if sz.direct:
        small_end(r.early_ea, r.o_early, r.early_sem)
        small_end(r.late_ea, r.o_late, r.late_sem)
    piece_end(0)
    piece_end(1)
    for copy in stores + keeps:
        copy.wait()
    for copy in started[-pool:]:
        copy.wait_send()
    assert len(receive) <= sz.arrivals, len(receive)


def flat_row(ref):
    return ref[...].reshape(1, -1)


def fit(values, rows):
    have = values.shape[0]
    if have >= rows:
        return values[:rows]
    return jnp.concatenate([values, jnp.zeros((rows - have, values.shape[1]), F32)])


def run_block(sz, inputs):
    nq, ea, d, cs, qt = sz.nq, sz.ea, sz.d, sz.cs, sz.qt
    dma = pltpu.SemaphoreType.DMA
    rows = sz.blocks * cs
    outs = dict(
        o_out=((sz.images, sz.lp, d), BF16),
        o_in=((sz.tp, d), BF16),
        o_early=((sz.early, d), F32),
        o_late=((8, d), F32),
        o_up=((d, sz.hidden), BF16),
        o_down=((sz.hidden, d), BF16),
        o_bias=((8, d), F32),
    )
    flat = (sz.images, sz.lp, sz.inner)
    block = (cs, d)
    buffers = dict(
        tok_v=((sz.images, sz.length, d), BF16),
        cot_v=((sz.images, sz.length, d), BF16),
        qkv_w=((3, sz.inner, d), BF16),
        up_w=((d, sz.hidden), BF16),
        down_w=((sz.hidden, d), BF16),
        w_full=((nq, 2, sz.half, d), BF16),
        padded=((sz.images, sz.lp, d), BF16),
        perm_col=((sz.tp, 128), F32),
        place_row=((4, qt), jnp.int32),
        place_col=((qt, 128), jnp.int32),
        a_low=((sz.tp, d), BF16),
        q=(flat, BF16),
        k=(flat, BF16),
        v=(flat, BF16),
        mixed=(flat, BF16),
        dproj=((3,) + flat, BF16),
        mix_send=((nq, qt, sz.inner), BF16),
        mix_in=((2, nq, qt, sz.inner), BF16),
        dy_mine=((qt, d), BF16),
        hidden=((qt, d), F32),
        dhidden=((qt, d), F32),
        b_low=((qt, d), BF16),
        probs=((sz.ep, qt), F32),
        dy_send=((2, ea) + block, BF16),
        gate_send=((ea, 2, 8, 128), F32),
        dy_all=((nq, ea) + block, BF16),
        rows_all=((nq, ea) + block, BF16),
        gate_in=((ea, 2, 8, 128), F32),
        gate_near=((ea, 2, 8, 128), F32),
        act_t=((sz.kept, rows, sz.hidden), BF16),
        pre_t=((sz.kept, rows, sz.hidden), BF16),
        slot_t=((sz.kept, rows, d), BF16),
        out_t=((sz.kept, rows, d), BF16),
        dg_send=((nq, ea, 8, 128), F32),
        dg_in=((nq, ea, 8, 128), F32),
        rg_in=((2, ea) + block, BF16),
        rg_relay=((2, ea, cs // 2, d), BF16),
        eo_in=((2, ea) + block, BF16),
        eo_relay=((2, ea, cs // 2, d), BF16),
        rgz_send=((ea,) + block, BF16),
        dgz_send=((ea, 8, 128), F32),
        rg_back=((ea,) + block, BF16),
        eo_back=((ea,) + block, BF16),
        dg_back=((ea, 8, 128), F32),
        up_acc=((d, sz.hidden), F32),
        down_acc=((sz.hidden, d), F32),
        bias_acc=((8, d), F32),
        up_low=((d, sz.hidden), BF16),
        down_low=((sz.hidden, d), BF16),
        up_in=((d, sz.hidden), BF16),
        down_in=((sz.hidden, d), BF16),
        bias_in=((8, d), F32),
        da_all=((nq, qt, d), BF16),
        ig_all=((nq, qt, d), BF16),
        out_all=((nq, qt, d), BF16),
        in_send=((nq, qt, d), BF16),
        in_part=((nq, qt, d), BF16),
    )
    if sz.direct:
        outs["p_all"] = ((4, 2, ea, sz.piece, d), BF16)
        buffers |= dict(
            early_ta=((nq, sz.early, d), F32),
            early_dev=((2, sz.early, d), F32),
            early_ea=((ea, sz.early, d), F32),
            late_ta=((nq, 8, d), F32),
            late_dev=((2, 8, d), F32),
            late_ea=((ea, 8, d), F32),
            pd_send=((4, 2, sz.half, d), BF16),
            pd_in=((4, sz.half, d), BF16),
            pz_send=((4, ea, sz.piece, d), BF16),
            pz_in=((4, ea, sz.piece, d), BF16),
        )
    else:
        outs["o_piece"] = ((4, sz.inner, d), F32)
    if sz.direct:
        buffers["row_send"] = ((2, ea) + block, BF16)
        buffers["kept_probs"] = ((sz.images, sz.heads * sz.lp, sz.lp), F32)
    names = list(inputs) + list(outs) + list(buffers) + ["sent", "arrived", "load_sem"]
    vm = pl.BlockSpec(memory_space=pltpu.VMEM)
    far = pl.BlockSpec(memory_space=pltpu.HBM)
    results = pl.pallas_call(
        functools.partial(block_kernel, sz, names),
        out_shape=[jax.ShapeDtypeStruct(*spec) for spec in outs.values()],
        in_specs=[far if name in ("tok", "cot", "w_qkv", "w_up", "w_down") else vm for name in inputs],
        out_specs=[far if name in ("o_up", "o_down", "o_in", "o_out") else vm for name in outs],
        scratch_shapes=[pltpu.VMEM(*spec) for spec in buffers.values()]
        + [dma((sz.pool,)), dma((sz.arrivals,)), dma((5,))],
        name="block",
        compiler_params=pltpu.CompilerParams(
            collective_id=0, has_side_effects=True, vmem_limit_bytes=60 << 20
        ),
    )(*inputs.values())
    return dict(zip(outs, results))


def finish_kernel(sz, names, *refs):
    r = types.SimpleNamespace(**dict(zip(names, refs)))
    n, d = sz.experts, sz.d
    loads, stores = [], []

    def load(src, dst):
        loads.append(pltpu.make_async_copy(src, dst, r.sem_in.at[len(loads)]))
        loads[-1].start()

    def store(src, dst):
        stores.append(pltpu.make_async_copy(src, dst, r.sem_out.at[len(stores)]))
        stores[-1].start()

    third = d // 3
    spans = [pl.ds(k * third, third) for k in range(3)]
    for src, dst in ((r.up, r.up_v), (r.down, r.down_v)):
        for span in spans:
            load(src.at[span], dst.at[span])
    load(r.grad, r.grad_v)
    load(r.out, r.out_v)
    load(r.piece, r.piece_v)
    for dst, src in (
        (r.f_b, r.early[n + 2 : n + 3]),
        (r.f_g1, r.late[0:1]),
        (r.f_c1, r.late[1:2]),
        (r.f_g2, r.early[n : n + 1]),
        (r.f_c2, r.early[n + 1 : n + 2]),
    ):
        dst[...] = src.reshape(d)
    r.f_router[...] = r.early[0:n]
    r.f_qv[...] = r.late[2:4, 0 : sz.inner]
    r.f_upb[...] = r.bias[0:1]
    r.f_downb[...] = r.bias[1:2]
    at = 0
    for src, wide, dst in ((r.up_v, r.up_w, r.f_up), (r.down_v, r.down_w, r.f_down)):
        for span in spans:
            loads[at].wait()
            at += 1
            wide[span] = src[span].astype(F32)
            store(wide.at[span], dst.at[span])
    loads[at].wait()
    for image in range(sz.images):
        r.grad_w[:, image, :] = r.grad_v[image * sz.lp : image * sz.lp + sz.length].astype(F32)
    store(r.grad_w, r.f_grad)
    loads[at + 1].wait()
    for image in range(sz.images):
        r.out_w[:, image, :] = r.out_v[image, 0 : sz.length]
    store(r.out_w, r.f_out)
    loads[at + 2].wait()
    for k in range(4):
        for core in range(2):
            for e in range(sz.ea):
                start = core * sz.half + e * sz.piece
                r.piece_w[k, start : start + sz.piece] = r.piece_v[k, core, e].astype(F32)
        store(r.piece_w.at[k], r.f_qkv.at[k - 1] if k else r.f_o)
    for copy in stores:
        copy.wait()


def finish(sz, got):
    d, n = sz.d, sz.experts
    inputs = dict(
        up=got["o_up"],
        down=got["o_down"],
        out=got["o_out"],
        grad=got["o_in"],
        piece=got["p_all"],
        early=got["o_early"],
        late=got["o_late"],
        bias=got["o_bias"],
    )
    outs = dict(
        f_out=((sz.length, sz.images, d), BF16),
        f_grad=((sz.length, sz.images, d), F32),
        f_qkv=((3, sz.inner, d), F32),
        f_qv=((2, sz.inner), F32),
        f_o=((sz.inner, d), F32),
        f_b=((d,), F32),
        f_g1=((d,), F32),
        f_c1=((d,), F32),
        f_g2=((d,), F32),
        f_c2=((d,), F32),
        f_router=((n, d), F32),
        f_up=((d, sz.hidden), F32),
        f_upb=((1, sz.hidden), F32),
        f_down=((sz.hidden, d), F32),
        f_downb=((1, d), F32),
    )
    buffers = dict(
        up_v=((d, sz.hidden), BF16),
        down_v=((sz.hidden, d), BF16),
        grad_v=((sz.tp, d), BF16),
        out_v=((sz.images, sz.lp, d), BF16),
        piece_v=((4, 2, sz.ea, sz.piece, d), BF16),
        up_w=((d, sz.hidden), F32),
        down_w=((sz.hidden, d), F32),
        grad_w=((sz.length, sz.images, d), F32),
        out_w=((sz.length, sz.images, d), BF16),
        piece_w=((4, sz.inner, d), F32),
    )
    vm = pl.BlockSpec(memory_space=pltpu.VMEM)
    far = pl.BlockSpec(memory_space=pltpu.HBM)
    large = ("up", "down", "out", "grad", "piece", "f_out", "f_grad", "f_qkv", "f_o", "f_up", "f_down")
    names = list(inputs) + list(outs) + list(buffers) + ["sem_in", "sem_out"]
    results = pl.pallas_call(
        functools.partial(finish_kernel, sz, names),
        out_shape=[jax.ShapeDtypeStruct(*spec) for spec in outs.values()],
        in_specs=[far if name in large else vm for name in inputs],
        out_specs=[far if name in large else vm for name in outs],
        scratch_shapes=[pltpu.VMEM(*spec) for spec in buffers.values()]
        + [pltpu.SemaphoreType.DMA((16,)), pltpu.SemaphoreType.DMA((16,))],
        name="finish",
        compiler_params=pltpu.CompilerParams(vmem_limit_bytes=60 << 20),
    )(*inputs.values())
    (out, grad, qkv, qv, o, b, g1, c1, g2, c2, router, up, up_b, down, down_b) = results
    turn = lambda t: jnp.swapaxes(t, 0, 1)
    return (
        turn(out),
        turn(grad),
        jnp.swapaxes(qkv, 1, 2),
        qv,
        o,
        b,
        g1,
        c1,
        g2,
        c2,
        router.T,
        up[None],
        up_b,
        down[None],
        down_b,
    )


def local(
    tokens,
    expert_ids,
    pair_ranks,
    cotangent,
    w_qkv,
    b_qv,
    w_out,
    b_out,
    ln1_gain,
    ln1_bias,
    ln2_gain,
    ln2_bias,
    w_router,
    w_up,
    b_up,
    w_down,
    b_down,
):
    sz = Sizes(tokens, expert_ids, w_qkv, w_up)
    pairs = jnp.stack([jnp.transpose(t, (2, 0, 1)) for t in (expert_ids, pair_ranks)])
    pairs = jnp.pad(
        pairs, ((0, 0), (0, 0), (0, 0), (0, sz.lp - sz.length)), constant_values=sz.tokens * 2
    )
    table = jnp.pad(pairs.reshape(4, sz.tp).astype(F32), ((0, 4), (0, ceil_to(sz.tp, 128) - sz.tp)))
    inputs = dict(
        tok=tokens,
        cot=cotangent,
        w_qkv=jnp.swapaxes(w_qkv, 1, 2),
        b_qv=b_qv,
        w_out=w_out.reshape(2, sz.half, sz.d),
        b_out=b_out,
        gain1=ln1_gain,
        bias1=ln1_bias,
        gain2=ln2_gain,
        bias2=ln2_bias,
        router=w_router.T,
        w_up=w_up[0],
        b_up=b_up,
        w_down=w_down[0],
        b_down=b_down,
        table=table,
    )
    got = run_block(sz, inputs)
    if sz.direct:
        return finish(sz, got)
    n = sz.experts
    piece, shared = lax.psum((got["o_piece"], got["o_late"][2:4]), ("ea", "dev"))
    early, late = lax.psum((got["o_early"], got["o_late"][:2]), ("ea", "ta", "dev"))
    return (
        got["o_out"][:, : sz.length],
        got["o_in"].reshape(got["o_out"].shape)[:, : sz.length].astype(F32),
        jnp.swapaxes(piece[1:], 1, 2),
        shared[:, : sz.inner],
        piece[0],
        early[n + 2],
        late[0],
        late[1],
        early[n],
        early[n + 1],
        early[:n].T,
        got["o_up"].astype(F32)[None],
        got["o_bias"][0:1],
        got["o_down"].astype(F32)[None],
        got["o_bias"][1:2],
    )


def solution(mesh):
    in_specs = (
        P(("ea", "dev"), None, None),
        P(("ea", "dev"), None, None),
        P(("ea", "dev"), None, None),
        P(("ea", "dev"), None, None),
        P(None, None, "ta"),
        P(None, "ta"),
        P("ta", None),
        P(),
        P(),
        P(),
        P(),
        P(),
        P(),
        P("ea", None, "ta"),
        P("ea", "ta"),
        P("ea", "ta", None),
        P("ea", None),
    )
    out_specs = (
        P(("ea", "dev"), None, None),
        P(("ea", "dev"), None, None),
        P(None, None, "ta"),
        P(None, "ta"),
        P("ta", None),
        P(),
        P(),
        P(),
        P(),
        P(),
        P(),
        P("ea", None, "ta"),
        P("ea", "ta"),
        P("ea", "ta", None),
        P("ea", None),
    )
    return jax.shard_map(local, mesh=mesh, in_specs=in_specs, out_specs=out_specs, check_vma=False)
```

```python
import functools
import types

import jax
import jax.numpy as jnp
from jax import lax
from jax.experimental import pallas as pl
from jax.experimental.pallas import tpu as pltpu
from jax.sharding import PartitionSpec as P

HDIM = 64
EPSILON = 1e-06
F32, BF16 = jnp.float32, jnp.bfloat16
EXACT = lax.Precision.HIGHEST
MESH = pl.DeviceIdType.MESH
NT = (((1,), (1,)), ((), ()))
TN = (((0,), (0,)), ((), ()))
NN = (((1,), (0,)), ((), ()))


def ceil_to(value, unit):
    return -(-value // unit) * unit


def mm(a, b, dims=NN, precision=None):
    return lax.dot_general(a, b, dims, precision=precision, preferred_element_type=F32)


def iota(shape, dim):
    return lax.broadcasted_iota(jnp.int32, shape, dim)


def onehot(mask):
    return jnp.where(mask, 1.0, 0.0).astype(F32)


class Sizes:
    def __init__(self, tokens, expert_ids, w_qkv, w_up):
        self.images, self.length, self.d = tokens.shape
        self.top = expert_ids.shape[2]
        self.tokens = self.images * self.length
        self.ea = lax.axis_size("ea")
        self.nq = lax.axis_size("ta")
        assert w_up.shape[0] == 1
        self.experts = self.ea
        self.cap = (9 * self.tokens * self.top + 8 * self.experts - 1) // (8 * self.experts)
        self.inner = w_qkv.shape[2]
        self.heads = self.inner // HDIM
        self.hidden = w_up.shape[2]
        self.lp = ceil_to(self.length, 16)
        self.tp = self.images * self.lp
        per_quarter = -(-self.tokens // self.nq)
        self.qt = ceil_to(per_quarter, 8)
        spread = (self.cap + (self.nq - 1) * self.experts) // self.nq
        self.cs = ceil_to(min(self.cap, per_quarter, spread), 16)
        self.ep = ceil_to(self.experts, 16)
        self.half = self.inner // 2
        self.piece = self.half // self.ea
        self.early = ceil_to(self.experts + 3, 8)
        self.blocks = max(1, min(self.ea, (256 if self.ea <= 8 else 64) // self.cs))
        self.chunks = self.ea // self.blocks
        self.direct = self.ea <= 8
        self.relay = [2] if self.direct else []
        self.dy_relay = [2] if self.direct else []
        self.kept = self.nq if self.chunks == 1 else 1
        self.pool = 40
        self.arrivals = 145 if self.direct else 48 + 13 * self.ea
        assert self.top == 2 and self.nq == 4 and self.experts * self.nq <= 128


def pair_table(sz, ids, ranks):
    wide = ceil_to(sz.tp, 128)
    spread, inside = jnp.zeros((8, wide), F32), jnp.zeros((1, wide), F32)
    for image in range(sz.images):
        experts, rank = ids[image].astype(F32), ranks[image].astype(F32)
        high = jnp.floor(rank * (1.0 / 64))
        rows = jnp.concatenate([experts, high, rank - high * 64, jnp.zeros_like(rank)], axis=0)
        lane = iota((sz.length, wide), 1)
        move = onehot(lane == iota((sz.length, wide), 0) + image * sz.lp).astype(BF16)
        spread = spread + mm(rows.astype(BF16), move)
        at = iota((1, wide), 1) - image * sz.lp
        inside = inside + onehot((at >= 0) & (at < sz.length))
    rank = spread[2:4] * 64 + spread[4:6]
    table = jnp.concatenate([spread[0:2], rank, jnp.zeros((4, wide), F32)], axis=0)
    return jnp.where(inside > 0, table, float(2 * sz.tokens))


def route(sz, table):
    cols = table.T[: sz.tp]
    wide = iota((sz.tp, 128), 1)
    lane = wide.astype(F32)

    def flip(*columns):
        spread = jnp.zeros((sz.tp, 128), F32)
        for n, column in enumerate(columns):
            spread = spread + jnp.where(wide == n, column, 0.0)
        turned = spread.T
        return [turned[n : n + 1] for n in range(len(columns))]

    def total(values):
        return jnp.sum(values, axis=1, keepdims=True)

    ids = [cols[:, k : k + 1] for k in range(2)]
    real = ids[0] < sz.experts
    member = [onehot(lane == column) for column in ids]
    dest = []
    for k in range(2):
        before = jnp.zeros((sz.tp, 128), F32)
        for m in range(2):
            mask = onehot(table[2 + m : 3 + m, : sz.tp] < cols[:, 2 + k : 3 + k])
            before = before + mm(mask.astype(BF16), member[m].astype(BF16))
        kept = (total(before * member[k]) < sz.cap) & real
        dest.append(jnp.where(kept, ids[k], float(sz.experts)))
    low, high = jnp.minimum(*dest), jnp.maximum(*dest)
    index = iota((sz.tp, 1), 0).astype(F32)
    kind = jnp.where(real, low * (sz.experts + 1) + high, float((sz.experts + 1) ** 2))
    key = kind * sz.tp + index
    (key_row,) = flip(key)
    earlier = onehot(key_row < key).astype(BF16)
    order = mm(earlier, jnp.ones((sz.tp, 128), BF16))[:, 0:1]
    lap = jnp.floor((order + 0.5) * (1.0 / sz.nq))
    quarter = order - lap * sz.nq
    perm = jnp.where(real, quarter * sz.qt + lap, -1.0)
    group = [
        onehot((lane == d * sz.nq + quarter) & (d < sz.experts)) for d in dest
    ]
    ahead = mm(earlier, (group[0] + group[1]).astype(BF16))
    place = []
    for k in range(2):
        slot = total(ahead * group[k])
        place.append(jnp.where(dest[k] < sz.experts, dest[k] * sz.cs + slot + 1.0, 0.0))
    perm_row, *place_row = flip(perm, *place)
    return perm, perm_row, place, place_row


def layer_norm(values, gain_vec, shift_vec):
    row_mean = jnp.mean(values, axis=-1, keepdims=True)
    centered = values - row_mean
    variance = jnp.mean(centered * centered, axis=-1, keepdims=True)
    inverse = lax.rsqrt(variance + EPSILON)
    normed = centered * inverse
    return (normed * gain_vec + shift_vec, normed, inverse)


def norm_back(grad_rows, normed, inverse, gain_vec):
    scaled = grad_rows * gain_vec
    return inverse * (
        scaled
        - jnp.mean(scaled, axis=-1, keepdims=True)
        - normed * jnp.mean(scaled * normed, axis=-1, keepdims=True)
    )


def push(src, dst, send_sem, recv_sem, device):
    return pltpu.make_async_remote_copy(
        src_ref=src,
        dst_ref=dst,
        send_sem=send_sem,
        recv_sem=recv_sem,
        device_id=device,
        device_id_type=MESH,
    )


def greet(devices):
    barrier = pltpu.get_barrier_semaphore()
    for device in devices:
        pl.semaphore_signal(barrier, inc=1, device_id=device, device_id_type=MESH)


def head_mask(sz, head, dtype):
    lane = iota((1, sz.inner), 1)
    return onehot((lane >= head * HDIM) & (lane < (head + 1) * HDIM)).astype(dtype)


def gelu_parts(values):
    cdf = 0.5 * (1.0 + lax.erf(values * (0.5**0.5)))
    density = jnp.exp(-0.5 * values * values) * (0.5 / jnp.pi) ** 0.5
    return cdf, density


class Sent:
    def __init__(self, copy):
        self.copy, self.done = copy, False

    def wait_send(self):
        if not self.done:
            self.copy.wait_send()
        self.done = True


class Refs(types.SimpleNamespace):
    def __getattr__(self, name):
        return name


def block_kernel(sz, names, *refs):
    r = Refs(**dict(zip(names, refs)))
    z, j, c = lax.axis_index("ea"), lax.axis_index("ta"), lax.axis_index("dev")
    nq, ea, d, cs, qt = sz.nq, sz.ea, sz.d, sz.cs, sz.qt
    quarter = [j, j + 1 - 2 * lax.rem(j, 2), j + 2 - 4 * lax.div(j, 2), 3 - j]
    ta_peer = [{"ta": q} for q in quarter]
    ea_peer = [{"ea": lax.rem(z + s, ea)} for s in range(ea)]
    source = [lax.rem(z - s + ea, ea) for s in range(ea)]
    target = [lax.rem(z + s, ea) for s in range(ea)]
    other = {"dev": 1 - c}
    later = [s for s in range(1, ea)]
    partners = (1, 2, 3)
    pool, started, receive = sz.pool, [], {}

    def go(src, dst, kind, index, device):
        at = receive.setdefault((kind, index), len(receive))
        n = len(started)
        if n >= pool:
            started[n - pool].wait_send()
        copy = push(src, dst, r.sent.at[n % pool], r.arrived.at[at], device)
        copy.start()
        started.append(Sent(copy))
        return started[-1]

    def got(dst, kind, index, device):
        at = receive.setdefault((kind, index), len(receive))
        push(dst, dst, r.sent.at[0], r.arrived.at[at], device).wait_recv()

    everyone = ta_peer[1:] + ea_peer[1:] + [other]
    greet(everyone)
    loads = []
    for n, (src, dst) in enumerate(
        ((r.cot, r.cot_v), (r.tok, r.tok_v), (r.w_qkv, r.qkv_w), (r.w_up, r.up_w), (r.w_down, r.down_w))
    ):
        loads.append(pltpu.make_async_copy(src, dst, r.load_sem.at[n]))
        loads[-1].start()
    pl.semaphore_wait(pltpu.get_barrier_semaphore(), len(everyone))

    for p in partners:
        go(r.w_out.at[c], r.w_full.at[j, c], r.w_sem, p, ta_peer[p])
    r.w_full[j] = r.w_out[...]

    perm_col, perm, place, place_rows = route(sz, pair_table(sz, r.ids, r.ranks))
    perm = perm.astype(jnp.int32)
    r.perm_col[...] = jnp.broadcast_to(perm_col, (sz.tp, 128))
    pick_all = onehot(iota((nq * qt, sz.tp), 0) == perm).astype(BF16)

    def pick_of(q):
        return onehot(iota((qt, sz.tp), 0) + q * qt == perm).astype(BF16)

    spread = iota((8, 1), 0)
    both = jnp.where(spread == 0, place_rows[0], 0.0) + jnp.where(spread == 1, place_rows[1], 0.0)
    for which, q in ((0, quarter[0]), (1, quarter[3])):
        chosen = mm(both, onehot(iota((qt, sz.tp), 0) + q * qt == perm), NT, EXACT)
        r.place_row[2 * which : 2 * which + 2] = (chosen[0:2] + 0.5).astype(jnp.int32) - 1
    pair_col = jnp.where(iota((1, 128), 1) == 0, place[0], 0.0)
    pair_col = pair_col + jnp.where(iota((1, 128), 1) == 1, place[1], 0.0)
    chosen = mm(onehot(iota((qt, sz.tp), 0) + j * qt == perm), pair_col, NN, EXACT)
    r.place_col[...] = (chosen + 0.5).astype(jnp.int32) - 1

    def slots_of(expert, which):
        row = iota((cs, qt), 0) + expert * cs
        first, second = r.place_row[2 * which : 2 * which + 1], r.place_row[2 * which + 1 : 2 * which + 2]
        return onehot((row == first) | (row == second))

    tail = (sz.length // 16) * 16
    loads[0].wait()
    for image in range(sz.images):
        r.padded[image, tail:] = jnp.zeros((sz.lp - tail, d), BF16)
        r.padded[image, 0 : sz.length] = r.cot_v[image]
    for which, q in ((0, quarter[0]), (1, quarter[3])):
        dy_rows = mm(pick_of(q), r.padded[...].reshape(sz.tp, d)).astype(BF16)
        if which == 0:
            r.dy_mine[...] = dy_rows
        for expert in range(sz.experts):
            r.dy_send[which, expert] = mm(slots_of(expert, which).astype(BF16), dy_rows).astype(BF16)
    dy_copies = []
    near_first = later[:1] + later[2:] + later[1:2]

    def send_dy(which, q, planes):
        for s in planes:
            block = r.dy_send.at[which, target[s]]
            dy_copies.append(go(block, r.dy_all.at[q, z], r.dyz_sem, (which, s), ea_peer[s]))

    send_dy(0, quarter[0], near_first)
    for which, q in ((0, quarter[0]), (1, quarter[3])):
        r.dy_all[q, z] = r.dy_send[which, z]

    def forward(ref, z_sem, t_sem, order):
        copies = []
        for s in order:
            block = ref.at[j, source[s]]
            if s:
                got(block, z_sem, (0, s), ea_peer[s])
            for p in (1, 2):
                copies.append(go(block, block, t_sem, (p, s), ta_peer[p]))
        return copies

    dy_forwards = forward(r.dy_all, r.dyz_sem, r.dyt_sem, [0])

    low_half, high_half = pl.ds(0, cs // 2), pl.ds(cs // 2, cs // 2)

    def relay(ref, t_sem, sem, planes):
        copies = []
        for s in planes:
            for p, part in ((1, high_half), (2, low_half)):
                got(ref.at[quarter[p], source[s]], t_sem, (p, s), ta_peer[p])
                half = ref.at[quarter[p], source[s], part]
                copies.append(go(half, half, sem, (3 - p, s), ta_peer[3 - p]))
        return copies

    loads[1].wait()
    loads[2].wait()
    for image in range(sz.images):
        r.padded[image, 0 : sz.length] = r.tok_v[image]
    normed_one, _, _ = layer_norm(
        r.padded[...].reshape(sz.tp, d).astype(F32), flat_row(r.gain1), flat_row(r.bias1)
    )
    a_low = normed_one.astype(BF16)
    r.a_low[...] = a_low
    flat = (sz.images, sz.lp, sz.inner)
    r.q[...] = (mm(a_low, r.qkv_w[0], NT) + r.b_qv[0:1]).astype(BF16).reshape(flat)
    r.k[...] = mm(a_low, r.qkv_w[1], NT).astype(BF16).reshape(flat)
    r.v[...] = (mm(a_low, r.qkv_w[2], NT) + r.b_qv[1:2]).astype(BF16).reshape(flat)

    for p in partners:
        block = r.w_full.at[quarter[p], c]
        got(block, r.w_sem, p, ta_peer[p])
        go(block, block, r.wd_sem, p, other)

    scale = HDIM ** (-0.5)
    live = iota((1, sz.lp), 1) < sz.length

    def stack(values):
        return jnp.concatenate([values * head_mask(sz, h, BF16) for h in range(sz.heads)], axis=0)

    def unstack(values):
        return sum(
            values[h * sz.lp : (h + 1) * sz.lp] * head_mask(sz, h, F32) for h in range(sz.heads)
        )

    def attention_probs(image):
        scores = mm(stack(r.q[image]), r.k[image], NT) * scale
        scores = jnp.where(live, scores, -1e30)
        exps = jnp.exp(scores - jnp.max(scores, axis=-1, keepdims=True))
        return exps / jnp.sum(exps, axis=-1, keepdims=True)

    for image in range(sz.images):
        probs = attention_probs(image)
        if sz.direct:
            r.kept_probs[image] = probs
        r.mixed[image] = unstack(mm(probs.astype(BF16), r.v[image])).astype(BF16)
    dealt = mm(pick_all, r.mixed[...].reshape(sz.tp, sz.inner)).astype(BF16)
    r.mix_send[...] = dealt.reshape(nq, qt, sz.inner)
    for p in partners:
        go(r.mix_send.at[quarter[p]], r.mix_in.at[0, j], r.mix_sem, (0, p), ta_peer[p])
        go(r.mix_send.at[quarter[3 - p]], r.mix_in.at[1, j], r.mix_sem, (1, p), ta_peer[p])
    for copy in list(dy_copies):
        copy.wait_send()
    send_dy(1, quarter[3], [s for s in near_first if s not in sz.dy_relay])
    dy_forwards += forward(r.dy_all, r.dyz_sem, r.dyt_sem, near_first)
    r.mix_in[0, j] = r.mix_send[j]
    r.mix_in[1, j] = r.mix_send[quarter[3]]
    x_rows = [mm(pick_of(q), r.padded[...].reshape(sz.tp, d)) for q in (quarter[0], quarter[3])]
    for p in partners:
        got(r.w_full.at[quarter[p], 1 - c], r.wd_sem, p, other)
    for p in partners:
        got(r.mix_in.at[0, quarter[p]], r.mix_sem, (0, p), ta_peer[p])
        got(r.mix_in.at[1, quarter[p]], r.mix_sem, (1, p), ta_peer[p])

    if not sz.direct:
        r.row_send = r.dy_send
        for copy in dy_copies:
            copy.wait_send()
    router_w = r.router[...]
    if sz.ep > sz.experts:
        router_w = jnp.concatenate([router_w, jnp.zeros((sz.ep - sz.experts, d), BF16)])
    def send_rows(which, q, planes):
        return [
            go(r.row_send.at[which, target[s]], r.rows_all.at[q, z], r.rowz_sem, (which, s), ea_peer[s])
            for s in planes
        ]

    for which in (0, 1):
        attention = flat_row(r.b_out)
        for q in range(nq):
            attention = attention + mm(r.mix_in[which, q], r.w_full[q].reshape(sz.inner, d))
        hidden = x_rows[which] + attention
        normed_two, _, _ = layer_norm(hidden, flat_row(r.gain2), flat_row(r.bias2))
        b_low = normed_two.astype(BF16)
        logits = mm(router_w, b_low, NT)
        logits = jnp.where(iota((sz.ep, 1), 0) < sz.experts, logits, -1e30)
        exps = jnp.exp(logits - jnp.max(logits, axis=0, keepdims=True))
        router = exps / jnp.sum(exps, axis=0, keepdims=True)
        if which == 0:
            r.hidden[...], r.b_low[...], r.probs[...] = hidden, b_low, router
        for expert in range(sz.experts):
            slots = slots_of(expert, which)
            r.row_send[which, expert] = mm(slots.astype(BF16), b_low).astype(BF16)
            level = jnp.broadcast_to(router[expert : expert + 1], (8, qt))
            r.gate_send[expert, which, :, 0:cs] = mm(level, slots, NT, EXACT)
        q = quarter[3 * which]
        if which:
            for s in later:
                go(r.gate_send.at[target[s]], r.gate_in.at[z], r.gatez_sem, s, ea_peer[s])
            r.gate_in[z] = r.gate_send[z]
        if which == 0:
            row_copies = send_rows(0, q, near_first[:-1])
        r.rows_all[q, z] = r.row_send[which, z]
    row_forwards = forward(r.rows_all, r.rowz_sem, r.rowt_sem, [0])
    for copy in row_copies:
        copy.wait_send()
    row_copies = send_rows(0, quarter[0], near_first[-1:])
    row_forwards += forward(r.rows_all, r.rowz_sem, r.rowt_sem, near_first[:-1])
    for copy in row_copies:
        copy.wait_send()
    send_rows(1, quarter[3], [s for s in near_first if s not in sz.relay])
    row_forwards += forward(r.rows_all, r.rowz_sem, r.rowt_sem, near_first[-1:])
    for s in later:
        got(r.gate_in.at[source[s]], r.gatez_sem, s, ea_peer[s])
    go(r.gate_in, r.gate_near, r.gatet_sem, 0, ta_peer[1])

    row_relays = relay(r.rows_all, r.rowt_sem, r.rowr_sem, [s for s in near_first if s in sz.relay])
    row_relays += relay(r.dy_all, r.dyt_sem, r.dyr_sem, sz.dy_relay)

    loads[3].wait()
    loads[4].wait()
    first = jnp.where(j == 0, 1.0, 0.0)
    spot = iota((cs, cs), 0) == iota((cs, cs), 1)
    rows_n = sz.blocks * cs

    def expert_chunk(q, p, chunk):
        at = pl.ds(chunk * sz.blocks, sz.blocks) if sz.chunks > 1 else slice(None)
        keep = p if sz.kept > 1 else 0
        rows = r.rows_all[q, at].reshape(rows_n, d)
        dy = r.dy_all[q, at].reshape(rows_n, d).astype(F32)
        gates = []
        for b in range(sz.blocks):
            g = chunk * sz.blocks + b
            held, which = ((r.gate_in, 0), (r.gate_near, 0), (r.gate_near, 1), (r.gate_in, 1))[p]
            level = held[g, which][0:1, 0:cs]
            gates.append(jnp.sum(jnp.where(spot, level, 0.0), axis=1, keepdims=True))
        gate = jnp.concatenate(gates, axis=0) if len(gates) > 1 else gates[0]
        pre_act = mm(rows, r.up_w[...]) + r.b_up[...]
        cdf, density = gelu_parts(pre_act)
        act_low = (pre_act * cdf).astype(BF16)
        slot_grad = (gate * dy).astype(BF16)
        pre_grad = (mm(slot_grad, r.down_w[...], NT) * (cdf + pre_act * density)).astype(BF16)
        row_grad = mm(pre_grad, r.up_w[...], NT).astype(BF16)
        r.act_t[keep], r.pre_t[keep], r.slot_t[keep] = act_low, pre_grad, slot_grad
        r.dy_all[q, at] = row_grad.reshape(sz.blocks, cs, d)
        expert_out = mm(act_low, r.down_w[...]) + first * r.b_down[...]
        r.out_t[keep] = (gate * expert_out).astype(BF16)
        dgate = jnp.sum(expert_out * dy, axis=1, keepdims=True)
        for b in range(sz.blocks):
            g = chunk * sz.blocks + b
            level = jnp.sum(
                jnp.where(spot, dgate[b * cs : (b + 1) * cs], 0.0), axis=0, keepdims=True
            )
            r.dg_send[p, g, :, 0:cs] = jnp.broadcast_to(level, (8, cs))

    def weight_chunk(q, p, chunk, fresh):
        at = pl.ds(chunk * sz.blocks, sz.blocks) if sz.chunks > 1 else slice(None)
        keep = p if sz.kept > 1 else 0
        rows = r.rows_all[q, at].reshape(rows_n, d)
        up = mm(rows, r.pre_t[keep], TN)
        down = mm(r.act_t[keep], r.slot_t[keep], TN)
        biases = jnp.concatenate(
            [
                jnp.sum(r.pre_t[keep].astype(F32), axis=0, keepdims=True),
                jnp.sum(r.slot_t[keep].astype(F32), axis=0, keepdims=True),
                jnp.zeros((6, d), F32),
            ]
        )
        if fresh:
            r.up_acc[...], r.down_acc[...], r.bias_acc[...] = up, down, biases
        else:
            r.up_acc[...] += up
            r.down_acc[...] += down
            r.bias_acc[...] += biases
        r.rows_all[q, at] = r.out_t[keep].reshape(sz.blocks, cs, d)

    parts = (None, (low_half, high_half), (high_half, low_half))
    blocks = later[1:2] + later[:1] + later[2:] + [0]
    early_planes = (ea + 1) // 2

    fine = [(s, target[s]) for s in blocks] if sz.direct else [(0, slice(None))]
    whole = [(0, slice(None))]

    def share_diagonal(ref, relay_in, kind, groups):
        for s, g in groups:
            for n, p, part in ((0, 2, low_half), (1, 1, high_half)):
                half = ref.at[quarter[3], g, part]
                go(half, relay_in.at[n, g], kind, (n, s), ta_peer[p])

    def share_straight(ref, taken, kind, groups, p):
        for s, g in groups:
            half = parts[p][1]
            go(ref.at[quarter[p], g, half], taken.at[p - 1, g, half], kind, (1 + p, s), ta_peer[p])

    def share_joined(ref, taken, relay_in, kind, groups, p):
        for s, g in groups:
            half = parts[p][0]
            got(relay_in.at[p - 1, g], kind, (p - 1, s), ta_peer[3 - p])
            joined = ref[quarter[p], g, half].astype(F32) + relay_in[p - 1, g].astype(F32)
            ref[quarter[p], g, half] = joined.astype(BF16)
            go(ref.at[quarter[p], g, half], taken.at[p - 1, g, half], kind, (3 + p, s), ta_peer[p])

    def share_got(taken, kind, s, g):
        for p in (1, 2):
            got(taken.at[p - 1, g, parts[p][1]], kind, (1 + p, s), ta_peer[p])
            got(taken.at[p - 1, g, parts[p][0]], kind, (3 + p, s), ta_peer[p])

    def share_sum(ref, taken, g):
        return ref[j, g].astype(F32) + taken[0, g].astype(F32) + taken[1, g].astype(F32)

    for p in (0, 3, 1, 2):
        q = quarter[p]
        if p == 0:
            for copy in dy_forwards + row_forwards:
                copy.wait_send()
        elif p == 3:
            for s in later:
                if s in sz.dy_relay:
                    got(r.dy_all.at[q, source[s], low_half], r.dyr_sem, (1, s), ta_peer[1])
                    got(r.dy_all.at[q, source[s], high_half], r.dyr_sem, (2, s), ta_peer[2])
                else:
                    got(r.dy_all.at[q, source[s]], r.dyz_sem, (1, s), ea_peer[s])
                if s in sz.relay:
                    got(r.rows_all.at[q, source[s], low_half], r.rowr_sem, (1, s), ta_peer[1])
                    got(r.rows_all.at[q, source[s], high_half], r.rowr_sem, (2, s), ta_peer[2])
                else:
                    got(r.rows_all.at[q, source[s]], r.rowz_sem, (1, s), ea_peer[s])
        else:
            if p == 1:
                got(r.gate_near, r.gatet_sem, 0, ta_peer[1])
            for s in range(ea):
                if s not in sz.dy_relay:
                    got(r.dy_all.at[q, source[s]], r.dyt_sem, (p, s), ta_peer[p])
                if s not in sz.relay:
                    got(r.rows_all.at[q, source[s]], r.rowt_sem, (p, s), ta_peer[p])
            if p == 1:
                for copy in row_relays:
                    copy.wait_send()
        if sz.chunks == 1:
            expert_chunk(q, p, 0)
            if p == 0:
                weight_chunk(q, p, 0, True)
        else:
            if p == 0:
                r.up_acc[...] = jnp.zeros((d, sz.hidden), F32)
                r.down_acc[...] = jnp.zeros((sz.hidden, d), F32)
                r.bias_acc[...] = jnp.zeros((8, d), F32)

            @pl.loop(0, sz.chunks)
            def _(chunk):
                expert_chunk(q, p, chunk)
                weight_chunk(q, p, chunk, False)

        if p:
            go(r.dg_send.at[p], r.dg_in.at[p], r.dg_sem, p, ta_peer[p])
        group = fine[:early_planes]
        if p == 3:
            share_diagonal(r.dy_all, r.rg_relay, r.rg_sem, group)
        elif p:
            share_straight(r.dy_all, r.rg_in, r.rg_sem, group, p)
    first_sent = list(started)
    for p in (1, 2):
        share_joined(r.dy_all, r.rg_in, r.rg_relay, r.rg_sem, group, p)
    if sz.chunks == 1:
        weight_chunk(quarter[3], 3, 0, False)
    group = fine[early_planes:]
    for copy in first_sent:
        copy.wait_send()
    if group:
        share_diagonal(r.dy_all, r.rg_relay, r.rg_sem, group)
        for p in (1, 2):
            share_straight(r.dy_all, r.rg_in, r.rg_sem, group, p)
    if sz.chunks == 1:
        weight_chunk(quarter[1], 1, 0, False)
    for p in (1, 2):
        share_joined(r.dy_all, r.rg_in, r.rg_relay, r.rg_sem, group, p)

    home_copies = []
    for p in partners:
        got(r.dg_in.at[p], r.dg_sem, p, ta_peer[p])

    def send_home(planes):
        for s in planes:
            g = target[s]
            if sz.direct or s == blocks[0]:
                share_got(r.rg_in, r.rg_sem, *((s, g) if sz.direct else whole[0]))
            share = share_sum(r.dy_all, r.rg_in, g)
            dgate = r.dg_send[0, g]
            for p in partners:
                dgate = dgate + r.dg_in[p, g]
            if s:
                r.rgz_send[g] = share.astype(BF16)
                r.dgz_send[g] = dgate
                go(r.dgz_send.at[g], r.dg_back.at[z], r.dgz_sem, s, ea_peer[s])
                home_copies.append(go(r.rgz_send.at[g], r.rg_back.at[z], r.rgz_sem, s, ea_peer[s]))
            else:
                r.rg_back[z] = share.astype(BF16)
                r.dg_back[z] = dgate

    send_home(blocks[:early_planes])
    if sz.chunks == 1:
        weight_chunk(quarter[2], 2, 0, False)
    send_home(blocks[early_planes:])
    share_diagonal(r.rows_all, r.eo_relay, r.eo_sem, whole)
    for p in (1, 2):
        share_straight(r.rows_all, r.eo_in, r.eo_sem, whole, p)

    r.up_low[...] = r.up_acc[...].astype(BF16)
    r.down_low[...] = r.down_acc[...].astype(BF16)
    go(r.up_low, r.up_in, r.rep_sem, 0, other)
    go(r.down_low, r.down_in, r.rep_sem, 1, other)
    go(r.bias_acc, r.bias_in, r.rep_sem, 2, other)

    place_0, place_1 = r.place_col[:, 0:1], r.place_col[:, 1:2]
    lane = iota((qt, sz.experts * cs), 1)
    back = onehot((lane == place_0) | (lane == place_1)).astype(BF16)
    for s in later:
        got(r.dg_back.at[source[s]], r.dgz_sem, s, ea_peer[s])
        got(r.rg_back.at[source[s]], r.rgz_sem, s, ea_peer[s])

    drouter = jnp.zeros((sz.ep, qt), F32)
    for expert in range(sz.experts):
        level = mm(r.dg_back[expert][:, 0:cs], slots_of(expert, 0), NN, EXACT)
        drouter = drouter + jnp.where(iota((sz.ep, 1), 0) == expert, level[0:1], 0.0)
    router = r.probs[...]
    dlogits = (router * (drouter - jnp.sum(router * drouter, axis=0, keepdims=True))).astype(BF16)
    into_two = mm(back, r.rg_back[...].reshape(sz.experts * cs, d)) + mm(dlogits, router_w, TN)
    _, hat_two, inv_two = layer_norm(r.hidden[...], flat_row(r.gain2), flat_row(r.bias2))
    dhidden = r.dy_mine[...].astype(F32) + norm_back(into_two, hat_two, inv_two, flat_row(r.gain2))
    r.dhidden[...] = dhidden
    dattn = dhidden.astype(BF16)
    r.da_all[j] = dattn
    for p in partners:
        go(r.da_all.at[j], r.da_all.at[j], r.da_sem, p, ta_peer[p])
    router_grad = mm(dlogits, r.b_low[...])
    rows_at = iota((sz.early, 1), 0)
    early = jnp.where(rows_at < sz.experts, fit(router_grad, sz.early), 0.0)
    for offset, values in enumerate((into_two * hat_two, into_two, dattn.astype(F32))):
        total = jnp.sum(values, axis=0, keepdims=True)
        early = early + jnp.where(rows_at == sz.experts + offset, total, 0.0)

    def small_start(values, by_ta, sem):
        by_ta[j] = values
        for p in partners:
            go(by_ta.at[j], by_ta.at[j], sem, (0, p), ta_peer[p])

    def small_middle(by_ta, by_dev, sem, own_rows):
        for p in partners:
            got(by_ta.at[quarter[p]], sem, (0, p), ta_peer[p])
        total = by_ta[0]
        for q in range(1, nq):
            total = total + by_ta[q]
        if own_rows:
            total = jnp.where(iota((8, 1), 0) < 2, total, by_ta[j])
        by_dev[c] = total
        go(by_dev.at[c], by_dev.at[c], sem, (1, 0), other)

    def small_last(by_dev, by_ea, sem):
        got(by_dev.at[1 - c], sem, (1, 0), other)
        by_ea[z] = by_dev[0] + by_dev[1]
        for s in later:
            go(by_ea.at[z], by_ea.at[z], sem, (2, s), ea_peer[s])

    def small_end(by_ea, out, sem):
        for s in later:
            got(by_ea.at[source[s]], sem, (2, s), ea_peer[s])
        total = by_ea[0]
        for e in range(1, ea):
            total = total + by_ea[e]
        out[...] = total

    if sz.direct:
        small_start(early, r.early_ta, r.early_sem)
    else:
        r.o_early[...] = early

    for p in partners:
        got(r.da_all.at[quarter[p]], r.da_sem, p, ta_peer[p])
    for p in (1, 2):
        share_joined(r.rows_all, r.eo_in, r.eo_relay, r.eo_sem, whole, p)
    if sz.direct:
        small_middle(r.early_ta, r.early_dev, r.early_sem, False)

    unpick = onehot(iota((sz.tp, nq * qt), 1) == r.perm_col[:, 0:1].astype(jnp.int32)).astype(BF16)
    dattn = mm(unpick, r.da_all[...].reshape(nq * qt, d)).astype(BF16)
    w_out = r.w_out[...].reshape(sz.inner, d)
    dmixed = mm(dattn, w_out, NT).astype(BF16).reshape(flat)

    spans = (pl.ds(0, 1), pl.ds(1, 3))

    def piece_start(n, values):
        r.pd_send[n] = values.reshape(2, sz.half, d).astype(BF16)

    def piece_send(n):
        go(r.pd_send.at[spans[n], 1 - c], r.pd_in.at[spans[n]], r.pd_sem, n, other)

    def piece_middle(n):
        span = spans[n]
        got(r.pd_in.at[span], r.pd_sem, n, other)
        for k in ((0,), (1, 2, 3))[n]:
            both = r.pd_send[k, c].astype(F32) + r.pd_in[k].astype(F32)
            for e in range(ea):
                r.pz_send[k, e] = both[e * sz.piece : (e + 1) * sz.piece].astype(BF16)
            r.pz_in[k, z] = r.pz_send[k, z]
        for s in later:
            go(r.pz_send.at[span, target[s]], r.pz_in.at[span, z], r.pz_sem, (n, s), ea_peer[s])

    def piece_last(n):
        span = spans[n]
        for s in later:
            got(r.pz_in.at[span, source[s]], r.pz_sem, (n, s), ea_peer[s])
        for k in ((0,), (1, 2, 3))[n]:
            total = r.pz_in[k, 0].astype(F32)
            for e in range(1, ea):
                total = total + r.pz_in[k, e].astype(F32)
            r.p_all[k, c, z] = total.astype(BF16)
        block = r.p_all.at[span, c, z]
        for s in later:
            go(block, block, r.pa_sem, (n, s), ea_peer[s])
        go(block, block, r.pb_sem, (n, 0), other)

    def piece_pass(n):
        for s in later:
            block = r.p_all.at[spans[n], c, source[s]]
            got(block, r.pa_sem, (n, s), ea_peer[s])
            go(block, block, r.pb_sem, (n, s), other)

    def piece_end(n):
        for s in range(ea):
            got(r.p_all.at[spans[n], 1 - c, source[s]], r.pb_sem, (n, s), other)

    if not sz.direct:

        def piece_start(n, values):
            r.o_piece[n] = values

        piece_send = piece_middle = piece_last = piece_pass = piece_end = lambda n: None

    piece_start(0, mm(r.mixed[...].reshape(sz.tp, sz.inner), dattn, TN))
    piece_send(0)
    if sz.direct:
        small_last(r.early_dev, r.early_ea, r.early_sem)

    def attention_back(image):
        dmix = stack(dmixed[image])
        probs = r.kept_probs[image] if sz.direct else attention_probs(image)
        dprobs = mm(dmix, r.v[image], NT)
        dvalue = mm(probs.astype(BF16), dmix, TN)
        inner = jnp.sum(probs * dprobs, axis=-1, keepdims=True)
        dscores = (probs * (dprobs - inner)).astype(BF16)
        dquery = unstack(mm(dscores, r.k[image])) * scale
        dkey = mm(dscores, stack(r.q[image]), TN) * scale
        for n, values in enumerate((dquery, dkey, dvalue)):
            r.dproj[n, image] = values.astype(BF16)

    attention_back(0)
    piece_middle(0)
    for image in range(1, sz.images):
        attention_back(image)
    dproj = [r.dproj[n].reshape(sz.tp, sz.inner) for n in range(3)]
    for n in (2, 0, 1):
        piece_start(n + 1, mm(dproj[n], r.a_low[...], TN))
    piece_send(1)
    share_got(r.eo_in, r.eo_sem, *whole[0])
    for copy in home_copies:
        copy.wait_send()
    for s in later + [0]:
        g = target[s]
        share = share_sum(r.rows_all, r.eo_in, g)
        if s:
            r.rgz_send[g] = share.astype(BF16)
            go(r.rgz_send.at[g], r.eo_back.at[z], r.eoz_sem, s, ea_peer[s])
        else:
            r.eo_back[z] = share.astype(BF16)

    piece_last(0)
    into_part = mm(dproj[0], r.qkv_w[0]) + mm(dproj[1], r.qkv_w[1]) + mm(dproj[2], r.qkv_w[2])
    r.in_send[...] = mm(pick_all, into_part.astype(BF16)).astype(BF16).reshape(nq, qt, d)
    for p in partners:
        go(r.in_send.at[quarter[p]], r.in_part.at[j], r.ip_sem, p, ta_peer[p])
    r.in_part[j] = r.in_send[j]
    _, hat_one, _ = layer_norm(r.padded[...].reshape(sz.tp, d).astype(F32), flat_row(r.gain1), flat_row(r.bias1))
    rows_at = iota((8, 1), 0)
    late = jnp.where(rows_at == 0, jnp.sum(into_part * hat_one, axis=0, keepdims=True), 0.0)
    late = late + jnp.where(rows_at == 1, jnp.sum(into_part, axis=0, keepdims=True), 0.0)
    for row, n in ((2, 0), (3, 2)):
        total = jnp.sum(dproj[n].astype(F32), axis=0, keepdims=True)
        wide = jnp.concatenate([total, jnp.zeros((1, d - sz.inner), F32)], axis=1)
        late = late + jnp.where(rows_at == row, wide, 0.0)
    if sz.direct:
        small_start(late, r.late_ta, r.late_sem)
    else:
        r.o_late[...] = late
    piece_middle(1)
    keeps = []
    for n, own, taken, out in ((0, r.up_low, r.up_in, r.o_up), (1, r.down_low, r.down_in, r.o_down)):
        got(taken, r.rep_sem, n, other)
        taken[...] = (own[...].astype(F32) + taken[...].astype(F32)).astype(BF16)
        keeps.append(pltpu.make_async_copy(taken, out, r.load_sem.at[n]))
        keeps[-1].start()
    got(r.bias_in, r.rep_sem, 2, other)
    r.o_bias[...] = r.bias_acc[...] + r.bias_in[...]
    if sz.direct:
        small_middle(r.late_ta, r.late_dev, r.late_sem, True)

    for p in partners:
        got(r.in_part.at[quarter[p]], r.ip_sem, p, ta_peer[p])
    into_one = r.in_part[0].astype(F32)
    for q in range(1, nq):
        into_one = into_one + r.in_part[q].astype(F32)
    x_mine = mm(pick_of(j), r.padded[...].reshape(sz.tp, d))
    _, hat_mine, inv_mine = layer_norm(x_mine, flat_row(r.gain1), flat_row(r.bias1))
    grad = r.dhidden[...] + norm_back(into_one, hat_mine, inv_mine, flat_row(r.gain1))
    r.ig_all[j] = grad.astype(BF16)
    for p in partners:
        go(r.ig_all.at[j], r.ig_all.at[j], r.ig_sem, p, ta_peer[p])
    if sz.direct:
        small_last(r.late_dev, r.late_ea, r.late_sem)

    for s in later:
        got(r.eo_back.at[source[s]], r.eoz_sem, s, ea_peer[s])
    output = r.hidden[...] + mm(back, r.eo_back[...].reshape(sz.experts * cs, d))
    r.out_all[j] = output.astype(BF16)
    for p in partners:
        go(r.out_all.at[j], r.out_all.at[j], r.out_sem, p, ta_peer[p])
    piece_last(1)
    piece_pass(0)
    piece_pass(1)
    stores = []

    def store(n, values, src, dst):
        src[...] = values.reshape(src.shape)
        stores.append(pltpu.make_async_copy(src, dst, r.load_sem.at[n]))
        stores[-1].start()

    for p in partners:
        got(r.ig_all.at[quarter[p]], r.ig_sem, p, ta_peer[p])
    store(2, mm(unpick, r.ig_all[...].reshape(nq * qt, d)).astype(BF16), r.a_low, r.o_in)
    for p in partners:
        got(r.out_all.at[quarter[p]], r.out_sem, p, ta_peer[p])
    store(3, mm(unpick, r.out_all[...].reshape(nq * qt, d)).astype(BF16), r.padded, r.o_out)
    if sz.direct:
        small_end(r.early_ea, r.o_early, r.early_sem)
        small_end(r.late_ea, r.o_late, r.late_sem)
    piece_end(0)
    piece_end(1)
    for copy in stores + keeps:
        copy.wait()
    for copy in started[-pool:]:
        copy.wait_send()
    assert len(receive) <= sz.arrivals, len(receive)


def flat_row(ref):
    return ref[...].reshape(1, -1)


def fit(values, rows):
    have = values.shape[0]
    if have >= rows:
        return values[:rows]
    return jnp.concatenate([values, jnp.zeros((rows - have, values.shape[1]), F32)])


def run_block(sz, inputs):
    nq, ea, d, cs, qt = sz.nq, sz.ea, sz.d, sz.cs, sz.qt
    dma = pltpu.SemaphoreType.DMA
    rows = sz.blocks * cs
    outs = dict(
        o_out=((sz.images, sz.lp, d), BF16),
        o_in=((sz.tp, d), BF16),
        o_early=((sz.early, d), F32),
        o_late=((8, d), F32),
        o_up=((d, sz.hidden), BF16),
        o_down=((sz.hidden, d), BF16),
        o_bias=((8, d), F32),
    )
    flat = (sz.images, sz.lp, sz.inner)
    block = (cs, d)
    buffers = dict(
        tok_v=((sz.images, sz.length, d), BF16),
        cot_v=((sz.images, sz.length, d), BF16),
        qkv_w=((3, sz.inner, d), BF16),
        up_w=((d, sz.hidden), BF16),
        down_w=((sz.hidden, d), BF16),
        w_full=((nq, 2, sz.half, d), BF16),
        padded=((sz.images, sz.lp, d), BF16),
        perm_col=((sz.tp, 128), F32),
        place_row=((4, qt), jnp.int32),
        place_col=((qt, 128), jnp.int32),
        a_low=((sz.tp, d), BF16),
        q=(flat, BF16),
        k=(flat, BF16),
        v=(flat, BF16),
        mixed=(flat, BF16),
        dproj=((3,) + flat, BF16),
        mix_send=((nq, qt, sz.inner), BF16),
        mix_in=((2, nq, qt, sz.inner), BF16),
        dy_mine=((qt, d), BF16),
        hidden=((qt, d), F32),
        dhidden=((qt, d), F32),
        b_low=((qt, d), BF16),
        probs=((sz.ep, qt), F32),
        dy_send=((2, ea) + block, BF16),
        gate_send=((ea, 2, 8, 128), F32),
        dy_all=((nq, ea) + block, BF16),
        rows_all=((nq, ea) + block, BF16),
        gate_in=((ea, 2, 8, 128), F32),
        gate_near=((ea, 2, 8, 128), F32),
        act_t=((sz.kept, rows, sz.hidden), BF16),
        pre_t=((sz.kept, rows, sz.hidden), BF16),
        slot_t=((sz.kept, rows, d), BF16),
        out_t=((sz.kept, rows, d), BF16),
        dg_send=((nq, ea, 8, 128), F32),
        dg_in=((nq, ea, 8, 128), F32),
        rg_in=((2, ea) + block, BF16),
        rg_relay=((2, ea, cs // 2, d), BF16),
        eo_in=((2, ea) + block, BF16),
        eo_relay=((2, ea, cs // 2, d), BF16),
        rgz_send=((ea,) + block, BF16),
        dgz_send=((ea, 8, 128), F32),
        rg_back=((ea,) + block, BF16),
        eo_back=((ea,) + block, BF16),
        dg_back=((ea, 8, 128), F32),
        up_acc=((d, sz.hidden), F32),
        down_acc=((sz.hidden, d), F32),
        bias_acc=((8, d), F32),
        up_low=((d, sz.hidden), BF16),
        down_low=((sz.hidden, d), BF16),
        up_in=((d, sz.hidden), BF16),
        down_in=((sz.hidden, d), BF16),
        bias_in=((8, d), F32),
        da_all=((nq, qt, d), BF16),
        ig_all=((nq, qt, d), BF16),
        out_all=((nq, qt, d), BF16),
        in_send=((nq, qt, d), BF16),
        in_part=((nq, qt, d), BF16),
    )
    if sz.direct:
        outs["p_all"] = ((4, 2, ea, sz.piece, d), BF16)
        buffers |= dict(
            early_ta=((nq, sz.early, d), F32),
            early_dev=((2, sz.early, d), F32),
            early_ea=((ea, sz.early, d), F32),
            late_ta=((nq, 8, d), F32),
            late_dev=((2, 8, d), F32),
            late_ea=((ea, 8, d), F32),
            pd_send=((4, 2, sz.half, d), BF16),
            pd_in=((4, sz.half, d), BF16),
            pz_send=((4, ea, sz.piece, d), BF16),
            pz_in=((4, ea, sz.piece, d), BF16),
        )
    else:
        outs["o_piece"] = ((4, sz.inner, d), F32)
    if sz.direct:
        buffers["row_send"] = ((2, ea) + block, BF16)
        buffers["kept_probs"] = ((sz.images, sz.heads * sz.lp, sz.lp), F32)
    names = list(inputs) + list(outs) + list(buffers) + ["sent", "arrived", "load_sem"]
    vm = pl.BlockSpec(memory_space=pltpu.VMEM)
    far = pl.BlockSpec(memory_space=pltpu.HBM)
    results = pl.pallas_call(
        functools.partial(block_kernel, sz, names),
        out_shape=[jax.ShapeDtypeStruct(*spec) for spec in outs.values()],
        in_specs=[far if name in ("tok", "cot", "w_qkv", "w_up", "w_down") else vm for name in inputs],
        out_specs=[far if name in ("o_up", "o_down", "o_in", "o_out") else vm for name in outs],
        scratch_shapes=[pltpu.VMEM(*spec) for spec in buffers.values()]
        + [dma((sz.pool,)), dma((sz.arrivals,)), dma((5,))],
        name="block",
        compiler_params=pltpu.CompilerParams(
            collective_id=0, has_side_effects=True, vmem_limit_bytes=60 << 20
        ),
    )(*inputs.values())
    return dict(zip(outs, results))


def finish_kernel(sz, names, *refs):
    r = types.SimpleNamespace(**dict(zip(names, refs)))
    n, d = sz.experts, sz.d
    loads, stores = [], []

    def load(src, dst):
        loads.append(pltpu.make_async_copy(src, dst, r.sem_in.at[len(loads)]))
        loads[-1].start()

    def store(src, dst):
        stores.append(pltpu.make_async_copy(src, dst, r.sem_out.at[len(stores)]))
        stores[-1].start()

    third = d // 3
    spans = [pl.ds(k * third, third) for k in range(3)]
    for src, dst in ((r.up, r.up_v), (r.down, r.down_v)):
        for span in spans:
            load(src.at[span], dst.at[span])
    load(r.grad, r.grad_v)
    load(r.out, r.out_v)
    load(r.piece, r.piece_v)
    for dst, src in (
        (r.f_b, r.early[n + 2 : n + 3]),
        (r.f_g1, r.late[0:1]),
        (r.f_c1, r.late[1:2]),
        (r.f_g2, r.early[n : n + 1]),
        (r.f_c2, r.early[n + 1 : n + 2]),
    ):
        dst[...] = src.reshape(d)
    r.f_router[...] = r.early[0:n]
    r.f_qv[...] = r.late[2:4, 0 : sz.inner]
    r.f_upb[...] = r.bias[0:1]
    r.f_downb[...] = r.bias[1:2]
    at = 0
    for src, wide, dst in ((r.up_v, r.up_w, r.f_up), (r.down_v, r.down_w, r.f_down)):
        for span in spans:
            loads[at].wait()
            at += 1
            wide[span] = src[span].astype(F32)
            store(wide.at[span], dst.at[span])
    loads[at].wait()
    for image in range(sz.images):
        r.grad_w[:, image, :] = r.grad_v[image * sz.lp : image * sz.lp + sz.length].astype(F32)
    store(r.grad_w, r.f_grad)
    loads[at + 1].wait()
    for image in range(sz.images):
        r.out_w[:, image, :] = r.out_v[image, 0 : sz.length]
    store(r.out_w, r.f_out)
    loads[at + 2].wait()
    for k in range(4):
        for core in range(2):
            for e in range(sz.ea):
                start = core * sz.half + e * sz.piece
                r.piece_w[k, start : start + sz.piece] = r.piece_v[k, core, e].astype(F32)
        store(r.piece_w.at[k], r.f_qkv.at[k - 1] if k else r.f_o)
    for copy in stores:
        copy.wait()


def finish(sz, got):
    d, n = sz.d, sz.experts
    inputs = dict(
        up=got["o_up"],
        down=got["o_down"],
        out=got["o_out"],
        grad=got["o_in"],
        piece=got["p_all"],
        early=got["o_early"],
        late=got["o_late"],
        bias=got["o_bias"],
    )
    outs = dict(
        f_out=((sz.length, sz.images, d), BF16),
        f_grad=((sz.length, sz.images, d), F32),
        f_qkv=((3, sz.inner, d), F32),
        f_qv=((2, sz.inner), F32),
        f_o=((sz.inner, d), F32),
        f_b=((d,), F32),
        f_g1=((d,), F32),
        f_c1=((d,), F32),
        f_g2=((d,), F32),
        f_c2=((d,), F32),
        f_router=((n, d), F32),
        f_up=((d, sz.hidden), F32),
        f_upb=((1, sz.hidden), F32),
        f_down=((sz.hidden, d), F32),
        f_downb=((1, d), F32),
    )
    buffers = dict(
        up_v=((d, sz.hidden), BF16),
        down_v=((sz.hidden, d), BF16),
        grad_v=((sz.tp, d), BF16),
        out_v=((sz.images, sz.lp, d), BF16),
        piece_v=((4, 2, sz.ea, sz.piece, d), BF16),
        up_w=((d, sz.hidden), F32),
        down_w=((sz.hidden, d), F32),
        grad_w=((sz.length, sz.images, d), F32),
        out_w=((sz.length, sz.images, d), BF16),
        piece_w=((4, sz.inner, d), F32),
    )
    vm = pl.BlockSpec(memory_space=pltpu.VMEM)
    far = pl.BlockSpec(memory_space=pltpu.HBM)
    large = ("up", "down", "out", "grad", "piece", "f_out", "f_grad", "f_qkv", "f_o", "f_up", "f_down")
    names = list(inputs) + list(outs) + list(buffers) + ["sem_in", "sem_out"]
    results = pl.pallas_call(
        functools.partial(finish_kernel, sz, names),
        out_shape=[jax.ShapeDtypeStruct(*spec) for spec in outs.values()],
        in_specs=[far if name in large else vm for name in inputs],
        out_specs=[far if name in large else vm for name in outs],
        scratch_shapes=[pltpu.VMEM(*spec) for spec in buffers.values()]
        + [pltpu.SemaphoreType.DMA((16,)), pltpu.SemaphoreType.DMA((16,))],
        name="finish",
        compiler_params=pltpu.CompilerParams(vmem_limit_bytes=60 << 20),
    )(*inputs.values())
    (out, grad, qkv, qv, o, b, g1, c1, g2, c2, router, up, up_b, down, down_b) = results
    turn = lambda t: jnp.swapaxes(t, 0, 1)
    return (
        turn(out),
        turn(grad),
        jnp.swapaxes(qkv, 1, 2),
        qv,
        o,
        b,
        g1,
        c1,
        g2,
        c2,
        router.T,
        up[None],
        up_b,
        down[None],
        down_b,
    )


def local(
    tokens,
    expert_ids,
    pair_ranks,
    cotangent,
    w_qkv,
    b_qv,
    w_out,
    b_out,
    ln1_gain,
    ln1_bias,
    ln2_gain,
    ln2_bias,
    w_router,
    w_up,
    b_up,
    w_down,
    b_down,
):
    sz = Sizes(tokens, expert_ids, w_qkv, w_up)
    inputs = dict(
        tok=tokens,
        cot=cotangent,
        w_qkv=jnp.swapaxes(w_qkv, 1, 2),
        b_qv=b_qv,
        w_out=w_out.reshape(2, sz.half, sz.d),
        b_out=b_out,
        gain1=ln1_gain,
        bias1=ln1_bias,
        gain2=ln2_gain,
        bias2=ln2_bias,
        router=w_router.T,
        w_up=w_up[0],
        b_up=b_up,
        w_down=w_down[0],
        b_down=b_down,
        ids=jnp.transpose(expert_ids, (0, 2, 1)),
        ranks=jnp.transpose(pair_ranks, (0, 2, 1)),
    )
    got = run_block(sz, inputs)
    if sz.direct:
        return finish(sz, got)
    n = sz.experts
    piece, shared = lax.psum((got["o_piece"], got["o_late"][2:4]), ("ea", "dev"))
    early, late = lax.psum((got["o_early"], got["o_late"][:2]), ("ea", "ta", "dev"))
    return (
        got["o_out"][:, : sz.length],
        got["o_in"].reshape(got["o_out"].shape)[:, : sz.length].astype(F32),
        jnp.swapaxes(piece[1:], 1, 2),
        shared[:, : sz.inner],
        piece[0],
        early[n + 2],
        late[0],
        late[1],
        early[n],
        early[n + 1],
        early[:n].T,
        got["o_up"].astype(F32)[None],
        got["o_bias"][0:1],
        got["o_down"].astype(F32)[None],
        got["o_bias"][1:2],
    )


def solution(mesh):
    in_specs = (
        P(("ea", "dev"), None, None),
        P(("ea", "dev"), None, None),
        P(("ea", "dev"), None, None),
        P(("ea", "dev"), None, None),
        P(None, None, "ta"),
        P(None, "ta"),
        P("ta", None),
        P(),
        P(),
        P(),
        P(),
        P(),
        P(),
        P("ea", None, "ta"),
        P("ea", "ta"),
        P("ea", "ta", None),
        P("ea", None),
    )
    out_specs = (
        P(("ea", "dev"), None, None),
        P(("ea", "dev"), None, None),
        P(None, None, "ta"),
        P(None, "ta"),
        P("ta", None),
        P(),
        P(),
        P(),
        P(),
        P(),
        P(),
        P("ea", None, "ta"),
        P("ea", "ta"),
        P("ea", "ta", None),
        P("ea", None),
    )
    return jax.shard_map(local, mesh=mesh, in_specs=in_specs, out_specs=out_specs, check_vma=False)
```

```python
import functools
import types

import jax
import jax.numpy as jnp
from jax import lax
from jax.experimental import pallas as pl
from jax.experimental.pallas import tpu as pltpu
from jax.sharding import PartitionSpec as P

HDIM = 64
EPSILON = 1e-06
F32, BF16 = jnp.float32, jnp.bfloat16
EXACT = lax.Precision.HIGHEST
MESH = pl.DeviceIdType.MESH
NT = (((1,), (1,)), ((), ()))
TN = (((0,), (0,)), ((), ()))
NN = (((1,), (0,)), ((), ()))


def ceil_to(value, unit):
    return -(-value // unit) * unit


def mm(a, b, dims=NN, precision=None):
    return lax.dot_general(a, b, dims, precision=precision, preferred_element_type=F32)


def iota(shape, dim):
    return lax.broadcasted_iota(jnp.int32, shape, dim)


def onehot(mask):
    return jnp.where(mask, 1.0, 0.0).astype(F32)


class Sizes:
    def __init__(self, tokens, expert_ids, w_qkv, w_up):
        self.images, self.length, self.d = tokens.shape
        self.top = expert_ids.shape[2]
        self.tokens = self.images * self.length
        self.ea = lax.axis_size("ea")
        self.nq = lax.axis_size("ta")
        assert w_up.shape[0] == 1
        self.experts = self.ea
        self.cap = (9 * self.tokens * self.top + 8 * self.experts - 1) // (8 * self.experts)
        self.inner = w_qkv.shape[2]
        self.heads = self.inner // HDIM
        self.hidden = w_up.shape[2]
        self.lp = ceil_to(self.length, 16)
        self.tp = self.images * self.lp
        per_quarter = -(-self.tokens // self.nq)
        self.qt = ceil_to(per_quarter, 8)
        spread = (self.cap + (self.nq - 1) * self.experts) // self.nq
        self.cs = ceil_to(min(self.cap, per_quarter, spread), 16)
        self.ep = ceil_to(self.experts, 16)
        self.half = self.inner // 2
        self.piece = self.half // self.ea
        self.early = ceil_to(self.experts + 3, 8)
        self.blocks = max(1, min(self.ea, (256 if self.ea <= 8 else 64) // self.cs))
        self.chunks = self.ea // self.blocks
        self.direct = self.ea <= 8
        self.relay = [2] if self.direct else []
        self.dy_relay = [2] if self.direct else []
        self.kept = self.nq if self.chunks == 1 else 1
        self.pool = 40
        self.arrivals = 145 if self.direct else 48 + 13 * self.ea
        assert self.top == 2 and self.nq == 4 and self.experts * self.nq <= 128


def pair_table(sz, ids, ranks):
    wide = ceil_to(sz.tp, 128)
    spread, inside = jnp.zeros((8, wide), F32), jnp.zeros((1, wide), F32)
    for image in range(sz.images):
        experts, rank = ids[image].astype(F32), ranks[image].astype(F32)
        high = jnp.floor(rank * (1.0 / 64))
        rows = jnp.concatenate([experts, high, rank - high * 64, jnp.zeros_like(rank)], axis=0)
        lane = iota((sz.length, wide), 1)
        move = onehot(lane == iota((sz.length, wide), 0) + image * sz.lp).astype(BF16)
        spread = spread + mm(rows.astype(BF16), move)
        at = iota((1, wide), 1) - image * sz.lp
        inside = inside + onehot((at >= 0) & (at < sz.length))
    rank = spread[2:4] * 64 + spread[4:6]
    table = jnp.concatenate([spread[0:2], rank, jnp.zeros((4, wide), F32)], axis=0)
    return jnp.where(inside > 0, table, float(2 * sz.tokens))


def route(sz, table):
    cols = table.T[: sz.tp]
    wide = iota((sz.tp, 128), 1)
    lane = wide.astype(F32)

    def flip(*columns):
        spread = jnp.zeros((sz.tp, 128), F32)
        for n, column in enumerate(columns):
            spread = spread + jnp.where(wide == n, column, 0.0)
        turned = spread.T
        return [turned[n : n + 1] for n in range(len(columns))]

    def total(values):
        return jnp.sum(values, axis=1, keepdims=True)

    ids = [cols[:, k : k + 1] for k in range(2)]
    real = ids[0] < sz.experts
    member = [onehot(lane == column) for column in ids]
    dest = []
    for k in range(2):
        before = jnp.zeros((sz.tp, 128), F32)
        for m in range(2):
            mask = onehot(table[2 + m : 3 + m, : sz.tp] < cols[:, 2 + k : 3 + k])
            before = before + mm(mask.astype(BF16), member[m].astype(BF16))
        kept = (total(before * member[k]) < sz.cap) & real
        dest.append(jnp.where(kept, ids[k], float(sz.experts)))
    low, high = jnp.minimum(*dest), jnp.maximum(*dest)
    index = iota((sz.tp, 1), 0).astype(F32)
    kind = jnp.where(real, low * (sz.experts + 1) + high, float((sz.experts + 1) ** 2))
    key = kind * sz.tp + index
    (key_row,) = flip(key)
    earlier = onehot(key_row < key).astype(BF16)
    order = mm(earlier, jnp.ones((sz.tp, 128), BF16))[:, 0:1]
    lap = jnp.floor((order + 0.5) * (1.0 / sz.nq))
    quarter = order - lap * sz.nq
    perm = jnp.where(real, quarter * sz.qt + lap, -1.0)
    group = [
        onehot((lane == d * sz.nq + quarter) & (d < sz.experts)) for d in dest
    ]
    ahead = mm(earlier, (group[0] + group[1]).astype(BF16))
    place = []
    for k in range(2):
        slot = total(ahead * group[k])
        place.append(jnp.where(dest[k] < sz.experts, dest[k] * sz.cs + slot + 1.0, 0.0))
    perm_row, *place_row = flip(perm, *place)
    return perm, perm_row, place, place_row


def layer_norm(values, gain_vec, shift_vec):
    row_mean = jnp.mean(values, axis=-1, keepdims=True)
    centered = values - row_mean
    variance = jnp.mean(centered * centered, axis=-1, keepdims=True)
    inverse = lax.rsqrt(variance + EPSILON)
    normed = centered * inverse
    return (normed * gain_vec + shift_vec, normed, inverse)


def norm_back(grad_rows, normed, inverse, gain_vec):
    scaled = grad_rows * gain_vec
    return inverse * (
        scaled
        - jnp.mean(scaled, axis=-1, keepdims=True)
        - normed * jnp.mean(scaled * normed, axis=-1, keepdims=True)
    )


def push(src, dst, send_sem, recv_sem, device):
    return pltpu.make_async_remote_copy(
        src_ref=src,
        dst_ref=dst,
        send_sem=send_sem,
        recv_sem=recv_sem,
        device_id=device,
        device_id_type=MESH,
    )


def greet(devices):
    barrier = pltpu.get_barrier_semaphore()
    for device in devices:
        pl.semaphore_signal(barrier, inc=1, device_id=device, device_id_type=MESH)


def head_mask(sz, head, dtype):
    lane = iota((1, sz.inner), 1)
    return onehot((lane >= head * HDIM) & (lane < (head + 1) * HDIM)).astype(dtype)


def gelu_parts(values):
    cdf = 0.5 * (1.0 + lax.erf(values * (0.5**0.5)))
    density = jnp.exp(-0.5 * values * values) * (0.5 / jnp.pi) ** 0.5
    return cdf, density


class Sent:
    def __init__(self, copy):
        self.copy, self.done = copy, False

    def wait_send(self):
        if not self.done:
            self.copy.wait_send()
        self.done = True


class Refs(types.SimpleNamespace):
    def __getattr__(self, name):
        return name


def block_kernel(sz, names, *refs):
    r = Refs(**dict(zip(names, refs)))
    z, j, c = lax.axis_index("ea"), lax.axis_index("ta"), lax.axis_index("dev")
    nq, ea, d, cs, qt = sz.nq, sz.ea, sz.d, sz.cs, sz.qt
    quarter = [j, j + 1 - 2 * lax.rem(j, 2), j + 2 - 4 * lax.div(j, 2), 3 - j]
    ta_peer = [{"ta": q} for q in quarter]
    ea_peer = [{"ea": lax.rem(z + s, ea)} for s in range(ea)]
    source = [lax.rem(z - s + ea, ea) for s in range(ea)]
    target = [lax.rem(z + s, ea) for s in range(ea)]
    other = {"dev": 1 - c}
    later = [s for s in range(1, ea)]
    partners = (1, 2, 3)
    pool, started, receive = sz.pool, [], {}

    def go(src, dst, kind, index, device):
        at = receive.setdefault((kind, index), len(receive))
        n = len(started)
        if n >= pool:
            started[n - pool].wait_send()
        copy = push(src, dst, r.sent.at[n % pool], r.arrived.at[at], device)
        copy.start()
        started.append(Sent(copy))
        return started[-1]

    def got(dst, kind, index, device):
        at = receive.setdefault((kind, index), len(receive))
        push(dst, dst, r.sent.at[0], r.arrived.at[at], device).wait_recv()

    everyone = ta_peer[1:] + ea_peer[1:] + [other]
    greet(everyone)
    loads = []
    for n, (src, dst) in enumerate(
        ((r.cot, r.cot_v), (r.tok, r.tok_v), (r.w_qkv, r.qkv_w), (r.w_up, r.up_w), (r.w_down, r.down_w))
    ):
        loads.append(pltpu.make_async_copy(src, dst, r.load_sem.at[n]))
        loads[-1].start()
    pl.semaphore_wait(pltpu.get_barrier_semaphore(), len(everyone))

    for p in partners:
        go(r.w_out.at[c], r.w_full.at[j, c], r.w_sem, p, ta_peer[p])
    r.w_full[j] = r.w_out[...]

    perm_col, perm, place, place_rows = route(sz, pair_table(sz, r.ids, r.ranks))
    perm = perm.astype(jnp.int32)
    r.perm_col[...] = jnp.broadcast_to(perm_col, (sz.tp, 128))
    pick_all = onehot(iota((nq * qt, sz.tp), 0) == perm).astype(BF16)

    def pick_of(q):
        return onehot(iota((qt, sz.tp), 0) + q * qt == perm).astype(BF16)

    spread = iota((8, 1), 0)
    both = jnp.where(spread == 0, place_rows[0], 0.0) + jnp.where(spread == 1, place_rows[1], 0.0)
    for which, q in ((0, quarter[0]), (1, quarter[3])):
        chosen = mm(both, onehot(iota((qt, sz.tp), 0) + q * qt == perm), NT, EXACT)
        r.place_row[2 * which : 2 * which + 2] = (chosen[0:2] + 0.5).astype(jnp.int32) - 1
    pair_col = jnp.where(iota((1, 128), 1) == 0, place[0], 0.0)
    pair_col = pair_col + jnp.where(iota((1, 128), 1) == 1, place[1], 0.0)
    chosen = mm(onehot(iota((qt, sz.tp), 0) + j * qt == perm), pair_col, NN, EXACT)
    r.place_col[...] = (chosen + 0.5).astype(jnp.int32) - 1

    def slots_of(expert, which):
        row = iota((cs, qt), 0) + expert * cs
        first, second = r.place_row[2 * which : 2 * which + 1], r.place_row[2 * which + 1 : 2 * which + 2]
        return onehot((row == first) | (row == second))

    tail = (sz.length // 16) * 16
    loads[0].wait()
    for image in range(sz.images):
        r.padded[image, tail:] = jnp.zeros((sz.lp - tail, d), BF16)
        r.padded[image, 0 : sz.length] = r.cot_v[:, image, :]
    for which, q in ((0, quarter[0]), (1, quarter[3])):
        dy_rows = mm(pick_of(q), r.padded[...].reshape(sz.tp, d)).astype(BF16)
        if which == 0:
            r.dy_mine[...] = dy_rows
        for expert in range(sz.experts):
            r.dy_send[which, expert] = mm(slots_of(expert, which).astype(BF16), dy_rows).astype(BF16)
    dy_copies = []
    near_first = later[:1] + later[2:] + later[1:2]

    def send_dy(which, q, planes):
        for s in planes:
            block = r.dy_send.at[which, target[s]]
            dy_copies.append(go(block, r.dy_all.at[q, z], r.dyz_sem, (which, s), ea_peer[s]))

    send_dy(0, quarter[0], near_first)
    for which, q in ((0, quarter[0]), (1, quarter[3])):
        r.dy_all[q, z] = r.dy_send[which, z]

    def forward(ref, z_sem, t_sem, order):
        copies = []
        for s in order:
            block = ref.at[j, source[s]]
            if s:
                got(block, z_sem, (0, s), ea_peer[s])
            for p in (1, 2):
                copies.append(go(block, block, t_sem, (p, s), ta_peer[p]))
        return copies

    dy_forwards = forward(r.dy_all, r.dyz_sem, r.dyt_sem, [0])

    low_half, high_half = pl.ds(0, cs // 2), pl.ds(cs // 2, cs // 2)

    def relay(ref, t_sem, sem, planes):
        copies = []
        for s in planes:
            for p, part in ((1, high_half), (2, low_half)):
                got(ref.at[quarter[p], source[s]], t_sem, (p, s), ta_peer[p])
                half = ref.at[quarter[p], source[s], part]
                copies.append(go(half, half, sem, (3 - p, s), ta_peer[3 - p]))
        return copies

    loads[1].wait()
    loads[2].wait()
    for image in range(sz.images):
        r.padded[image, 0 : sz.length] = r.tok_v[:, image, :]
    normed_one, _, _ = layer_norm(
        r.padded[...].reshape(sz.tp, d).astype(F32), flat_row(r.gain1), flat_row(r.bias1)
    )
    a_low = normed_one.astype(BF16)
    r.a_low[...] = a_low
    flat = (sz.images, sz.lp, sz.inner)
    r.q[...] = (mm(a_low, r.qkv_w[0], NT) + r.b_qv[0:1]).astype(BF16).reshape(flat)
    r.k[...] = mm(a_low, r.qkv_w[1], NT).astype(BF16).reshape(flat)
    r.v[...] = (mm(a_low, r.qkv_w[2], NT) + r.b_qv[1:2]).astype(BF16).reshape(flat)

    for p in partners:
        block = r.w_full.at[quarter[p], c]
        got(block, r.w_sem, p, ta_peer[p])
        go(block, block, r.wd_sem, p, other)

    scale = HDIM ** (-0.5)
    live = iota((1, sz.lp), 1) < sz.length

    def stack(values):
        return jnp.concatenate([values * head_mask(sz, h, BF16) for h in range(sz.heads)], axis=0)

    def unstack(values):
        return sum(
            values[h * sz.lp : (h + 1) * sz.lp] * head_mask(sz, h, F32) for h in range(sz.heads)
        )

    def attention_probs(image):
        scores = mm(stack(r.q[image]), r.k[image], NT) * scale
        scores = jnp.where(live, scores, -1e30)
        exps = jnp.exp(scores - jnp.max(scores, axis=-1, keepdims=True))
        return exps / jnp.sum(exps, axis=-1, keepdims=True)

    for image in range(sz.images):
        probs = attention_probs(image)
        if sz.direct:
            r.kept_probs[image] = probs
        r.mixed[image] = unstack(mm(probs.astype(BF16), r.v[image])).astype(BF16)
    dealt = mm(pick_all, r.mixed[...].reshape(sz.tp, sz.inner)).astype(BF16)
    r.mix_send[...] = dealt.reshape(nq, qt, sz.inner)
    for p in partners:
        go(r.mix_send.at[quarter[p]], r.mix_in.at[0, j], r.mix_sem, (0, p), ta_peer[p])
        go(r.mix_send.at[quarter[3 - p]], r.mix_in.at[1, j], r.mix_sem, (1, p), ta_peer[p])
    for copy in list(dy_copies):
        copy.wait_send()
    send_dy(1, quarter[3], [s for s in near_first if s not in sz.dy_relay])
    dy_forwards += forward(r.dy_all, r.dyz_sem, r.dyt_sem, near_first)
    r.mix_in[0, j] = r.mix_send[j]
    r.mix_in[1, j] = r.mix_send[quarter[3]]
    x_rows = [mm(pick_of(q), r.padded[...].reshape(sz.tp, d)) for q in (quarter[0], quarter[3])]
    for p in partners:
        got(r.w_full.at[quarter[p], 1 - c], r.wd_sem, p, other)
    for p in partners:
        got(r.mix_in.at[0, quarter[p]], r.mix_sem, (0, p), ta_peer[p])
        got(r.mix_in.at[1, quarter[p]], r.mix_sem, (1, p), ta_peer[p])

    if not sz.direct:
        r.row_send = r.dy_send
        for copy in dy_copies:
            copy.wait_send()
    router_w = r.router[...]
    if sz.ep > sz.experts:
        router_w = jnp.concatenate([router_w, jnp.zeros((sz.ep - sz.experts, d), BF16)])
    def send_rows(which, q, planes):
        return [
            go(r.row_send.at[which, target[s]], r.rows_all.at[q, z], r.rowz_sem, (which, s), ea_peer[s])
            for s in planes
        ]

    for which in (0, 1):
        attention = flat_row(r.b_out)
        for q in range(nq):
            attention = attention + mm(r.mix_in[which, q], r.w_full[q].reshape(sz.inner, d))
        hidden = x_rows[which] + attention
        normed_two, _, _ = layer_norm(hidden, flat_row(r.gain2), flat_row(r.bias2))
        b_low = normed_two.astype(BF16)
        logits = mm(router_w, b_low, NT)
        logits = jnp.where(iota((sz.ep, 1), 0) < sz.experts, logits, -1e30)
        exps = jnp.exp(logits - jnp.max(logits, axis=0, keepdims=True))
        router = exps / jnp.sum(exps, axis=0, keepdims=True)
        if which == 0:
            r.hidden[...], r.b_low[...], r.probs[...] = hidden, b_low, router
        for expert in range(sz.experts):
            slots = slots_of(expert, which)
            r.row_send[which, expert] = mm(slots.astype(BF16), b_low).astype(BF16)
            level = jnp.broadcast_to(router[expert : expert + 1], (8, qt))
            r.gate_send[expert, which, :, 0:cs] = mm(level, slots, NT, EXACT)
        q = quarter[3 * which]
        if which:
            for s in later:
                go(r.gate_send.at[target[s]], r.gate_in.at[z], r.gatez_sem, s, ea_peer[s])
            r.gate_in[z] = r.gate_send[z]
        if which == 0:
            row_copies = send_rows(0, q, near_first[:-1])
        r.rows_all[q, z] = r.row_send[which, z]
    row_forwards = forward(r.rows_all, r.rowz_sem, r.rowt_sem, [0])
    for copy in row_copies:
        copy.wait_send()
    row_copies = send_rows(0, quarter[0], near_first[-1:])
    row_forwards += forward(r.rows_all, r.rowz_sem, r.rowt_sem, near_first[:-1])
    for copy in row_copies:
        copy.wait_send()
    send_rows(1, quarter[3], [s for s in near_first if s not in sz.relay])
    row_forwards += forward(r.rows_all, r.rowz_sem, r.rowt_sem, near_first[-1:])
    for s in later:
        got(r.gate_in.at[source[s]], r.gatez_sem, s, ea_peer[s])
    go(r.gate_in, r.gate_near, r.gatet_sem, 0, ta_peer[1])

    row_relays = relay(r.rows_all, r.rowt_sem, r.rowr_sem, [s for s in near_first if s in sz.relay])
    row_relays += relay(r.dy_all, r.dyt_sem, r.dyr_sem, sz.dy_relay)

    loads[3].wait()
    loads[4].wait()
    first = jnp.where(j == 0, 1.0, 0.0)
    spot = iota((cs, cs), 0) == iota((cs, cs), 1)
    rows_n = sz.blocks * cs

    def expert_chunk(q, p, chunk):
        at = pl.ds(chunk * sz.blocks, sz.blocks) if sz.chunks > 1 else slice(None)
        keep = p if sz.kept > 1 else 0
        rows = r.rows_all[q, at].reshape(rows_n, d)
        dy = r.dy_all[q, at].reshape(rows_n, d).astype(F32)
        gates = []
        for b in range(sz.blocks):
            g = chunk * sz.blocks + b
            held, which = ((r.gate_in, 0), (r.gate_near, 0), (r.gate_near, 1), (r.gate_in, 1))[p]
            level = held[g, which][0:1, 0:cs]
            gates.append(jnp.sum(jnp.where(spot, level, 0.0), axis=1, keepdims=True))
        gate = jnp.concatenate(gates, axis=0) if len(gates) > 1 else gates[0]
        pre_act = mm(rows, r.up_w[...]) + r.b_up[...]
        cdf, density = gelu_parts(pre_act)
        act_low = (pre_act * cdf).astype(BF16)
        slot_grad = (gate * dy).astype(BF16)
        pre_grad = (mm(slot_grad, r.down_w[...], NT) * (cdf + pre_act * density)).astype(BF16)
        row_grad = mm(pre_grad, r.up_w[...], NT).astype(BF16)
        r.act_t[keep], r.pre_t[keep], r.slot_t[keep] = act_low, pre_grad, slot_grad
        r.dy_all[q, at] = row_grad.reshape(sz.blocks, cs, d)
        expert_out = mm(act_low, r.down_w[...]) + first * r.b_down[...]
        r.out_t[keep] = (gate * expert_out).astype(BF16)
        dgate = jnp.sum(expert_out * dy, axis=1, keepdims=True)
        for b in range(sz.blocks):
            g = chunk * sz.blocks + b
            level = jnp.sum(
                jnp.where(spot, dgate[b * cs : (b + 1) * cs], 0.0), axis=0, keepdims=True
            )
            r.dg_send[p, g, :, 0:cs] = jnp.broadcast_to(level, (8, cs))

    def weight_chunk(q, p, chunk, fresh):
        at = pl.ds(chunk * sz.blocks, sz.blocks) if sz.chunks > 1 else slice(None)
        keep = p if sz.kept > 1 else 0
        rows = r.rows_all[q, at].reshape(rows_n, d)
        up = mm(rows, r.pre_t[keep], TN)
        down = mm(r.act_t[keep], r.slot_t[keep], TN)
        biases = jnp.concatenate(
            [
                jnp.sum(r.pre_t[keep].astype(F32), axis=0, keepdims=True),
                jnp.sum(r.slot_t[keep].astype(F32), axis=0, keepdims=True),
                jnp.zeros((6, d), F32),
            ]
        )
        if fresh:
            r.up_acc[...], r.down_acc[...], r.bias_acc[...] = up, down, biases
        else:
            r.up_acc[...] += up
            r.down_acc[...] += down
            r.bias_acc[...] += biases
        r.rows_all[q, at] = r.out_t[keep].reshape(sz.blocks, cs, d)

    parts = (None, (low_half, high_half), (high_half, low_half))
    blocks = later[1:2] + later[:1] + later[2:] + [0]
    early_planes = ea - 1

    fine = [(s, target[s]) for s in blocks] if sz.direct else [(0, slice(None))]
    whole = [(0, slice(None))]

    def share_diagonal(ref, relay_in, kind, groups):
        for s, g in groups:
            for n, p, part in ((0, 2, low_half), (1, 1, high_half)):
                half = ref.at[quarter[3], g, part]
                go(half, relay_in.at[n, g], kind, (n, s), ta_peer[p])

    def share_straight(ref, taken, kind, groups, p):
        for s, g in groups:
            half = parts[p][1]
            go(ref.at[quarter[p], g, half], taken.at[p - 1, g, half], kind, (1 + p, s), ta_peer[p])

    def share_joined(ref, taken, relay_in, kind, groups, p):
        for s, g in groups:
            half = parts[p][0]
            got(relay_in.at[p - 1, g], kind, (p - 1, s), ta_peer[3 - p])
            joined = ref[quarter[p], g, half].astype(F32) + relay_in[p - 1, g].astype(F32)
            ref[quarter[p], g, half] = joined.astype(BF16)
            go(ref.at[quarter[p], g, half], taken.at[p - 1, g, half], kind, (3 + p, s), ta_peer[p])

    def share_got(taken, kind, s, g):
        for p in (1, 2):
            got(taken.at[p - 1, g, parts[p][1]], kind, (1 + p, s), ta_peer[p])
            got(taken.at[p - 1, g, parts[p][0]], kind, (3 + p, s), ta_peer[p])

    def share_sum(ref, taken, g):
        return ref[j, g].astype(F32) + taken[0, g].astype(F32) + taken[1, g].astype(F32)

    for p in (0, 3, 1, 2):
        q = quarter[p]
        if p == 0:
            for copy in dy_forwards + row_forwards:
                copy.wait_send()
        elif p == 3:
            for s in later:
                if s in sz.dy_relay:
                    got(r.dy_all.at[q, source[s], low_half], r.dyr_sem, (1, s), ta_peer[1])
                    got(r.dy_all.at[q, source[s], high_half], r.dyr_sem, (2, s), ta_peer[2])
                else:
                    got(r.dy_all.at[q, source[s]], r.dyz_sem, (1, s), ea_peer[s])
                if s in sz.relay:
                    got(r.rows_all.at[q, source[s], low_half], r.rowr_sem, (1, s), ta_peer[1])
                    got(r.rows_all.at[q, source[s], high_half], r.rowr_sem, (2, s), ta_peer[2])
                else:
                    got(r.rows_all.at[q, source[s]], r.rowz_sem, (1, s), ea_peer[s])
        else:
            if p == 1:
                got(r.gate_near, r.gatet_sem, 0, ta_peer[1])
            for s in range(ea):
                if s not in sz.dy_relay:
                    got(r.dy_all.at[q, source[s]], r.dyt_sem, (p, s), ta_peer[p])
                if s not in sz.relay:
                    got(r.rows_all.at[q, source[s]], r.rowt_sem, (p, s), ta_peer[p])
            if p == 1:
                for copy in row_relays:
                    copy.wait_send()
        if sz.chunks == 1:
            expert_chunk(q, p, 0)
            if p == 0:
                weight_chunk(q, p, 0, True)
        else:
            if p == 0:
                r.up_acc[...] = jnp.zeros((d, sz.hidden), F32)
                r.down_acc[...] = jnp.zeros((sz.hidden, d), F32)
                r.bias_acc[...] = jnp.zeros((8, d), F32)

            @pl.loop(0, sz.chunks)
            def _(chunk):
                expert_chunk(q, p, chunk)
                weight_chunk(q, p, chunk, False)

        if p:
            go(r.dg_send.at[p], r.dg_in.at[p], r.dg_sem, p, ta_peer[p])
        group = fine[:early_planes]
        if p == 3:
            share_diagonal(r.dy_all, r.rg_relay, r.rg_sem, group)
        elif p:
            share_straight(r.dy_all, r.rg_in, r.rg_sem, group, p)
    first_sent = list(started)
    for p in (1, 2):
        share_joined(r.dy_all, r.rg_in, r.rg_relay, r.rg_sem, group, p)
    if sz.chunks == 1:
        weight_chunk(quarter[3], 3, 0, False)
    group = fine[early_planes:]
    for copy in first_sent:
        copy.wait_send()
    if group:
        share_diagonal(r.dy_all, r.rg_relay, r.rg_sem, group)
        for p in (1, 2):
            share_straight(r.dy_all, r.rg_in, r.rg_sem, group, p)
    if sz.chunks == 1:
        weight_chunk(quarter[1], 1, 0, False)
    for p in (1, 2):
        share_joined(r.dy_all, r.rg_in, r.rg_relay, r.rg_sem, group, p)

    home_copies = []
    for p in partners:
        got(r.dg_in.at[p], r.dg_sem, p, ta_peer[p])

    def send_home(planes):
        for s in planes:
            g = target[s]
            if sz.direct or s == blocks[0]:
                share_got(r.rg_in, r.rg_sem, *((s, g) if sz.direct else whole[0]))
            share = share_sum(r.dy_all, r.rg_in, g)
            dgate = r.dg_send[0, g]
            for p in partners:
                dgate = dgate + r.dg_in[p, g]
            if s:
                r.rgz_send[g] = share.astype(BF16)
                r.dgz_send[g] = dgate
                go(r.dgz_send.at[g], r.dg_back.at[z], r.dgz_sem, s, ea_peer[s])
                home_copies.append(go(r.rgz_send.at[g], r.rg_back.at[z], r.rgz_sem, s, ea_peer[s]))
            else:
                r.rg_back[z] = share.astype(BF16)
                r.dg_back[z] = dgate

    send_home(blocks[:early_planes])
    if sz.chunks == 1:
        weight_chunk(quarter[2], 2, 0, False)
    send_home(blocks[early_planes:])
    share_diagonal(r.rows_all, r.eo_relay, r.eo_sem, whole)
    for p in (1, 2):
        share_straight(r.rows_all, r.eo_in, r.eo_sem, whole, p)

    r.up_low[...] = r.up_acc[...].astype(BF16)
    r.down_low[...] = r.down_acc[...].astype(BF16)
    go(r.up_low, r.up_in, r.rep_sem, 0, other)
    go(r.down_low, r.down_in, r.rep_sem, 1, other)
    go(r.bias_acc, r.bias_in, r.rep_sem, 2, other)

    place_0, place_1 = r.place_col[:, 0:1], r.place_col[:, 1:2]
    lane = iota((qt, sz.experts * cs), 1)
    back = onehot((lane == place_0) | (lane == place_1)).astype(BF16)
    for s in later:
        got(r.dg_back.at[source[s]], r.dgz_sem, s, ea_peer[s])
        got(r.rg_back.at[source[s]], r.rgz_sem, s, ea_peer[s])

    drouter = jnp.zeros((sz.ep, qt), F32)
    for expert in range(sz.experts):
        level = mm(r.dg_back[expert][:, 0:cs], slots_of(expert, 0), NN, EXACT)
        drouter = drouter + jnp.where(iota((sz.ep, 1), 0) == expert, level[0:1], 0.0)
    router = r.probs[...]
    dlogits = (router * (drouter - jnp.sum(router * drouter, axis=0, keepdims=True))).astype(BF16)
    into_two = mm(back, r.rg_back[...].reshape(sz.experts * cs, d)) + mm(dlogits, router_w, TN)
    _, hat_two, inv_two = layer_norm(r.hidden[...], flat_row(r.gain2), flat_row(r.bias2))
    dhidden = r.dy_mine[...].astype(F32) + norm_back(into_two, hat_two, inv_two, flat_row(r.gain2))
    r.dhidden[...] = dhidden
    dattn = dhidden.astype(BF16)
    r.da_all[j] = dattn
    for p in partners:
        go(r.da_all.at[j], r.da_all.at[j], r.da_sem, p, ta_peer[p])
    router_grad = mm(dlogits, r.b_low[...])
    rows_at = iota((sz.early, 1), 0)
    early = jnp.where(rows_at < sz.experts, fit(router_grad, sz.early), 0.0)
    for offset, values in enumerate((into_two * hat_two, into_two, dattn.astype(F32))):
        total = jnp.sum(values, axis=0, keepdims=True)
        early = early + jnp.where(rows_at == sz.experts + offset, total, 0.0)

    def small_start(values, by_ta, sem):
        by_ta[j] = values
        for p in partners:
            go(by_ta.at[j], by_ta.at[j], sem, (0, p), ta_peer[p])

    def small_middle(by_ta, by_dev, sem, own_rows):
        for p in partners:
            got(by_ta.at[quarter[p]], sem, (0, p), ta_peer[p])
        total = by_ta[0]
        for q in range(1, nq):
            total = total + by_ta[q]
        if own_rows:
            total = jnp.where(iota((8, 1), 0) < 2, total, by_ta[j])
        by_dev[c] = total
        go(by_dev.at[c], by_dev.at[c], sem, (1, 0), other)

    def small_last(by_dev, by_ea, sem):
        got(by_dev.at[1 - c], sem, (1, 0), other)
        by_ea[z] = by_dev[0] + by_dev[1]
        for s in later:
            go(by_ea.at[z], by_ea.at[z], sem, (2, s), ea_peer[s])

    def small_end(by_ea, out, sem):
        for s in later:
            got(by_ea.at[source[s]], sem, (2, s), ea_peer[s])
        total = by_ea[0]
        for e in range(1, ea):
            total = total + by_ea[e]
        out[...] = total

    if sz.direct:
        small_start(early, r.early_ta, r.early_sem)
    else:
        r.o_early[...] = early

    for p in partners:
        got(r.da_all.at[quarter[p]], r.da_sem, p, ta_peer[p])
    for p in (1, 2):
        share_joined(r.rows_all, r.eo_in, r.eo_relay, r.eo_sem, whole, p)
    if sz.direct:
        small_middle(r.early_ta, r.early_dev, r.early_sem, False)

    unpick = onehot(iota((sz.tp, nq * qt), 1) == r.perm_col[:, 0:1].astype(jnp.int32)).astype(BF16)
    dattn = mm(unpick, r.da_all[...].reshape(nq * qt, d)).astype(BF16)
    w_out = r.w_out[...].reshape(sz.inner, d)
    dmixed = mm(dattn, w_out, NT).astype(BF16).reshape(flat)

    spans = (pl.ds(0, 1), pl.ds(1, 3))

    def piece_start(n, values):
        r.pd_send[n] = values.reshape(2, sz.half, d).astype(BF16)

    def piece_send(n):
        go(r.pd_send.at[spans[n], 1 - c], r.pd_in.at[spans[n]], r.pd_sem, n, other)

    def piece_middle(n):
        span = spans[n]
        got(r.pd_in.at[span], r.pd_sem, n, other)
        for k in ((0,), (1, 2, 3))[n]:
            both = r.pd_send[k, c].astype(F32) + r.pd_in[k].astype(F32)
            for e in range(ea):
                r.pz_send[k, e] = both[e * sz.piece : (e + 1) * sz.piece].astype(BF16)
            r.pz_in[k, z] = r.pz_send[k, z]
        for s in later:
            go(r.pz_send.at[span, target[s]], r.pz_in.at[span, z], r.pz_sem, (n, s), ea_peer[s])

    def piece_last(n):
        span = spans[n]
        for s in later:
            got(r.pz_in.at[span, source[s]], r.pz_sem, (n, s), ea_peer[s])
        for k in ((0,), (1, 2, 3))[n]:
            total = r.pz_in[k, 0].astype(F32)
            for e in range(1, ea):
                total = total + r.pz_in[k, e].astype(F32)
            r.p_all[k, c, z] = total.astype(BF16)
        block = r.p_all.at[span, c, z]
        for s in later:
            go(block, block, r.pa_sem, (n, s), ea_peer[s])
        go(block, block, r.pb_sem, (n, 0), other)

    def piece_pass(n):
        for s in later:
            block = r.p_all.at[spans[n], c, source[s]]
            got(block, r.pa_sem, (n, s), ea_peer[s])
            go(block, block, r.pb_sem, (n, s), other)

    def piece_end(n):
        for s in range(ea):
            got(r.p_all.at[spans[n], 1 - c, source[s]], r.pb_sem, (n, s), other)

    if not sz.direct:

        def piece_start(n, values):
            r.o_piece[n] = values

        piece_send = piece_middle = piece_last = piece_pass = piece_end = lambda n: None

    piece_start(0, mm(r.mixed[...].reshape(sz.tp, sz.inner), dattn, TN))
    piece_send(0)
    if sz.direct:
        small_last(r.early_dev, r.early_ea, r.early_sem)

    def attention_back(image):
        dmix = stack(dmixed[image])
        probs = r.kept_probs[image] if sz.direct else attention_probs(image)
        dprobs = mm(dmix, r.v[image], NT)
        dvalue = mm(probs.astype(BF16), dmix, TN)
        inner = jnp.sum(probs * dprobs, axis=-1, keepdims=True)
        dscores = (probs * (dprobs - inner)).astype(BF16)
        dquery = unstack(mm(dscores, r.k[image])) * scale
        dkey = mm(dscores, stack(r.q[image]), TN) * scale
        for n, values in enumerate((dquery, dkey, dvalue)):
            r.dproj[n, image] = values.astype(BF16)

    attention_back(0)
    piece_middle(0)
    for image in range(1, sz.images):
        attention_back(image)
    dproj = [r.dproj[n].reshape(sz.tp, sz.inner) for n in range(3)]
    for n in (2, 0, 1):
        piece_start(n + 1, mm(dproj[n], r.a_low[...], TN))
    piece_send(1)
    share_got(r.eo_in, r.eo_sem, *whole[0])
    for copy in home_copies:
        copy.wait_send()
    for s in later + [0]:
        g = target[s]
        share = share_sum(r.rows_all, r.eo_in, g)
        if s:
            r.rgz_send[g] = share.astype(BF16)
            go(r.rgz_send.at[g], r.eo_back.at[z], r.eoz_sem, s, ea_peer[s])
        else:
            r.eo_back[z] = share.astype(BF16)

    piece_last(0)
    into_part = mm(dproj[0], r.qkv_w[0]) + mm(dproj[1], r.qkv_w[1]) + mm(dproj[2], r.qkv_w[2])
    r.in_send[...] = mm(pick_all, into_part.astype(BF16)).astype(BF16).reshape(nq, qt, d)
    for p in partners:
        go(r.in_send.at[quarter[p]], r.in_part.at[j], r.ip_sem, p, ta_peer[p])
    r.in_part[j] = r.in_send[j]
    _, hat_one, _ = layer_norm(r.padded[...].reshape(sz.tp, d).astype(F32), flat_row(r.gain1), flat_row(r.bias1))
    rows_at = iota((8, 1), 0)
    late = jnp.where(rows_at == 0, jnp.sum(into_part * hat_one, axis=0, keepdims=True), 0.0)
    late = late + jnp.where(rows_at == 1, jnp.sum(into_part, axis=0, keepdims=True), 0.0)
    for row, n in ((2, 0), (3, 2)):
        total = jnp.sum(dproj[n].astype(F32), axis=0, keepdims=True)
        wide = jnp.concatenate([total, jnp.zeros((1, d - sz.inner), F32)], axis=1)
        late = late + jnp.where(rows_at == row, wide, 0.0)
    if sz.direct:
        small_start(late, r.late_ta, r.late_sem)
    else:
        r.o_late[...] = late
    piece_middle(1)
    keeps = []
    for n, own, taken, out in ((0, r.up_low, r.up_in, r.o_up), (1, r.down_low, r.down_in, r.o_down)):
        got(taken, r.rep_sem, n, other)
        taken[...] = (own[...].astype(F32) + taken[...].astype(F32)).astype(BF16)
        keeps.append(pltpu.make_async_copy(taken, out, r.load_sem.at[n]))
        keeps[-1].start()
    got(r.bias_in, r.rep_sem, 2, other)
    r.o_bias[...] = r.bias_acc[...] + r.bias_in[...]
    if sz.direct:
        small_middle(r.late_ta, r.late_dev, r.late_sem, True)

    for p in partners:
        got(r.in_part.at[quarter[p]], r.ip_sem, p, ta_peer[p])
    into_one = r.in_part[0].astype(F32)
    for q in range(1, nq):
        into_one = into_one + r.in_part[q].astype(F32)
    x_mine = mm(pick_of(j), r.padded[...].reshape(sz.tp, d))
    _, hat_mine, inv_mine = layer_norm(x_mine, flat_row(r.gain1), flat_row(r.bias1))
    grad = r.dhidden[...] + norm_back(into_one, hat_mine, inv_mine, flat_row(r.gain1))
    r.ig_all[j] = grad.astype(BF16)
    for p in partners:
        go(r.ig_all.at[j], r.ig_all.at[j], r.ig_sem, p, ta_peer[p])
    if sz.direct:
        small_last(r.late_dev, r.late_ea, r.late_sem)

    for s in later:
        got(r.eo_back.at[source[s]], r.eoz_sem, s, ea_peer[s])
    output = r.hidden[...] + mm(back, r.eo_back[...].reshape(sz.experts * cs, d))
    r.out_all[j] = output.astype(BF16)
    for p in partners:
        go(r.out_all.at[j], r.out_all.at[j], r.out_sem, p, ta_peer[p])
    piece_last(1)
    piece_pass(0)
    piece_pass(1)
    stores = []

    def store(n, values, src, dst):
        src[...] = values.reshape(src.shape)
        stores.append(pltpu.make_async_copy(src, dst, r.load_sem.at[n]))
        stores[-1].start()

    for p in partners:
        got(r.ig_all.at[quarter[p]], r.ig_sem, p, ta_peer[p])
    store(2, mm(unpick, r.ig_all[...].reshape(nq * qt, d)).astype(BF16), r.a_low, r.o_in)
    for p in partners:
        got(r.out_all.at[quarter[p]], r.out_sem, p, ta_peer[p])
    store(3, mm(unpick, r.out_all[...].reshape(nq * qt, d)).astype(BF16), r.padded, r.o_out)
    if sz.direct:
        small_end(r.early_ea, r.o_early, r.early_sem)
        small_end(r.late_ea, r.o_late, r.late_sem)
    piece_end(0)
    piece_end(1)
    for copy in stores + keeps:
        copy.wait()
    for copy in started[-pool:]:
        copy.wait_send()
    assert len(receive) <= sz.arrivals, len(receive)


def flat_row(ref):
    return ref[...].reshape(1, -1)


def fit(values, rows):
    have = values.shape[0]
    if have >= rows:
        return values[:rows]
    return jnp.concatenate([values, jnp.zeros((rows - have, values.shape[1]), F32)])


def run_block(sz, inputs):
    nq, ea, d, cs, qt = sz.nq, sz.ea, sz.d, sz.cs, sz.qt
    dma = pltpu.SemaphoreType.DMA
    rows = sz.blocks * cs
    outs = dict(
        o_out=((sz.images, sz.lp, d), BF16),
        o_in=((sz.tp, d), BF16),
        o_early=((sz.early, d), F32),
        o_late=((8, d), F32),
        o_up=((d, sz.hidden), BF16),
        o_down=((sz.hidden, d), BF16),
        o_bias=((8, d), F32),
    )
    flat = (sz.images, sz.lp, sz.inner)
    block = (cs, d)
    buffers = dict(
        tok_v=((sz.length, sz.images, d), BF16),
        cot_v=((sz.length, sz.images, d), BF16),
        qkv_w=((3, sz.inner, d), BF16),
        up_w=((d, sz.hidden), BF16),
        down_w=((sz.hidden, d), BF16),
        w_full=((nq, 2, sz.half, d), BF16),
        padded=((sz.images, sz.lp, d), BF16),
        perm_col=((sz.tp, 128), F32),
        place_row=((4, qt), jnp.int32),
        place_col=((qt, 128), jnp.int32),
        a_low=((sz.tp, d), BF16),
        q=(flat, BF16),
        k=(flat, BF16),
        v=(flat, BF16),
        mixed=(flat, BF16),
        dproj=((3,) + flat, BF16),
        mix_send=((nq, qt, sz.inner), BF16),
        mix_in=((2, nq, qt, sz.inner), BF16),
        dy_mine=((qt, d), BF16),
        hidden=((qt, d), F32),
        dhidden=((qt, d), F32),
        b_low=((qt, d), BF16),
        probs=((sz.ep, qt), F32),
        dy_send=((2, ea) + block, BF16),
        gate_send=((ea, 2, 8, 128), F32),
        dy_all=((nq, ea) + block, BF16),
        rows_all=((nq, ea) + block, BF16),
        gate_in=((ea, 2, 8, 128), F32),
        gate_near=((ea, 2, 8, 128), F32),
        act_t=((sz.kept, rows, sz.hidden), BF16),
        pre_t=((sz.kept, rows, sz.hidden), BF16),
        slot_t=((sz.kept, rows, d), BF16),
        out_t=((sz.kept, rows, d), BF16),
        dg_send=((nq, ea, 8, 128), F32),
        dg_in=((nq, ea, 8, 128), F32),
        rg_in=((2, ea) + block, BF16),
        rg_relay=((2, ea, cs // 2, d), BF16),
        eo_in=((2, ea) + block, BF16),
        eo_relay=((2, ea, cs // 2, d), BF16),
        rgz_send=((ea,) + block, BF16),
        dgz_send=((ea, 8, 128), F32),
        rg_back=((ea,) + block, BF16),
        eo_back=((ea,) + block, BF16),
        dg_back=((ea, 8, 128), F32),
        up_acc=((d, sz.hidden), F32),
        down_acc=((sz.hidden, d), F32),
        bias_acc=((8, d), F32),
        up_low=((d, sz.hidden), BF16),
        down_low=((sz.hidden, d), BF16),
        up_in=((d, sz.hidden), BF16),
        down_in=((sz.hidden, d), BF16),
        bias_in=((8, d), F32),
        da_all=((nq, qt, d), BF16),
        ig_all=((nq, qt, d), BF16),
        out_all=((nq, qt, d), BF16),
        in_send=((nq, qt, d), BF16),
        in_part=((nq, qt, d), BF16),
    )
    if sz.direct:
        outs["p_all"] = ((4, 2, ea, sz.piece, d), BF16)
        buffers |= dict(
            early_ta=((nq, sz.early, d), F32),
            early_dev=((2, sz.early, d), F32),
            early_ea=((ea, sz.early, d), F32),
            late_ta=((nq, 8, d), F32),
            late_dev=((2, 8, d), F32),
            late_ea=((ea, 8, d), F32),
            pd_send=((4, 2, sz.half, d), BF16),
            pd_in=((4, sz.half, d), BF16),
            pz_send=((4, ea, sz.piece, d), BF16),
            pz_in=((4, ea, sz.piece, d), BF16),
        )
    else:
        outs["o_piece"] = ((4, sz.inner, d), F32)
    if sz.direct:
        buffers["row_send"] = ((2, ea) + block, BF16)
        buffers["kept_probs"] = ((sz.images, sz.heads * sz.lp, sz.lp), F32)
    names = list(inputs) + list(outs) + list(buffers) + ["sent", "arrived", "load_sem"]
    vm = pl.BlockSpec(memory_space=pltpu.VMEM)
    far = pl.BlockSpec(memory_space=pltpu.HBM)
    results = pl.pallas_call(
        functools.partial(block_kernel, sz, names),
        out_shape=[jax.ShapeDtypeStruct(*spec) for spec in outs.values()],
        in_specs=[far if name in ("tok", "cot", "w_qkv", "w_up", "w_down") else vm for name in inputs],
        out_specs=[far if name in ("o_up", "o_down", "o_in", "o_out") else vm for name in outs],
        scratch_shapes=[pltpu.VMEM(*spec) for spec in buffers.values()]
        + [dma((sz.pool,)), dma((sz.arrivals,)), dma((5,))],
        name="block",
        compiler_params=pltpu.CompilerParams(
            collective_id=0, has_side_effects=True, vmem_limit_bytes=60 << 20
        ),
    )(*inputs.values())
    return dict(zip(outs, results))


def finish_kernel(sz, names, *refs):
    r = types.SimpleNamespace(**dict(zip(names, refs)))
    n, d = sz.experts, sz.d
    loads, stores = [], []

    def load(src, dst):
        loads.append(pltpu.make_async_copy(src, dst, r.sem_in.at[len(loads)]))
        loads[-1].start()

    def store(src, dst):
        stores.append(pltpu.make_async_copy(src, dst, r.sem_out.at[len(stores)]))
        stores[-1].start()

    third = d // 3
    spans = [pl.ds(k * third, third) for k in range(3)]
    for src, dst in ((r.up, r.up_v), (r.down, r.down_v)):
        for span in spans:
            load(src.at[span], dst.at[span])
    load(r.grad, r.grad_v)
    load(r.out, r.out_v)
    load(r.piece, r.piece_v)
    for dst, src in (
        (r.f_b, r.early[n + 2 : n + 3]),
        (r.f_g1, r.late[0:1]),
        (r.f_c1, r.late[1:2]),
        (r.f_g2, r.early[n : n + 1]),
        (r.f_c2, r.early[n + 1 : n + 2]),
    ):
        dst[...] = src.reshape(d)
    r.f_router[...] = r.early[0:n]
    r.f_qv[...] = r.late[2:4, 0 : sz.inner]
    r.f_upb[...] = r.bias[0:1]
    r.f_downb[...] = r.bias[1:2]
    at = 0
    for src, wide, dst in ((r.up_v, r.up_w, r.f_up), (r.down_v, r.down_w, r.f_down)):
        for span in spans:
            loads[at].wait()
            at += 1
            wide[span] = src[span].astype(F32)
            store(wide.at[span], dst.at[span])
    loads[at].wait()
    for image in range(sz.images):
        r.grad_w[:, image, :] = r.grad_v[image * sz.lp : image * sz.lp + sz.length].astype(F32)
    store(r.grad_w, r.f_grad)
    loads[at + 1].wait()
    for image in range(sz.images):
        r.out_w[:, image, :] = r.out_v[image, 0 : sz.length]
    store(r.out_w, r.f_out)
    loads[at + 2].wait()
    for k in range(4):
        for core in range(2):
            for e in range(sz.ea):
                start = core * sz.half + e * sz.piece
                r.piece_w[k, start : start + sz.piece] = r.piece_v[k, core, e].astype(F32)
        store(r.piece_w.at[k], r.f_qkv.at[k - 1] if k else r.f_o)
    for copy in stores:
        copy.wait()


def finish(sz, got):
    d, n = sz.d, sz.experts
    inputs = dict(
        up=got["o_up"],
        down=got["o_down"],
        out=got["o_out"],
        grad=got["o_in"],
        piece=got["p_all"],
        early=got["o_early"],
        late=got["o_late"],
        bias=got["o_bias"],
    )
    outs = dict(
        f_out=((sz.length, sz.images, d), BF16),
        f_grad=((sz.length, sz.images, d), F32),
        f_qkv=((3, sz.inner, d), F32),
        f_qv=((2, sz.inner), F32),
        f_o=((sz.inner, d), F32),
        f_b=((d,), F32),
        f_g1=((d,), F32),
        f_c1=((d,), F32),
        f_g2=((d,), F32),
        f_c2=((d,), F32),
        f_router=((n, d), F32),
        f_up=((d, sz.hidden), F32),
        f_upb=((1, sz.hidden), F32),
        f_down=((sz.hidden, d), F32),
        f_downb=((1, d), F32),
    )
    buffers = dict(
        up_v=((d, sz.hidden), BF16),
        down_v=((sz.hidden, d), BF16),
        grad_v=((sz.tp, d), BF16),
        out_v=((sz.images, sz.lp, d), BF16),
        piece_v=((4, 2, sz.ea, sz.piece, d), BF16),
        up_w=((d, sz.hidden), F32),
        down_w=((sz.hidden, d), F32),
        grad_w=((sz.length, sz.images, d), F32),
        out_w=((sz.length, sz.images, d), BF16),
        piece_w=((4, sz.inner, d), F32),
    )
    vm = pl.BlockSpec(memory_space=pltpu.VMEM)
    far = pl.BlockSpec(memory_space=pltpu.HBM)
    large = ("up", "down", "out", "grad", "piece", "f_out", "f_grad", "f_qkv", "f_o", "f_up", "f_down")
    names = list(inputs) + list(outs) + list(buffers) + ["sem_in", "sem_out"]
    results = pl.pallas_call(
        functools.partial(finish_kernel, sz, names),
        out_shape=[jax.ShapeDtypeStruct(*spec) for spec in outs.values()],
        in_specs=[far if name in large else vm for name in inputs],
        out_specs=[far if name in large else vm for name in outs],
        scratch_shapes=[pltpu.VMEM(*spec) for spec in buffers.values()]
        + [pltpu.SemaphoreType.DMA((16,)), pltpu.SemaphoreType.DMA((16,))],
        name="finish",
        compiler_params=pltpu.CompilerParams(vmem_limit_bytes=60 << 20),
    )(*inputs.values())
    (out, grad, qkv, qv, o, b, g1, c1, g2, c2, router, up, up_b, down, down_b) = results
    turn = lambda t: jnp.swapaxes(t, 0, 1)
    return (
        turn(out),
        turn(grad),
        jnp.swapaxes(qkv, 1, 2),
        qv,
        o,
        b,
        g1,
        c1,
        g2,
        c2,
        router.T,
        up[None],
        up_b,
        down[None],
        down_b,
    )


def local(
    tokens,
    expert_ids,
    pair_ranks,
    cotangent,
    w_qkv,
    b_qv,
    w_out,
    b_out,
    ln1_gain,
    ln1_bias,
    ln2_gain,
    ln2_bias,
    w_router,
    w_up,
    b_up,
    w_down,
    b_down,
):
    sz = Sizes(tokens, expert_ids, w_qkv, w_up)
    inputs = dict(
        tok=jnp.swapaxes(tokens, 0, 1),
        cot=jnp.swapaxes(cotangent, 0, 1),
        w_qkv=jnp.swapaxes(w_qkv, 1, 2),
        b_qv=b_qv,
        w_out=w_out.reshape(2, sz.half, sz.d),
        b_out=b_out,
        gain1=ln1_gain,
        bias1=ln1_bias,
        gain2=ln2_gain,
        bias2=ln2_bias,
        router=w_router.T,
        w_up=w_up[0],
        b_up=b_up,
        w_down=w_down[0],
        b_down=b_down,
        ids=jnp.transpose(expert_ids, (0, 2, 1)),
        ranks=jnp.transpose(pair_ranks, (0, 2, 1)),
    )
    got = run_block(sz, inputs)
    if sz.direct:
        return finish(sz, got)
    n = sz.experts
    piece, shared = lax.psum((got["o_piece"], got["o_late"][2:4]), ("ea", "dev"))
    early, late = lax.psum((got["o_early"], got["o_late"][:2]), ("ea", "ta", "dev"))
    return (
        got["o_out"][:, : sz.length],
        got["o_in"].reshape(got["o_out"].shape)[:, : sz.length].astype(F32),
        jnp.swapaxes(piece[1:], 1, 2),
        shared[:, : sz.inner],
        piece[0],
        early[n + 2],
        late[0],
        late[1],
        early[n],
        early[n + 1],
        early[:n].T,
        got["o_up"].astype(F32)[None],
        got["o_bias"][0:1],
        got["o_down"].astype(F32)[None],
        got["o_bias"][1:2],
    )


def solution(mesh):
    in_specs = (
        P(("ea", "dev"), None, None),
        P(("ea", "dev"), None, None),
        P(("ea", "dev"), None, None),
        P(("ea", "dev"), None, None),
        P(None, None, "ta"),
        P(None, "ta"),
        P("ta", None),
        P(),
        P(),
        P(),
        P(),
        P(),
        P(),
        P("ea", None, "ta"),
        P("ea", "ta"),
        P("ea", "ta", None),
        P("ea", None),
    )
    out_specs = (
        P(("ea", "dev"), None, None),
        P(("ea", "dev"), None, None),
        P(None, None, "ta"),
        P(None, "ta"),
        P("ta", None),
        P(),
        P(),
        P(),
        P(),
        P(),
        P(),
        P("ea", None, "ta"),
        P("ea", "ta"),
        P("ea", "ta", None),
        P("ea", None),
    )
    return jax.shard_map(local, mesh=mesh, in_specs=in_specs, out_specs=out_specs, check_vma=False)
```

```python
import functools
import types

import jax
import jax.numpy as jnp
from jax import lax
from jax.experimental import pallas as pl
from jax.experimental.pallas import tpu as pltpu
from jax.sharding import PartitionSpec as P

HDIM = 64
EPSILON = 1e-06
F32, BF16 = jnp.float32, jnp.bfloat16
EXACT = lax.Precision.HIGHEST
MESH = pl.DeviceIdType.MESH
NT = (((1,), (1,)), ((), ()))
TN = (((0,), (0,)), ((), ()))
NN = (((1,), (0,)), ((), ()))


def ceil_to(value, unit):
    return -(-value // unit) * unit


def mm(a, b, dims=NN, precision=None):
    return lax.dot_general(a, b, dims, precision=precision, preferred_element_type=F32)


def iota(shape, dim):
    return lax.broadcasted_iota(jnp.int32, shape, dim)


def onehot(mask):
    return jnp.where(mask, 1.0, 0.0).astype(F32)


class Sizes:
    def __init__(self, tokens, expert_ids, w_qkv, w_up):
        self.images, self.length, self.d = tokens.shape
        self.top = expert_ids.shape[2]
        self.tokens = self.images * self.length
        self.ea = lax.axis_size("ea")
        self.nq = lax.axis_size("ta")
        assert w_up.shape[0] == 1
        self.experts = self.ea
        self.cap = (9 * self.tokens * self.top + 8 * self.experts - 1) // (8 * self.experts)
        self.inner = w_qkv.shape[2]
        self.heads = self.inner // HDIM
        self.hidden = w_up.shape[2]
        self.lp = ceil_to(self.length, 16)
        self.tp = self.images * self.lp
        per_quarter = -(-self.tokens // self.nq)
        self.qt = ceil_to(per_quarter, 8)
        spread = (self.cap + (self.nq - 1) * self.experts) // self.nq
        self.cs = ceil_to(min(self.cap, per_quarter, spread), 16)
        self.ep = ceil_to(self.experts, 16)
        self.half = self.inner // 2
        self.piece = self.half // self.ea
        self.early = ceil_to(self.experts + 3, 8)
        self.blocks = max(1, min(self.ea, (256 if self.ea <= 8 else 64) // self.cs))
        self.chunks = self.ea // self.blocks
        self.direct = self.ea <= 8
        self.relay = [2] if self.direct else []
        self.dy_relay = [2] if self.direct else []
        self.kept = self.nq if self.chunks == 1 else 1
        self.pool = 40
        self.arrivals = 145 if self.direct else 48 + 13 * self.ea
        assert self.top == 2 and self.nq == 4 and self.experts * self.nq <= 128


def pair_table(sz, ids, ranks):
    wide = ceil_to(sz.tp, 128)
    spread, inside = jnp.zeros((8, wide), F32), jnp.zeros((1, wide), F32)
    for image in range(sz.images):
        experts, rank = ids[image].astype(F32), ranks[image].astype(F32)
        high = jnp.floor(rank * (1.0 / 64))
        rows = jnp.concatenate([experts, high, rank - high * 64, jnp.zeros_like(rank)], axis=0)
        lane = iota((sz.length, wide), 1)
        move = onehot(lane == iota((sz.length, wide), 0) + image * sz.lp).astype(BF16)
        spread = spread + mm(rows.astype(BF16), move)
        at = iota((1, wide), 1) - image * sz.lp
        inside = inside + onehot((at >= 0) & (at < sz.length))
    rank = spread[2:4] * 64 + spread[4:6]
    table = jnp.concatenate([spread[0:2], rank, jnp.zeros((4, wide), F32)], axis=0)
    return jnp.where(inside > 0, table, float(2 * sz.tokens))


def route(sz, table):
    cols = table.T[: sz.tp]
    wide = iota((sz.tp, 128), 1)
    lane = wide.astype(F32)

    def flip(*columns):
        spread = jnp.zeros((sz.tp, 128), F32)
        for n, column in enumerate(columns):
            spread = spread + jnp.where(wide == n, column, 0.0)
        turned = spread.T
        return [turned[n : n + 1] for n in range(len(columns))]

    def total(values):
        return jnp.sum(values, axis=1, keepdims=True)

    ids = [cols[:, k : k + 1] for k in range(2)]
    real = ids[0] < sz.experts
    member = [onehot(lane == column) for column in ids]
    dest = []
    for k in range(2):
        before = jnp.zeros((sz.tp, 128), F32)
        for m in range(2):
            mask = onehot(table[2 + m : 3 + m, : sz.tp] < cols[:, 2 + k : 3 + k])
            before = before + mm(mask.astype(BF16), member[m].astype(BF16))
        kept = (total(before * member[k]) < sz.cap) & real
        dest.append(jnp.where(kept, ids[k], float(sz.experts)))
    low, high = jnp.minimum(*dest), jnp.maximum(*dest)
    index = iota((sz.tp, 1), 0).astype(F32)
    kind = jnp.where(real, low * (sz.experts + 1) + high, float((sz.experts + 1) ** 2))
    key = kind * sz.tp + index
    (key_row,) = flip(key)
    earlier = onehot(key_row < key).astype(BF16)
    order = mm(earlier, jnp.ones((sz.tp, 128), BF16))[:, 0:1]
    lap = jnp.floor((order + 0.5) * (1.0 / sz.nq))
    quarter = order - lap * sz.nq
    perm = jnp.where(real, quarter * sz.qt + lap, -1.0)
    group = [
        onehot((lane == d * sz.nq + quarter) & (d < sz.experts)) for d in dest
    ]
    ahead = mm(earlier, (group[0] + group[1]).astype(BF16))
    place = []
    for k in range(2):
        slot = total(ahead * group[k])
        place.append(jnp.where(dest[k] < sz.experts, dest[k] * sz.cs + slot + 1.0, 0.0))
    perm_row, *place_row = flip(perm, *place)
    return perm, perm_row, place, place_row


def layer_norm(values, gain_vec, shift_vec):
    row_mean = jnp.mean(values, axis=-1, keepdims=True)
    centered = values - row_mean
    variance = jnp.mean(centered * centered, axis=-1, keepdims=True)
    inverse = lax.rsqrt(variance + EPSILON)
    normed = centered * inverse
    return (normed * gain_vec + shift_vec, normed, inverse)


def norm_back(grad_rows, normed, inverse, gain_vec):
    scaled = grad_rows * gain_vec
    return inverse * (
        scaled
        - jnp.mean(scaled, axis=-1, keepdims=True)
        - normed * jnp.mean(scaled * normed, axis=-1, keepdims=True)
    )


def push(src, dst, send_sem, recv_sem, device):
    return pltpu.make_async_remote_copy(
        src_ref=src,
        dst_ref=dst,
        send_sem=send_sem,
        recv_sem=recv_sem,
        device_id=device,
        device_id_type=MESH,
    )


def greet(devices):
    barrier = pltpu.get_barrier_semaphore()
    for device in devices:
        pl.semaphore_signal(barrier, inc=1, device_id=device, device_id_type=MESH)


def head_mask(sz, head, dtype):
    lane = iota((1, sz.inner), 1)
    return onehot((lane >= head * HDIM) & (lane < (head + 1) * HDIM)).astype(dtype)


def gelu_parts(values):
    cdf = 0.5 * (1.0 + lax.erf(values * (0.5**0.5)))
    density = jnp.exp(-0.5 * values * values) * (0.5 / jnp.pi) ** 0.5
    return cdf, density


class Sent:
    def __init__(self, copy):
        self.copy, self.done = copy, False

    def wait_send(self):
        if not self.done:
            self.copy.wait_send()
        self.done = True


class Refs(types.SimpleNamespace):
    def __getattr__(self, name):
        return name


def block_kernel(sz, names, *refs):
    r = Refs(**dict(zip(names, refs)))
    z, j, c = lax.axis_index("ea"), lax.axis_index("ta"), lax.axis_index("dev")
    nq, ea, d, cs, qt = sz.nq, sz.ea, sz.d, sz.cs, sz.qt
    quarter = [j, j + 1 - 2 * lax.rem(j, 2), j + 2 - 4 * lax.div(j, 2), 3 - j]
    ta_peer = [{"ta": q} for q in quarter]
    ea_peer = [{"ea": lax.rem(z + s, ea)} for s in range(ea)]
    source = [lax.rem(z - s + ea, ea) for s in range(ea)]
    target = [lax.rem(z + s, ea) for s in range(ea)]
    other = {"dev": 1 - c}
    later = [s for s in range(1, ea)]
    partners = (1, 2, 3)
    pool, started, receive = sz.pool, [], {}

    def go(src, dst, kind, index, device):
        at = receive.setdefault((kind, index), len(receive))
        n = len(started)
        if n >= pool:
            started[n - pool].wait_send()
        copy = push(src, dst, r.sent.at[n % pool], r.arrived.at[at], device)
        copy.start()
        started.append(Sent(copy))
        return started[-1]

    def got(dst, kind, index, device):
        at = receive.setdefault((kind, index), len(receive))
        push(dst, dst, r.sent.at[0], r.arrived.at[at], device).wait_recv()

    everyone = ta_peer[1:] + ea_peer[1:] + [other]
    greet(everyone)
    loads = []
    for n, (src, dst) in enumerate(
        ((r.cot, r.cot_v), (r.tok, r.tok_v), (r.w_qkv, r.qkv_w), (r.w_up, r.up_w), (r.w_down, r.down_w))
    ):
        loads.append(pltpu.make_async_copy(src, dst, r.load_sem.at[n]))
        loads[-1].start()
    pl.semaphore_wait(pltpu.get_barrier_semaphore(), len(everyone))

    for p in partners:
        go(r.w_out.at[c], r.w_full.at[j, c], r.w_sem, p, ta_peer[p])
    r.w_full[j] = r.w_out[...]

    perm_col, perm, place, place_rows = route(sz, pair_table(sz, r.ids, r.ranks))
    perm = perm.astype(jnp.int32)
    r.perm_col[...] = jnp.broadcast_to(perm_col, (sz.tp, 128))
    pick_all = onehot(iota((nq * qt, sz.tp), 0) == perm).astype(BF16)

    def pick_of(q):
        return onehot(iota((qt, sz.tp), 0) + q * qt == perm).astype(BF16)

    spread = iota((8, 1), 0)
    both = jnp.where(spread == 0, place_rows[0], 0.0) + jnp.where(spread == 1, place_rows[1], 0.0)
    for which, q in ((0, quarter[0]), (1, quarter[3])):
        chosen = mm(both, onehot(iota((qt, sz.tp), 0) + q * qt == perm), NT, EXACT)
        r.place_row[2 * which : 2 * which + 2] = (chosen[0:2] + 0.5).astype(jnp.int32) - 1
    pair_col = jnp.where(iota((1, 128), 1) == 0, place[0], 0.0)
    pair_col = pair_col + jnp.where(iota((1, 128), 1) == 1, place[1], 0.0)
    chosen = mm(onehot(iota((qt, sz.tp), 0) + j * qt == perm), pair_col, NN, EXACT)
    r.place_col[...] = (chosen + 0.5).astype(jnp.int32) - 1

    def slots_of(expert, which):
        row = iota((cs, qt), 0) + expert * cs
        first, second = r.place_row[2 * which : 2 * which + 1], r.place_row[2 * which + 1 : 2 * which + 2]
        return onehot((row == first) | (row == second))

    tail = (sz.length // 16) * 16
    loads[0].wait()
    for image in range(sz.images):
        r.padded[image, tail:] = jnp.zeros((sz.lp - tail, d), BF16)
        r.padded[image, 0 : sz.length] = r.cot_v[:, image, :]
    for which, q in ((0, quarter[0]), (1, quarter[3])):
        dy_rows = mm(pick_of(q), r.padded[...].reshape(sz.tp, d)).astype(BF16)
        if which == 0:
            r.dy_mine[...] = dy_rows
        for expert in range(sz.experts):
            r.dy_send[which, expert] = mm(slots_of(expert, which).astype(BF16), dy_rows).astype(BF16)
    dy_copies = []
    near_first = later[:1] + later[2:] + later[1:2]

    def send_dy(which, q, planes):
        for s in planes:
            block = r.dy_send.at[which, target[s]]
            dy_copies.append(go(block, r.dy_all.at[q, z], r.dyz_sem, (which, s), ea_peer[s]))

    send_dy(0, quarter[0], near_first)
    for which, q in ((0, quarter[0]), (1, quarter[3])):
        r.dy_all[q, z] = r.dy_send[which, z]

    def forward(ref, z_sem, t_sem, order):
        copies = []
        for s in order:
            block = ref.at[j, source[s]]
            if s:
                got(block, z_sem, (0, s), ea_peer[s])
            for p in (1, 2):
                copies.append(go(block, block, t_sem, (p, s), ta_peer[p]))
        return copies

    dy_forwards = forward(r.dy_all, r.dyz_sem, r.dyt_sem, [0])

    low_half, high_half = pl.ds(0, cs // 2), pl.ds(cs // 2, cs // 2)

    def relay(ref, t_sem, sem, planes):
        copies = []
        for s in planes:
            for p, part in ((1, high_half), (2, low_half)):
                got(ref.at[quarter[p], source[s]], t_sem, (p, s), ta_peer[p])
                half = ref.at[quarter[p], source[s], part]
                copies.append(go(half, half, sem, (3 - p, s), ta_peer[3 - p]))
        return copies

    loads[1].wait()
    loads[2].wait()
    for image in range(sz.images):
        r.padded[image, 0 : sz.length] = r.tok_v[:, image, :]
    normed_one, _, _ = layer_norm(
        r.padded[...].reshape(sz.tp, d).astype(F32), flat_row(r.gain1), flat_row(r.bias1)
    )
    a_low = normed_one.astype(BF16)
    r.a_low[...] = a_low
    flat = (sz.images, sz.lp, sz.inner)
    r.q[...] = (mm(a_low, r.qkv_w[0], NT) + r.b_qv[0:1]).astype(BF16).reshape(flat)
    r.k[...] = mm(a_low, r.qkv_w[1], NT).astype(BF16).reshape(flat)
    r.v[...] = (mm(a_low, r.qkv_w[2], NT) + r.b_qv[1:2]).astype(BF16).reshape(flat)

    for p in partners:
        block = r.w_full.at[quarter[p], c]
        got(block, r.w_sem, p, ta_peer[p])
        go(block, block, r.wd_sem, p, other)

    scale = HDIM ** (-0.5)
    live = iota((1, sz.lp), 1) < sz.length

    def stack(values):
        return jnp.concatenate([values * head_mask(sz, h, BF16) for h in range(sz.heads)], axis=0)

    def unstack(values):
        return sum(
            values[h * sz.lp : (h + 1) * sz.lp] * head_mask(sz, h, F32) for h in range(sz.heads)
        )

    def attention_probs(image):
        scores = mm(stack(r.q[image]), r.k[image], NT) * scale
        scores = jnp.where(live, scores, -1e30)
        exps = jnp.exp(scores - jnp.max(scores, axis=-1, keepdims=True))
        return exps / jnp.sum(exps, axis=-1, keepdims=True)

    for image in range(sz.images):
        probs = attention_probs(image)
        if sz.direct:
            r.kept_probs[image] = probs
        r.mixed[image] = unstack(mm(probs.astype(BF16), r.v[image])).astype(BF16)
    dealt = mm(pick_all, r.mixed[...].reshape(sz.tp, sz.inner)).astype(BF16)
    r.mix_send[...] = dealt.reshape(nq, qt, sz.inner)
    for p in partners:
        go(r.mix_send.at[quarter[p]], r.mix_in.at[0, j], r.mix_sem, (0, p), ta_peer[p])
        go(r.mix_send.at[quarter[3 - p]], r.mix_in.at[1, j], r.mix_sem, (1, p), ta_peer[p])
    for copy in list(dy_copies):
        copy.wait_send()
    send_dy(1, quarter[3], [s for s in near_first if s not in sz.dy_relay])
    dy_forwards += forward(r.dy_all, r.dyz_sem, r.dyt_sem, near_first)
    r.mix_in[0, j] = r.mix_send[j]
    r.mix_in[1, j] = r.mix_send[quarter[3]]
    x_rows = [mm(pick_of(q), r.padded[...].reshape(sz.tp, d)) for q in (quarter[0], quarter[3])]
    for p in partners:
        got(r.w_full.at[quarter[p], 1 - c], r.wd_sem, p, other)
    for p in partners:
        got(r.mix_in.at[0, quarter[p]], r.mix_sem, (0, p), ta_peer[p])
        got(r.mix_in.at[1, quarter[p]], r.mix_sem, (1, p), ta_peer[p])

    if not sz.direct:
        r.row_send = r.dy_send
        for copy in dy_copies:
            copy.wait_send()
    router_w = r.router[...]
    if sz.ep > sz.experts:
        router_w = jnp.concatenate([router_w, jnp.zeros((sz.ep - sz.experts, d), BF16)])
    def send_rows(which, q, planes):
        return [
            go(r.row_send.at[which, target[s]], r.rows_all.at[q, z], r.rowz_sem, (which, s), ea_peer[s])
            for s in planes
        ]

    for which in (0, 1):
        attention = flat_row(r.b_out)
        for q in range(nq):
            attention = attention + mm(r.mix_in[which, q], r.w_full[q].reshape(sz.inner, d))
        hidden = x_rows[which] + attention
        normed_two, _, _ = layer_norm(hidden, flat_row(r.gain2), flat_row(r.bias2))
        b_low = normed_two.astype(BF16)
        logits = mm(router_w, b_low, NT)
        logits = jnp.where(iota((sz.ep, 1), 0) < sz.experts, logits, -1e30)
        exps = jnp.exp(logits - jnp.max(logits, axis=0, keepdims=True))
        router = exps / jnp.sum(exps, axis=0, keepdims=True)
        if which == 0:
            r.hidden[...], r.b_low[...], r.probs[...] = hidden, b_low, router
        for expert in range(sz.experts):
            slots = slots_of(expert, which)
            r.row_send[which, expert] = mm(slots.astype(BF16), b_low).astype(BF16)
            level = jnp.broadcast_to(router[expert : expert + 1], (8, qt))
            r.gate_send[expert, which, :, 0:cs] = mm(level, slots, NT, EXACT)
        q = quarter[3 * which]
        if which:
            for s in later:
                go(r.gate_send.at[target[s]], r.gate_in.at[z], r.gatez_sem, s, ea_peer[s])
            r.gate_in[z] = r.gate_send[z]
        if which == 0:
            row_copies = send_rows(0, q, near_first[:-1])
        r.rows_all[q, z] = r.row_send[which, z]
    row_forwards = forward(r.rows_all, r.rowz_sem, r.rowt_sem, [0])
    for copy in row_copies:
        copy.wait_send()
    row_copies = send_rows(0, quarter[0], near_first[-1:])
    row_forwards += forward(r.rows_all, r.rowz_sem, r.rowt_sem, near_first[:-1])
    for copy in row_copies:
        copy.wait_send()
    send_rows(1, quarter[3], [s for s in near_first if s not in sz.relay])
    row_forwards += forward(r.rows_all, r.rowz_sem, r.rowt_sem, near_first[-1:])
    for s in later:
        got(r.gate_in.at[source[s]], r.gatez_sem, s, ea_peer[s])
    go(r.gate_in, r.gate_near, r.gatet_sem, 0, ta_peer[1])

    row_relays = relay(r.rows_all, r.rowt_sem, r.rowr_sem, [s for s in near_first if s in sz.relay])
    row_relays += relay(r.dy_all, r.dyt_sem, r.dyr_sem, sz.dy_relay)

    loads[3].wait()
    loads[4].wait()
    first = jnp.where(j == 0, 1.0, 0.0)
    spot = iota((cs, cs), 0) == iota((cs, cs), 1)
    rows_n = sz.blocks * cs

    def expert_chunk(q, p, chunk):
        at = pl.ds(chunk * sz.blocks, sz.blocks) if sz.chunks > 1 else slice(None)
        keep = p if sz.kept > 1 else 0
        rows = r.rows_all[q, at].reshape(rows_n, d)
        dy = r.dy_all[q, at].reshape(rows_n, d).astype(F32)
        gates = []
        for b in range(sz.blocks):
            g = chunk * sz.blocks + b
            held, which = ((r.gate_in, 0), (r.gate_near, 0), (r.gate_near, 1), (r.gate_in, 1))[p]
            level = held[g, which][0:1, 0:cs]
            gates.append(jnp.sum(jnp.where(spot, level, 0.0), axis=1, keepdims=True))
        gate = jnp.concatenate(gates, axis=0) if len(gates) > 1 else gates[0]
        pre_act = mm(rows, r.up_w[...]) + r.b_up[...]
        cdf, density = gelu_parts(pre_act)
        act_low = (pre_act * cdf).astype(BF16)
        slot_grad = (gate * dy).astype(BF16)
        pre_grad = (mm(slot_grad, r.down_w[...], NT) * (cdf + pre_act * density)).astype(BF16)
        row_grad = mm(pre_grad, r.up_w[...], NT).astype(BF16)
        r.act_t[keep], r.pre_t[keep], r.slot_t[keep] = act_low, pre_grad, slot_grad
        r.dy_all[q, at] = row_grad.reshape(sz.blocks, cs, d)
        expert_out = mm(act_low, r.down_w[...]) + first * r.b_down[...]
        r.out_t[keep] = (gate * expert_out).astype(BF16)
        dgate = jnp.sum(expert_out * dy, axis=1, keepdims=True)
        for b in range(sz.blocks):
            g = chunk * sz.blocks + b
            level = jnp.sum(
                jnp.where(spot, dgate[b * cs : (b + 1) * cs], 0.0), axis=0, keepdims=True
            )
            r.dg_send[p, g, :, 0:cs] = jnp.broadcast_to(level, (8, cs))

    def weight_chunk(q, p, chunk, fresh):
        at = pl.ds(chunk * sz.blocks, sz.blocks) if sz.chunks > 1 else slice(None)
        keep = p if sz.kept > 1 else 0
        rows = r.rows_all[q, at].reshape(rows_n, d)
        up = mm(rows, r.pre_t[keep], TN)
        down = mm(r.act_t[keep], r.slot_t[keep], TN)
        biases = jnp.concatenate(
            [
                jnp.sum(r.pre_t[keep].astype(F32), axis=0, keepdims=True),
                jnp.sum(r.slot_t[keep].astype(F32), axis=0, keepdims=True),
                jnp.zeros((6, d), F32),
            ]
        )
        if fresh:
            r.up_acc[...], r.down_acc[...], r.bias_acc[...] = up, down, biases
        else:
            r.up_acc[...] += up
            r.down_acc[...] += down
            r.bias_acc[...] += biases
        r.rows_all[q, at] = r.out_t[keep].reshape(sz.blocks, cs, d)

    parts = (None, (low_half, high_half), (high_half, low_half))
    blocks = later[1:2] + later[:1] + later[2:] + [0]
    early_planes = ea - 1

    fine = [(s, target[s]) for s in blocks] if sz.direct else [(0, slice(None))]
    whole = [(0, slice(None))]

    def share_diagonal(ref, relay_in, kind, groups):
        for s, g in groups:
            for n, p, part in ((0, 2, low_half), (1, 1, high_half)):
                half = ref.at[quarter[3], g, part]
                go(half, relay_in.at[n, g], kind, (n, s), ta_peer[p])

    def share_straight(ref, taken, kind, groups, p):
        for s, g in groups:
            half = parts[p][1]
            go(ref.at[quarter[p], g, half], taken.at[p - 1, g, half], kind, (1 + p, s), ta_peer[p])

    def share_joined(ref, taken, relay_in, kind, groups, p):
        for s, g in groups:
            half = parts[p][0]
            got(relay_in.at[p - 1, g], kind, (p - 1, s), ta_peer[3 - p])
            joined = ref[quarter[p], g, half].astype(F32) + relay_in[p - 1, g].astype(F32)
            ref[quarter[p], g, half] = joined.astype(BF16)
            go(ref.at[quarter[p], g, half], taken.at[p - 1, g, half], kind, (3 + p, s), ta_peer[p])

    def share_got(taken, kind, s, g):
        for p in (1, 2):
            got(taken.at[p - 1, g, parts[p][1]], kind, (1 + p, s), ta_peer[p])
            got(taken.at[p - 1, g, parts[p][0]], kind, (3 + p, s), ta_peer[p])

    def share_sum(ref, taken, g):
        return ref[j, g].astype(F32) + taken[0, g].astype(F32) + taken[1, g].astype(F32)

    for p in (0, 3, 1, 2):
        q = quarter[p]
        if p == 0:
            for copy in dy_forwards + row_forwards:
                copy.wait_send()
        elif p == 3:
            for s in later:
                if s in sz.dy_relay:
                    got(r.dy_all.at[q, source[s], low_half], r.dyr_sem, (1, s), ta_peer[1])
                    got(r.dy_all.at[q, source[s], high_half], r.dyr_sem, (2, s), ta_peer[2])
                else:
                    got(r.dy_all.at[q, source[s]], r.dyz_sem, (1, s), ea_peer[s])
                if s in sz.relay:
                    got(r.rows_all.at[q, source[s], low_half], r.rowr_sem, (1, s), ta_peer[1])
                    got(r.rows_all.at[q, source[s], high_half], r.rowr_sem, (2, s), ta_peer[2])
                else:
                    got(r.rows_all.at[q, source[s]], r.rowz_sem, (1, s), ea_peer[s])
        else:
            if p == 1:
                got(r.gate_near, r.gatet_sem, 0, ta_peer[1])
            for s in range(ea):
                if s not in sz.dy_relay:
                    got(r.dy_all.at[q, source[s]], r.dyt_sem, (p, s), ta_peer[p])
                if s not in sz.relay:
                    got(r.rows_all.at[q, source[s]], r.rowt_sem, (p, s), ta_peer[p])
            if p == 1:
                for copy in row_relays:
                    copy.wait_send()
        if sz.chunks == 1:
            expert_chunk(q, p, 0)
            if p == 0:
                weight_chunk(q, p, 0, True)
        else:
            if p == 0:
                r.up_acc[...] = jnp.zeros((d, sz.hidden), F32)
                r.down_acc[...] = jnp.zeros((sz.hidden, d), F32)
                r.bias_acc[...] = jnp.zeros((8, d), F32)

            @pl.loop(0, sz.chunks)
            def _(chunk):
                expert_chunk(q, p, chunk)
                weight_chunk(q, p, chunk, False)

        if p:
            go(r.dg_send.at[p], r.dg_in.at[p], r.dg_sem, p, ta_peer[p])
        group = fine[:early_planes]
        if p == 3:
            share_diagonal(r.dy_all, r.rg_relay, r.rg_sem, group)
        elif p:
            share_straight(r.dy_all, r.rg_in, r.rg_sem, group, p)
    first_sent = list(started)
    for p in (1, 2):
        share_joined(r.dy_all, r.rg_in, r.rg_relay, r.rg_sem, group, p)
    if sz.chunks == 1:
        weight_chunk(quarter[3], 3, 0, False)
    group = fine[early_planes:]
    for copy in first_sent:
        copy.wait_send()
    if group:
        share_diagonal(r.dy_all, r.rg_relay, r.rg_sem, group)
        for p in (1, 2):
            share_straight(r.dy_all, r.rg_in, r.rg_sem, group, p)
    if sz.chunks == 1:
        weight_chunk(quarter[1], 1, 0, False)
    for p in (1, 2):
        share_joined(r.dy_all, r.rg_in, r.rg_relay, r.rg_sem, group, p)

    home_copies = []
    for p in partners:
        got(r.dg_in.at[p], r.dg_sem, p, ta_peer[p])

    def send_home(planes):
        for s in planes:
            g = target[s]
            if sz.direct or s == blocks[0]:
                share_got(r.rg_in, r.rg_sem, *((s, g) if sz.direct else whole[0]))
            share = share_sum(r.dy_all, r.rg_in, g)
            dgate = r.dg_send[0, g]
            for p in partners:
                dgate = dgate + r.dg_in[p, g]
            if s:
                r.rgz_send[g] = share.astype(BF16)
                r.dgz_send[g] = dgate
                go(r.dgz_send.at[g], r.dg_back.at[z], r.dgz_sem, s, ea_peer[s])
                home_copies.append(go(r.rgz_send.at[g], r.rg_back.at[z], r.rgz_sem, s, ea_peer[s]))
            else:
                r.rg_back[z] = share.astype(BF16)
                r.dg_back[z] = dgate

    send_home(blocks[:early_planes])
    if sz.chunks == 1:
        weight_chunk(quarter[2], 2, 0, False)
    send_home(blocks[early_planes:])
    share_diagonal(r.rows_all, r.eo_relay, r.eo_sem, whole)
    for p in (1, 2):
        share_straight(r.rows_all, r.eo_in, r.eo_sem, whole, p)

    r.up_low[...] = r.up_acc[...].astype(BF16)
    r.down_low[...] = r.down_acc[...].astype(BF16)
    go(r.up_low, r.up_in, r.rep_sem, 0, other)
    go(r.down_low, r.down_in, r.rep_sem, 1, other)
    go(r.bias_acc, r.bias_in, r.rep_sem, 2, other)

    place_0, place_1 = r.place_col[:, 0:1], r.place_col[:, 1:2]
    lane = iota((qt, sz.experts * cs), 1)
    back = onehot((lane == place_0) | (lane == place_1)).astype(BF16)
    for s in later:
        got(r.dg_back.at[source[s]], r.dgz_sem, s, ea_peer[s])
        got(r.rg_back.at[source[s]], r.rgz_sem, s, ea_peer[s])

    drouter = jnp.zeros((sz.ep, qt), F32)
    for expert in range(sz.experts):
        level = mm(r.dg_back[expert][:, 0:cs], slots_of(expert, 0), NN, EXACT)
        drouter = drouter + jnp.where(iota((sz.ep, 1), 0) == expert, level[0:1], 0.0)
    router = r.probs[...]
    dlogits = (router * (drouter - jnp.sum(router * drouter, axis=0, keepdims=True))).astype(BF16)
    into_two = mm(back, r.rg_back[...].reshape(sz.experts * cs, d)) + mm(dlogits, router_w, TN)
    _, hat_two, inv_two = layer_norm(r.hidden[...], flat_row(r.gain2), flat_row(r.bias2))
    dhidden = r.dy_mine[...].astype(F32) + norm_back(into_two, hat_two, inv_two, flat_row(r.gain2))
    r.dhidden[...] = dhidden
    dattn = dhidden.astype(BF16)
    r.da_all[j] = dattn
    for p in partners:
        go(r.da_all.at[j], r.da_all.at[j], r.da_sem, p, ta_peer[p])
    router_grad = mm(dlogits, r.b_low[...])
    rows_at = iota((sz.early, 1), 0)
    early = jnp.where(rows_at < sz.experts, fit(router_grad, sz.early), 0.0)
    for offset, values in enumerate((into_two * hat_two, into_two, dattn.astype(F32))):
        total = jnp.sum(values, axis=0, keepdims=True)
        early = early + jnp.where(rows_at == sz.experts + offset, total, 0.0)

    def small_start(values, by_ta, sem):
        by_ta[j] = values
        for p in partners:
            go(by_ta.at[j], by_ta.at[j], sem, (0, p), ta_peer[p])

    def small_middle(by_ta, by_dev, sem, own_rows):
        for p in partners:
            got(by_ta.at[quarter[p]], sem, (0, p), ta_peer[p])
        total = by_ta[0]
        for q in range(1, nq):
            total = total + by_ta[q]
        if own_rows:
            total = jnp.where(iota((8, 1), 0) < 2, total, by_ta[j])
        by_dev[c] = total
        go(by_dev.at[c], by_dev.at[c], sem, (1, 0), other)

    def small_last(by_dev, by_ea, sem):
        got(by_dev.at[1 - c], sem, (1, 0), other)
        by_ea[z] = by_dev[0] + by_dev[1]
        for s in later:
            go(by_ea.at[z], by_ea.at[z], sem, (2, s), ea_peer[s])

    def small_end(by_ea, out, sem):
        for s in later:
            got(by_ea.at[source[s]], sem, (2, s), ea_peer[s])
        total = by_ea[0]
        for e in range(1, ea):
            total = total + by_ea[e]
        out[...] = total

    if sz.direct:
        small_start(early, r.early_ta, r.early_sem)
    else:
        r.o_early[...] = early

    for p in partners:
        got(r.da_all.at[quarter[p]], r.da_sem, p, ta_peer[p])
    for p in (1, 2):
        share_joined(r.rows_all, r.eo_in, r.eo_relay, r.eo_sem, whole, p)
    if sz.direct:
        small_middle(r.early_ta, r.early_dev, r.early_sem, False)

    unpick = onehot(iota((sz.tp, nq * qt), 1) == r.perm_col[:, 0:1].astype(jnp.int32)).astype(BF16)
    dattn = mm(unpick, r.da_all[...].reshape(nq * qt, d)).astype(BF16)
    w_out = r.w_out[...].reshape(sz.inner, d)
    dmixed = mm(dattn, w_out, NT).astype(BF16).reshape(flat)

    spans = (pl.ds(0, 1), pl.ds(1, 3))

    def piece_start(n, values):
        r.pd_send[n] = values.reshape(2, sz.half, d).astype(BF16)

    def piece_send(n):
        go(r.pd_send.at[spans[n], 1 - c], r.pd_in.at[spans[n]], r.pd_sem, n, other)

    def piece_middle(n):
        span = spans[n]
        got(r.pd_in.at[span], r.pd_sem, n, other)
        for k in ((0,), (1, 2, 3))[n]:
            both = r.pd_send[k, c].astype(F32) + r.pd_in[k].astype(F32)
            for e in range(ea):
                r.pz_send[k, e] = both[e * sz.piece : (e + 1) * sz.piece].astype(BF16)
            r.pz_in[k, z] = r.pz_send[k, z]
        for s in later:
            go(r.pz_send.at[span, target[s]], r.pz_in.at[span, z], r.pz_sem, (n, s), ea_peer[s])

    def piece_last(n):
        span = spans[n]
        for s in later:
            got(r.pz_in.at[span, source[s]], r.pz_sem, (n, s), ea_peer[s])
        for k in ((0,), (1, 2, 3))[n]:
            total = r.pz_in[k, 0].astype(F32)
            for e in range(1, ea):
                total = total + r.pz_in[k, e].astype(F32)
            r.p_all[k, c, z] = total.astype(BF16)
        block = r.p_all.at[span, c, z]
        for s in later:
            go(block, block, r.pa_sem, (n, s), ea_peer[s])
        go(block, block, r.pb_sem, (n, 0), other)

    def piece_pass(n):
        for s in later:
            block = r.p_all.at[spans[n], c, source[s]]
            got(block, r.pa_sem, (n, s), ea_peer[s])
            go(block, block, r.pb_sem, (n, s), other)

    def piece_end(n):
        for s in range(ea):
            got(r.p_all.at[spans[n], 1 - c, source[s]], r.pb_sem, (n, s), other)

    if not sz.direct:

        def piece_start(n, values):
            r.o_piece[n] = values

        piece_send = piece_middle = piece_last = piece_pass = piece_end = lambda n: None

    piece_start(0, mm(r.mixed[...].reshape(sz.tp, sz.inner), dattn, TN))
    piece_send(0)
    if sz.direct:
        small_last(r.early_dev, r.early_ea, r.early_sem)

    def attention_back(image):
        dmix = stack(dmixed[image])
        probs = r.kept_probs[image] if sz.direct else attention_probs(image)
        dprobs = mm(dmix, r.v[image], NT)
        dvalue = mm(probs.astype(BF16), dmix, TN)
        inner = jnp.sum(probs * dprobs, axis=-1, keepdims=True)
        dscores = (probs * (dprobs - inner)).astype(BF16)
        dquery = unstack(mm(dscores, r.k[image])) * scale
        dkey = mm(dscores, stack(r.q[image]), TN) * scale
        for n, values in enumerate((dquery, dkey, dvalue)):
            r.dproj[n, image] = values.astype(BF16)

    attention_back(0)
    piece_middle(0)
    for image in range(1, sz.images):
        attention_back(image)
    dproj = [r.dproj[n].reshape(sz.tp, sz.inner) for n in range(3)]
    for n in (2, 0, 1):
        piece_start(n + 1, mm(dproj[n], r.a_low[...], TN))
    piece_send(1)
    share_got(r.eo_in, r.eo_sem, *whole[0])
    for copy in home_copies:
        copy.wait_send()
    for s in later + [0]:
        g = target[s]
        share = share_sum(r.rows_all, r.eo_in, g)
        if s:
            r.rgz_send[g] = share.astype(BF16)
            go(r.rgz_send.at[g], r.eo_back.at[z], r.eoz_sem, s, ea_peer[s])
        else:
            r.eo_back[z] = share.astype(BF16)

    piece_last(0)
    into_part = mm(dproj[0], r.qkv_w[0]) + mm(dproj[1], r.qkv_w[1]) + mm(dproj[2], r.qkv_w[2])
    r.in_send[...] = mm(pick_all, into_part.astype(BF16)).astype(BF16).reshape(nq, qt, d)
    for p in partners:
        go(r.in_send.at[quarter[p]], r.in_part.at[j], r.ip_sem, p, ta_peer[p])
    r.in_part[j] = r.in_send[j]
    _, hat_one, _ = layer_norm(r.padded[...].reshape(sz.tp, d).astype(F32), flat_row(r.gain1), flat_row(r.bias1))
    rows_at = iota((8, 1), 0)
    late = jnp.where(rows_at == 0, jnp.sum(into_part * hat_one, axis=0, keepdims=True), 0.0)
    late = late + jnp.where(rows_at == 1, jnp.sum(into_part, axis=0, keepdims=True), 0.0)
    for row, n in ((2, 0), (3, 2)):
        total = jnp.sum(dproj[n].astype(F32), axis=0, keepdims=True)
        wide = jnp.concatenate([total, jnp.zeros((1, d - sz.inner), F32)], axis=1)
        late = late + jnp.where(rows_at == row, wide, 0.0)
    if sz.direct:
        small_start(late, r.late_ta, r.late_sem)
    else:
        r.o_late[...] = late
    piece_middle(1)
    keeps = []
    for n, own, taken, out in ((0, r.up_low, r.up_in, r.o_up), (1, r.down_low, r.down_in, r.o_down)):
        got(taken, r.rep_sem, n, other)
        taken[...] = (own[...].astype(F32) + taken[...].astype(F32)).astype(BF16)
        keeps.append(pltpu.make_async_copy(taken, out, r.load_sem.at[n]))
        keeps[-1].start()
    got(r.bias_in, r.rep_sem, 2, other)
    r.o_bias[...] = r.bias_acc[...] + r.bias_in[...]
    if sz.direct:
        small_middle(r.late_ta, r.late_dev, r.late_sem, True)

    for p in partners:
        got(r.in_part.at[quarter[p]], r.ip_sem, p, ta_peer[p])
    into_one = r.in_part[0].astype(F32)
    for q in range(1, nq):
        into_one = into_one + r.in_part[q].astype(F32)
    x_mine = mm(pick_of(j), r.padded[...].reshape(sz.tp, d))
    _, hat_mine, inv_mine = layer_norm(x_mine, flat_row(r.gain1), flat_row(r.bias1))
    grad = r.dhidden[...] + norm_back(into_one, hat_mine, inv_mine, flat_row(r.gain1))
    r.ig_all[j] = grad.astype(BF16)
    for p in partners:
        go(r.ig_all.at[j], r.ig_all.at[j], r.ig_sem, p, ta_peer[p])
    if sz.direct:
        small_last(r.late_dev, r.late_ea, r.late_sem)

    for s in later:
        got(r.eo_back.at[source[s]], r.eoz_sem, s, ea_peer[s])
    output = r.hidden[...] + mm(back, r.eo_back[...].reshape(sz.experts * cs, d))
    r.out_all[j] = output.astype(BF16)
    for p in partners:
        go(r.out_all.at[j], r.out_all.at[j], r.out_sem, p, ta_peer[p])
    piece_last(1)
    piece_pass(0)
    piece_pass(1)
    stores = []

    def store(n, values, src, dst):
        src[...] = values.reshape(src.shape)
        stores.append(pltpu.make_async_copy(src, dst, r.load_sem.at[n]))
        stores[-1].start()

    for p in partners:
        got(r.ig_all.at[quarter[p]], r.ig_sem, p, ta_peer[p])
    store(2, mm(unpick, r.ig_all[...].reshape(nq * qt, d)).astype(BF16), r.a_low, r.o_in)
    for p in partners:
        got(r.out_all.at[quarter[p]], r.out_sem, p, ta_peer[p])
    store(3, mm(unpick, r.out_all[...].reshape(nq * qt, d)).astype(BF16), r.padded, r.o_out)
    if sz.direct:
        small_end(r.early_ea, r.o_early, r.early_sem)
        small_end(r.late_ea, r.o_late, r.late_sem)
    piece_end(0)
    piece_end(1)
    for copy in stores + keeps:
        copy.wait()
    for copy in started[-pool:]:
        copy.wait_send()
    assert len(receive) <= sz.arrivals, len(receive)


def flat_row(ref):
    return ref[...].reshape(1, -1)


def fit(values, rows):
    have = values.shape[0]
    if have >= rows:
        return values[:rows]
    return jnp.concatenate([values, jnp.zeros((rows - have, values.shape[1]), F32)])


def run_block(sz, inputs):
    nq, ea, d, cs, qt = sz.nq, sz.ea, sz.d, sz.cs, sz.qt
    dma = pltpu.SemaphoreType.DMA
    rows = sz.blocks * cs
    outs = dict(
        o_out=((sz.images, sz.lp, d), BF16),
        o_in=((sz.tp, d), BF16),
        o_early=((sz.early, d), F32),
        o_late=((8, d), F32),
        o_up=((d, sz.hidden), BF16),
        o_down=((sz.hidden, d), BF16),
        o_bias=((8, d), F32),
    )
    flat = (sz.images, sz.lp, sz.inner)
    block = (cs, d)
    buffers = dict(
        tok_v=((sz.length, sz.images, d), BF16),
        cot_v=((sz.length, sz.images, d), BF16),
        qkv_w=((3, sz.inner, d), BF16),
        up_w=((d, sz.hidden), BF16),
        down_w=((sz.hidden, d), BF16),
        w_full=((nq, 2, sz.half, d), BF16),
        padded=((sz.images, sz.lp, d), BF16),
        perm_col=((sz.tp, 128), F32),
        place_row=((4, qt), jnp.int32),
        place_col=((qt, 128), jnp.int32),
        a_low=((sz.tp, d), BF16),
        q=(flat, BF16),
        k=(flat, BF16),
        v=(flat, BF16),
        mixed=(flat, BF16),
        dproj=((3,) + flat, BF16),
        mix_send=((nq, qt, sz.inner), BF16),
        mix_in=((2, nq, qt, sz.inner), BF16),
        dy_mine=((qt, d), BF16),
        hidden=((qt, d), F32),
        dhidden=((qt, d), F32),
        b_low=((qt, d), BF16),
        probs=((sz.ep, qt), F32),
        dy_send=((2, ea) + block, BF16),
        gate_send=((ea, 2, 8, 128), F32),
        dy_all=((nq, ea) + block, BF16),
        rows_all=((nq, ea) + block, BF16),
        gate_in=((ea, 2, 8, 128), F32),
        gate_near=((ea, 2, 8, 128), F32),
        act_t=((sz.kept, rows, sz.hidden), BF16),
        pre_t=((sz.kept, rows, sz.hidden), BF16),
        slot_t=((sz.kept, rows, d), BF16),
        out_t=((sz.kept, rows, d), BF16),
        dg_send=((nq, ea, 8, 128), F32),
        dg_in=((nq, ea, 8, 128), F32),
        rg_in=((2, ea) + block, BF16),
        rg_relay=((2, ea, cs // 2, d), BF16),
        eo_in=((2, ea) + block, BF16),
        eo_relay=((2, ea, cs // 2, d), BF16),
        rgz_send=((ea,) + block, BF16),
        dgz_send=((ea, 8, 128), F32),
        rg_back=((ea,) + block, BF16),
        eo_back=((ea,) + block, BF16),
        dg_back=((ea, 8, 128), F32),
        up_acc=((d, sz.hidden), F32),
        down_acc=((sz.hidden, d), F32),
        bias_acc=((8, d), F32),
        up_low=((d, sz.hidden), BF16),
        down_low=((sz.hidden, d), BF16),
        up_in=((d, sz.hidden), BF16),
        down_in=((sz.hidden, d), BF16),
        bias_in=((8, d), F32),
        da_all=((nq, qt, d), BF16),
        ig_all=((nq, qt, d), BF16),
        out_all=((nq, qt, d), BF16),
        in_send=((nq, qt, d), BF16),
        in_part=((nq, qt, d), BF16),
    )
    if sz.direct:
        outs["p_all"] = ((4, 2, ea, sz.piece, d), BF16)
        buffers |= dict(
            early_ta=((nq, sz.early, d), F32),
            early_dev=((2, sz.early, d), F32),
            early_ea=((ea, sz.early, d), F32),
            late_ta=((nq, 8, d), F32),
            late_dev=((2, 8, d), F32),
            late_ea=((ea, 8, d), F32),
            pd_send=((4, 2, sz.half, d), BF16),
            pd_in=((4, sz.half, d), BF16),
            pz_send=((4, ea, sz.piece, d), BF16),
            pz_in=((4, ea, sz.piece, d), BF16),
        )
    else:
        outs["o_piece"] = ((4, sz.inner, d), F32)
    if sz.direct:
        buffers["row_send"] = ((2, ea) + block, BF16)
        buffers["kept_probs"] = ((sz.images, sz.heads * sz.lp, sz.lp), F32)
    names = list(inputs) + list(outs) + list(buffers) + ["sent", "arrived", "load_sem"]
    vm = pl.BlockSpec(memory_space=pltpu.VMEM)
    far = pl.BlockSpec(memory_space=pltpu.HBM)
    results = pl.pallas_call(
        functools.partial(block_kernel, sz, names),
        out_shape=[jax.ShapeDtypeStruct(*spec) for spec in outs.values()],
        in_specs=[far if name in ("tok", "cot", "w_qkv", "w_up", "w_down") else vm for name in inputs],
        out_specs=[far if name in ("o_up", "o_down", "o_in", "o_out") else vm for name in outs],
        scratch_shapes=[pltpu.VMEM(*spec) for spec in buffers.values()]
        + [dma((sz.pool,)), dma((sz.arrivals,)), dma((5,))],
        name="block",
        compiler_params=pltpu.CompilerParams(
            collective_id=0, has_side_effects=True, vmem_limit_bytes=60 << 20
        ),
    )(*inputs.values())
    return dict(zip(outs, results))


def finish_kernel(sz, names, *refs):
    r = types.SimpleNamespace(**dict(zip(names, refs)))
    n, d = sz.experts, sz.d
    loads, stores = [], []

    def load(src, dst):
        loads.append(pltpu.make_async_copy(src, dst, r.sem_in.at[len(loads)]))
        loads[-1].start()

    def store(src, dst):
        stores.append(pltpu.make_async_copy(src, dst, r.sem_out.at[len(stores)]))
        stores[-1].start()

    third = d // 3
    spans = [pl.ds(k * third, third) for k in range(3)]
    for src, dst in ((r.up, r.up_v), (r.down, r.down_v)):
        for span in spans:
            load(src.at[span], dst.at[span])
    for dst, src in (
        (r.f_b, r.early[n + 2 : n + 3]),
        (r.f_g1, r.late[0:1]),
        (r.f_c1, r.late[1:2]),
        (r.f_g2, r.early[n : n + 1]),
        (r.f_c2, r.early[n + 1 : n + 2]),
    ):
        dst[...] = src.reshape(d)
    r.f_router[...] = r.early[0:n]
    r.f_qv[...] = r.late[2:4, 0 : sz.inner]
    r.f_upb[...] = r.bias[0:1]
    r.f_downb[...] = r.bias[1:2]
    at = 0
    for src, wide, dst in ((r.up_v, r.up_w, r.f_up), (r.down_v, r.down_w, r.f_down)):
        for span in spans:
            loads[at].wait()
            at += 1
            if at == 3:
                load(r.grad, r.grad_v)
                load(r.out, r.out_v)
                load(r.piece, r.piece_v)
            wide[span] = src[span].astype(F32)
            store(wide.at[span], dst.at[span])
    loads[at].wait()
    for image in range(sz.images):
        r.grad_w[:, image, :] = r.grad_v[image * sz.lp : image * sz.lp + sz.length].astype(F32)
    store(r.grad_w, r.f_grad)
    loads[at + 1].wait()
    for image in range(sz.images):
        r.out_w[:, image, :] = r.out_v[image, 0 : sz.length]
    store(r.out_w, r.f_out)
    loads[at + 2].wait()
    for k in range(4):
        for core in range(2):
            for e in range(sz.ea):
                start = core * sz.half + e * sz.piece
                r.piece_w[k, start : start + sz.piece] = r.piece_v[k, core, e].astype(F32)
        store(r.piece_w.at[k], r.f_qkv.at[k - 1] if k else r.f_o)
    for copy in stores:
        copy.wait()


def finish(sz, got):
    d, n = sz.d, sz.experts
    inputs = dict(
        up=got["o_up"],
        down=got["o_down"],
        out=got["o_out"],
        grad=got["o_in"],
        piece=got["p_all"],
        early=got["o_early"],
        late=got["o_late"],
        bias=got["o_bias"],
    )
    outs = dict(
        f_out=((sz.length, sz.images, d), BF16),
        f_grad=((sz.length, sz.images, d), F32),
        f_qkv=((3, sz.inner, d), F32),
        f_qv=((2, sz.inner), F32),
        f_o=((sz.inner, d), F32),
        f_b=((d,), F32),
        f_g1=((d,), F32),
        f_c1=((d,), F32),
        f_g2=((d,), F32),
        f_c2=((d,), F32),
        f_router=((n, d), F32),
        f_up=((d, sz.hidden), F32),
        f_upb=((1, sz.hidden), F32),
        f_down=((sz.hidden, d), F32),
        f_downb=((1, d), F32),
    )
    buffers = dict(
        up_v=((d, sz.hidden), BF16),
        down_v=((sz.hidden, d), BF16),
        grad_v=((sz.tp, d), BF16),
        out_v=((sz.images, sz.lp, d), BF16),
        piece_v=((4, 2, sz.ea, sz.piece, d), BF16),
        up_w=((d, sz.hidden), F32),
        down_w=((sz.hidden, d), F32),
        grad_w=((sz.length, sz.images, d), F32),
        out_w=((sz.length, sz.images, d), BF16),
        piece_w=((4, sz.inner, d), F32),
    )
    vm = pl.BlockSpec(memory_space=pltpu.VMEM)
    far = pl.BlockSpec(memory_space=pltpu.HBM)
    large = ("up", "down", "out", "grad", "piece", "f_out", "f_grad", "f_qkv", "f_o", "f_up", "f_down")
    names = list(inputs) + list(outs) + list(buffers) + ["sem_in", "sem_out"]
    results = pl.pallas_call(
        functools.partial(finish_kernel, sz, names),
        out_shape=[jax.ShapeDtypeStruct(*spec) for spec in outs.values()],
        in_specs=[far if name in large else vm for name in inputs],
        out_specs=[far if name in large else vm for name in outs],
        scratch_shapes=[pltpu.VMEM(*spec) for spec in buffers.values()]
        + [pltpu.SemaphoreType.DMA((16,)), pltpu.SemaphoreType.DMA((16,))],
        name="finish",
        compiler_params=pltpu.CompilerParams(vmem_limit_bytes=60 << 20),
    )(*inputs.values())
    (out, grad, qkv, qv, o, b, g1, c1, g2, c2, router, up, up_b, down, down_b) = results
    turn = lambda t: jnp.swapaxes(t, 0, 1)
    return (
        turn(out),
        turn(grad),
        jnp.swapaxes(qkv, 1, 2),
        qv,
        o,
        b,
        g1,
        c1,
        g2,
        c2,
        router.T,
        up[None],
        up_b,
        down[None],
        down_b,
    )


def local(
    tokens,
    expert_ids,
    pair_ranks,
    cotangent,
    w_qkv,
    b_qv,
    w_out,
    b_out,
    ln1_gain,
    ln1_bias,
    ln2_gain,
    ln2_bias,
    w_router,
    w_up,
    b_up,
    w_down,
    b_down,
):
    sz = Sizes(tokens, expert_ids, w_qkv, w_up)
    inputs = dict(
        tok=jnp.swapaxes(tokens, 0, 1),
        cot=jnp.swapaxes(cotangent, 0, 1),
        w_qkv=jnp.swapaxes(w_qkv, 1, 2),
        b_qv=b_qv,
        w_out=w_out.reshape(2, sz.half, sz.d),
        b_out=b_out,
        gain1=ln1_gain,
        bias1=ln1_bias,
        gain2=ln2_gain,
        bias2=ln2_bias,
        router=w_router.T,
        w_up=w_up[0],
        b_up=b_up,
        w_down=w_down[0],
        b_down=b_down,
        ids=jnp.transpose(expert_ids, (0, 2, 1)),
        ranks=jnp.transpose(pair_ranks, (0, 2, 1)),
    )
    got = run_block(sz, inputs)
    if sz.direct:
        return finish(sz, got)
    n = sz.experts
    piece, shared = lax.psum((got["o_piece"], got["o_late"][2:4]), ("ea", "dev"))
    early, late = lax.psum((got["o_early"], got["o_late"][:2]), ("ea", "ta", "dev"))
    return (
        got["o_out"][:, : sz.length],
        got["o_in"].reshape(got["o_out"].shape)[:, : sz.length].astype(F32),
        jnp.swapaxes(piece[1:], 1, 2),
        shared[:, : sz.inner],
        piece[0],
        early[n + 2],
        late[0],
        late[1],
        early[n],
        early[n + 1],
        early[:n].T,
        got["o_up"].astype(F32)[None],
        got["o_bias"][0:1],
        got["o_down"].astype(F32)[None],
        got["o_bias"][1:2],
    )


def solution(mesh):
    in_specs = (
        P(("ea", "dev"), None, None),
        P(("ea", "dev"), None, None),
        P(("ea", "dev"), None, None),
        P(("ea", "dev"), None, None),
        P(None, None, "ta"),
        P(None, "ta"),
        P("ta", None),
        P(),
        P(),
        P(),
        P(),
        P(),
        P(),
        P("ea", None, "ta"),
        P("ea", "ta"),
        P("ea", "ta", None),
        P("ea", None),
    )
    out_specs = (
        P(("ea", "dev"), None, None),
        P(("ea", "dev"), None, None),
        P(None, None, "ta"),
        P(None, "ta"),
        P("ta", None),
        P(),
        P(),
        P(),
        P(),
        P(),
        P(),
        P("ea", None, "ta"),
        P("ea", "ta"),
        P("ea", "ta", None),
        P("ea", None),
    )
    return jax.shard_map(local, mesh=mesh, in_specs=in_specs, out_specs=out_specs, check_vma=False)
```
